32 devices in a mesh: slides: 2 (over y), seq: 4 (over z), head: 4 (over x, core).
Axes of the slice: x: 2, y: 2, z: 4, core: 2. Of those that a mesh axis runs over, the one named last changes fastest.
Arguments:
- query_rows: bfloat16 [8192, 768], P(('slides', 'seq'), 'head'), parts along dimension 0, may hold values from -64 to 64
- key_rows: bfloat16 [8192, 768], P(('slides', 'seq'), 'head'), parts along dimension 0, may hold values from -4.1 to 4.1
- value_rows: bfloat16 [8192, 768], P(('slides', 'seq'), 'head'), parts along dimension 0, may hold values from -6 to 6
Outputs:
- attended: bfloat16 [8192, 768], P(('slides', 'seq'), 'head'), parts along dimension 0
The draws below stay inside these ranges and needn't reach their ends.
There are 2 independent parts, one for each index of `slides`. The reference program is written for one: setup_inputs(seed, part) draws one part's arguments, and reference() takes and returns one part's arrays. A program takes and returns all parts, laid end to end along the dimension named above; each array names one. Nothing has to cross between parts.
All inputs are finite; a program needn't handle non-finite values.
Results may differ from the reference program's by a relative error of at most 0.0028.
Values may be sent and summed in bfloat16 or wider, within the bound.
No kernel may reach another device: no remote copies, remote signals or barrier semaphores. Data moves between devices by JAX's collectives and lax.ppermute only.
A program may use at most 64 MiB of HBM per device.

```python
import math
import jax
import jax.numpy as jnp
from jax import lax

HEADS = 16
HEAD_DIM = 48
SEG_A = 1024
SEG_B = 4096
TOKENS = 4096
SEG_C = 4096


def paired_draw(key):
    seed_keys = jax.random.fold_in(key, 11)
    seed_queries = jax.random.fold_in(key, 12)
    full_shape = (TOKENS, HEADS * HEAD_DIM)
    base_keys = jnp.clip(jax.random.normal(seed_keys, full_shape, jnp.float32), -4.0, 4.0)
    base_queries = 3.0 * jnp.clip(jax.random.normal(seed_queries, full_shape, jnp.float32), -4.0, 4.0)
    return (base_queries, base_keys)


def draw_query_rows(key, part):
    return paired_draw(key)[0].astype(jnp.bfloat16)


def draw_key_rows(key, part):
    return paired_draw(key)[1].astype(jnp.bfloat16)


def steps_of(key, extent, split, smallest, largest):
    factor_of = 1.0
    for axis_at, shards_of in split:
        draws = jax.random.uniform(jax.random.fold_in(jax.random.fold_in(key, 6), axis_at), (shards_of,), jnp.float32, smallest / len(split), largest / len(split))
        factor_of = factor_of * jnp.repeat(jnp.exp(draws), extent[axis_at] // shards_of).reshape((-1,) + (1,) * (len(extent) - 1 - axis_at))
    return factor_of


def bell_draw(stream_key, shape, width, most, cuts=(), held_as=jnp.bfloat16):
    entries = width * jax.random.normal(stream_key, shape, jnp.float32)
    if cuts:
        entries = entries * steps_of(stream_key, shape, cuts, -0.22, 0.18)
    return jnp.clip(entries, -most, most).astype(held_as)


def setup_inputs(seed: int = 0, part: int = 0) -> dict:
    streams_of = jax.random.split(jax.random.key(seed), 4)
    own_keys = jax.random.split(jax.random.fold_in(streams_of[3], part), 4)
    return {
        "query_rows": draw_query_rows(jax.random.fold_in(jax.random.fold_in(streams_of[3], part), 71), part),
        "key_rows": draw_key_rows(jax.random.fold_in(jax.random.fold_in(streams_of[3], part), 71), part),
        "value_rows": bell_draw(own_keys[2], (TOKENS, HEADS * HEAD_DIM), 1.0, 6.0, ((0, 4), (1, 4))),
    }


def attend_block(blocks):
    query_block, key_block, value_block = blocks
    count = query_block.shape[0]
    keys = key_block.shape[0]
    rows = math.gcd(count, max(1, 4194304 // (HEADS * keys)))
    key_full = key_block.astype(jnp.float32)
    value_full = value_block.astype(jnp.float32)

    def one_piece(query_piece):
        query_full = query_piece.astype(jnp.float32)
        scores = jnp.einsum("qhd,khd->hqk", query_full, key_full) * (HEAD_DIM ** -0.5)
        row_max = jnp.max(scores, axis=-1)
        exp_scores = jnp.exp(scores - row_max[:, :, None])
        row_total = jnp.sum(exp_scores, axis=-1)
        rounded = lax.optimization_barrier(exp_scores.astype(jnp.bfloat16)).astype(jnp.float32)
        weighted = jnp.einsum("hqk,khd->qhd", rounded, value_full)
        level_out = weighted / jnp.transpose(row_total)[:, :, None]
        return level_out, jnp.transpose(row_max + jnp.log(row_total))

    pieces = query_block.reshape(count // rows, rows, HEADS, HEAD_DIM)
    outs, lses = lax.map(one_piece, pieces)
    return outs.reshape(count, HEADS, HEAD_DIM), lses.reshape(count, HEADS)


def reference(query_rows, key_rows, value_rows):
    head_ids = jnp.arange(HEADS)
    shaped = [source.reshape(TOKENS, HEADS, HEAD_DIM) for source in (query_rows, key_rows, value_rows)]
    levels = [(1, SEG_A), (2, SEG_B), (4, SEG_C)]
    running_max = jnp.zeros((TOKENS, HEADS), jnp.float32)
    running_total = jnp.zeros((TOKENS, HEADS), jnp.float32)
    running_acc = jnp.zeros((TOKENS, HEADS, HEAD_DIM), jnp.float32)
    for stride, span in levels:
        used_count = TOKENS // stride
        seg_rows = span // stride
        offsets = head_ids % stride
        picked = [source.reshape(used_count, stride, HEADS, HEAD_DIM)[:, offsets, head_ids] for source in shaped]
        blocks = tuple(source.reshape(used_count // seg_rows, seg_rows, HEADS, HEAD_DIM) for source in picked)
        level_out, level_lse = lax.map(attend_block, blocks)
        level_out = level_out.reshape(used_count, HEADS, HEAD_DIM)
        level_lse = level_lse.reshape(used_count, HEADS)
        if stride == 1:
            running_max = level_lse
            running_total = jnp.ones((TOKENS, HEADS), jnp.float32)
            running_acc = level_out
        else:
            max_grid = running_max.reshape(used_count, stride, HEADS)
            total_grid = running_total.reshape(used_count, stride, HEADS)
            acc_grid = running_acc.reshape(used_count, stride, HEADS, HEAD_DIM)
            old_max = max_grid[:, offsets, head_ids]
            new_max = jnp.maximum(old_max, level_lse)
            keep_old = jnp.exp(old_max - new_max)
            take_new = jnp.exp(level_lse - new_max)
            new_total = total_grid[:, offsets, head_ids] * keep_old + take_new
            new_acc = acc_grid[:, offsets, head_ids] * keep_old[:, :, None] + take_new[:, :, None] * level_out
            running_max = max_grid.at[:, offsets, head_ids].set(new_max).reshape(TOKENS, HEADS)
            running_total = total_grid.at[:, offsets, head_ids].set(new_total).reshape(TOKENS, HEADS)
            running_acc = acc_grid.at[:, offsets, head_ids].set(new_acc).reshape(TOKENS, HEADS, HEAD_DIM)
    attended = running_acc / running_total[:, :, None]
    return attended.astype(jnp.bfloat16).reshape(TOKENS, HEADS * HEAD_DIM)
```

```python
import math

import jax
import jax.numpy as jnp
import numpy as np
from jax import lax
from jax.experimental import pallas as pl
from jax.experimental.pallas import tpu as pltpu
from jax.sharding import PartitionSpec as P

HEAD_DIM = 48
SEG_A = 1024
SEG_B = 4096


def swapped(shard, axis, stride):
    return lax.ppermute(shard, axis, [(i, i ^ 1 << stride) for i in range(lax.axis_size(axis))])


def attend(query_flat, key_flat, value_flat, score_scale):
    local_heads = query_flat.shape[1] // HEAD_DIM
    query_block = query_flat.reshape(query_flat.shape[0], local_heads, HEAD_DIM)
    key_block = key_flat.reshape(key_flat.shape[0], local_heads, HEAD_DIM)
    value_block = value_flat.reshape(value_flat.shape[0], local_heads, HEAD_DIM)
    scores = (
        jnp.einsum("qad,kad->qak", query_block, key_block, preferred_element_type=jnp.float32)
        * score_scale
    )
    row_max = jnp.max(scores, axis=-1)
    exp_scores = jnp.exp(scores - row_max[:, :, None])
    row_total = jnp.sum(exp_scores, axis=-1)
    weighted = jnp.einsum(
        "qak,kad->qad",
        exp_scores.astype(jnp.bfloat16),
        value_block,
        preferred_element_type=jnp.float32,
    )
    level_out = weighted / row_total[:, :, None]
    return (
        level_out.reshape(query_flat.shape[0], local_heads * HEAD_DIM),
        row_max + jnp.log(row_total),
    )


def attend_rows(query_flat, key_flat, value_flat, score_scale):
    count, feature_width = query_flat.shape
    local_heads = feature_width // HEAD_DIM
    keys = key_flat.shape[0]
    rows = math.gcd(count, max(1, 1048576 // (local_heads * keys)))

    def one_piece(query_piece):
        return attend(query_piece, key_flat, value_flat, score_scale)

    outs, lses = lax.map(one_piece, query_flat.reshape(count // rows, rows, feature_width))
    return (outs.reshape(count, feature_width), lses.reshape(count, local_heads))


def local_segments(query_flat, key_flat, value_flat, seg_rows, score_scale):
    count, feature_width = query_flat.shape
    local_heads = feature_width // HEAD_DIM
    shape = (count // seg_rows, seg_rows, feature_width)

    def one_segment(parts):
        return attend_rows(parts[0], parts[1], parts[2], score_scale)

    outs, lses = lax.map(
        one_segment, (query_flat.reshape(shape), key_flat.reshape(shape), value_flat.reshape(shape))
    )
    return (outs.reshape(count, feature_width), lses.reshape(count, local_heads))


def pick_rows(block, stride):
    row_count, feature_width = block.shape
    local_heads = feature_width // HEAD_DIM
    grid = block.reshape(row_count // stride, stride * feature_width)
    columns = []
    for head in range(local_heads):
        begin = head % stride * feature_width + head * HEAD_DIM
        columns.append(grid[:, begin : begin + HEAD_DIM])
    return jnp.concatenate(columns, axis=1)


def spread_rows(level_out, level_lse, stride):
    used_count, feature_width = level_out.shape
    local_heads = feature_width // HEAD_DIM
    head_of_column = np.arange(feature_width) // HEAD_DIM
    out_phases = []
    lse_phases = []
    for phase in range(stride):
        column_mask = jnp.asarray((head_of_column % stride == phase).astype(np.float32))
        head_mask = jnp.asarray(np.arange(local_heads) % stride == phase)
        out_phases.append(level_out * column_mask[None, :])
        lse_phases.append(jnp.where(head_mask[None, :], level_lse, -jnp.inf))
    full_out = jnp.stack(out_phases, axis=1).reshape(used_count * stride, feature_width)
    full_lse = jnp.stack(lse_phases, axis=1).reshape(used_count * stride, local_heads)
    return (full_out, full_lse)


def fold_block(fold_state, queries, keys, values, valid, score_scale):
    running_max, running_total, running_acc = fold_state
    local_heads = queries.shape[1] // HEAD_DIM
    query_block = queries.reshape(queries.shape[0], local_heads, HEAD_DIM)
    key_block = keys.reshape(keys.shape[0], local_heads, HEAD_DIM)
    value_block = values.reshape(values.shape[0], local_heads, HEAD_DIM)
    scores = (
        jnp.einsum("qad,kad->qak", query_block, key_block, preferred_element_type=jnp.float32)
        * score_scale
    )
    scores = jnp.where(valid[None, None, :], scores, -jnp.inf)
    new_max = jnp.maximum(running_max, jnp.max(scores, axis=-1))
    safe_max = jnp.where(new_max == -jnp.inf, 0.0, new_max)
    rescale = jnp.exp(running_max - safe_max)
    exp_scores = jnp.exp(scores - safe_max[:, :, None])
    new_total = running_total * rescale + jnp.sum(exp_scores, axis=-1)
    weighted = jnp.einsum(
        "qak,kad->qad",
        exp_scores.astype(jnp.bfloat16),
        value_block,
        preferred_element_type=jnp.float32,
    )
    new_acc = running_acc * rescale[:, :, None] + weighted
    return (new_max, new_total, new_acc)


def any_length(query_rows, key_rows, value_rows):
    row_count = query_rows.shape[0]
    feature_width = query_rows.shape[1]
    local_heads = feature_width // HEAD_DIM
    shards = lax.axis_size("seq")
    score_scale = HEAD_DIM ** (-0.5)
    first_out, first_lse = local_segments(query_rows, key_rows, value_rows, SEG_A, score_scale)
    used_two = row_count // 2
    seg_two = SEG_B // 2
    query_two = pick_rows(query_rows, 2)
    key_two = pick_rows(key_rows, 2)
    value_two = pick_rows(value_rows, 2)
    stacked = jnp.stack([key_two, value_two])
    for bit_index in range((seg_two // used_two).bit_length() - 1):
        partner = swapped(stacked, "seq", bit_index)
        stacked = jnp.concatenate([stacked, partner], axis=1)
    second_out, second_lse = attend_rows(query_two, stacked[0], stacked[1], score_scale)
    span_tokens = row_count * shards
    group_span = span_tokens // row_count
    used_three = row_count // 4
    wide_queries = pick_rows(query_rows, 4)
    wide_keys = pick_rows(key_rows, 4)
    wide_values = pick_rows(value_rows, 4)
    my_group = lax.axis_index("seq") // group_span
    key_limit = max(1, 1048576 // (local_heads * used_three))
    initial = (
        jnp.full((used_three, local_heads), -jnp.inf, jnp.float32),
        jnp.zeros((used_three, local_heads), jnp.float32),
        jnp.zeros((used_three, local_heads, HEAD_DIM), jnp.float32),
    )
    pieces = (
        lax.all_gather(wide_keys, "seq", axis=0, tiled=True),
        lax.all_gather(wide_values, "seq", axis=0, tiled=True),
    )
    piece_rows = pieces[0].shape[0]
    block = math.gcd(piece_rows, key_limit)
    key_blocks = pieces[0].reshape(piece_rows // block, block, feature_width)
    value_blocks = pieces[1].reshape(piece_rows // block, block, feature_width)
    block_starts = jnp.arange(piece_rows // block, dtype=jnp.int32) * block

    def fold_step(inner_state, items):
        owners = (items[2] + jnp.arange(block, dtype=jnp.int32)) // used_three
        valid = owners // group_span == my_group
        return (fold_block(inner_state, wide_queries, items[0], items[1], valid, score_scale), None)

    final_state, unused = lax.scan(fold_step, initial, (key_blocks, value_blocks, block_starts))
    final_max, final_total, final_acc = final_state
    third_out = (final_acc / final_total[:, :, None]).reshape(used_three, feature_width)
    third_lse = final_max + jnp.log(final_total)
    second_full, second_lse_full = spread_rows(second_out, second_lse, 2)
    third_full, third_lse_full = spread_rows(third_out, third_lse, 4)
    peak = jnp.maximum(jnp.maximum(first_lse, second_lse_full), third_lse_full)
    weight_one = jnp.exp(first_lse - peak)
    weight_two = jnp.exp(second_lse_full - peak)
    weight_three = jnp.exp(third_lse_full - peak)
    denominator = jnp.repeat(weight_one + weight_two + weight_three, HEAD_DIM, axis=1)
    numerator = jnp.repeat(weight_one, HEAD_DIM, axis=1) * first_out
    numerator = numerator + jnp.repeat(weight_two, HEAD_DIM, axis=1) * second_full
    numerator = numerator + jnp.repeat(weight_three, HEAD_DIM, axis=1) * third_full
    return (numerator / denominator).astype(jnp.bfloat16)


STRIDES = 4
LANES = 128
LOG2E = 1.4426950408889634
VMEM_BYTES = 60 * 1024 * 1024


def dot_nn(left, right):
    return lax.dot_general(left, right, (((1,), (0,)), ((), ())), preferred_element_type=jnp.float32)


def dot_nt(left, right):
    return lax.dot_general(left, right, (((1,), (1,)), ((), ())), preferred_element_type=jnp.float32)


def identity(size):
    rows = lax.broadcasted_iota(jnp.int32, (size, size), 0)
    columns = lax.broadcasted_iota(jnp.int32, (size, size), 1)
    return jnp.where(rows == columns, 1.0, 0.0).astype(jnp.bfloat16)


def call(kernel, outs, args, scratch, flops):
    return pl.pallas_call(
        kernel,
        out_shape=outs,
        in_specs=[pl.BlockSpec(memory_space=pltpu.VMEM)] * len(args),
        out_specs=jax.tree.map(lambda out: pl.BlockSpec(memory_space=pltpu.VMEM), outs),
        scratch_shapes=scratch,
        compiler_params=pltpu.CompilerParams(vmem_limit_bytes=VMEM_BYTES),
        cost_estimate=pl.CostEstimate(flops=flops, bytes_accessed=4 << 20, transcendentals=0),
    )(*args)


def pack_kernel(q_ref, k_ref, v_ref, m0, m1, m2, m3, qt_ref, kc_ref, vt_ref, wide, by_head):
    rows, width = q_ref.shape
    heads = width // HEAD_DIM
    part = rows // STRIDES
    eye = identity(width)
    for which, (ref, turned) in enumerate(((q_ref, qt_ref), (k_ref, None), (v_ref, vt_ref))):
        full = ref[...].astype(jnp.float32)
        wide[0] = full[:, :LANES]
        wide[1, :, pl.ds(0, width - LANES)] = full[:, LANES:]
        for phase in range(STRIDES):
            spread = pl.ds(phase, part, stride=STRIDES)
            chunk = jnp.concatenate([wide[0, spread, :], wide[1, spread, :][:, : width - LANES]], axis=1).astype(jnp.bfloat16)
            if which == 1:
                kc_ref[pl.ds(phase * part, part), :] = chunk
            flat = dot_nt(eye, chunk).astype(jnp.bfloat16)
            if turned is not None:
                turned[:, pl.ds(phase * part, part)] = flat
            for head in range(heads):
                offset = (phase - head) % STRIDES
                if offset % 2 == 0:
                    by_head[head, pl.ds(which * HEAD_DIM, HEAD_DIM), pl.ds(offset // 2 * part, part)] = flat[
                        head * HEAD_DIM : (head + 1) * HEAD_DIM
                    ]
    me = lax.axis_index("seq")
    for shift, message in enumerate((m0, m1, m2, m3)):
        message[...] = by_head[lax.rem(me + shift, heads)]


def with_ones(block):
    count = block.shape[1]
    extra = jnp.where(lax.broadcasted_iota(jnp.int32, (16, count), 0) == 0, 1.0, 0.0).astype(jnp.bfloat16)
    return jnp.concatenate([block, extra], axis=0)


def near_kernel(qt_ref, kc_ref, vt_ref, out_ref):
    width, rows = qt_ref.shape
    heads = width // HEAD_DIM
    part = rows // STRIDES
    factor = HEAD_DIM ** (-0.5) * LOG2E
    for head in range(heads):
        features = pl.ds(head * HEAD_DIM, HEAD_DIM)
        keys = kc_ref[...][:, head * HEAD_DIM : (head + 1) * HEAD_DIM]
        values = with_ones(vt_ref[features, :])
        for piece in range(STRIDES):
            lanes = pl.ds(piece * part, part)
            scores = dot_nn(keys, qt_ref[features, lanes])
            top = jnp.max(scores, axis=0, keepdims=True) * factor
            probs = jnp.exp2(scores * factor - top).astype(jnp.bfloat16)
            out_ref[head, :, lanes] = dot_nn(values, probs)
            out_ref[head, pl.ds(HEAD_DIM + 1, 1), lanes] = top


def far_kernel(m0, m1, m2, m3, o0, o1, o2, o3, keys_ref):
    count = m0.shape[1]
    half = count // 2
    factor = HEAD_DIM ** (-0.5) * LOG2E
    sources = (m0, m1, m2, m3)
    eye = identity(count)
    for at, source in enumerate(sources):
        keys_ref[pl.ds(at * count, count), :] = dot_nt(eye, source[pl.ds(HEAD_DIM, HEAD_DIM), :]).astype(jnp.bfloat16)
    values = [with_ones(source[pl.ds(2 * HEAD_DIM, HEAD_DIM), :]) for source in sources]
    for source, out in zip(sources, (o0, o1, o2, o3)):
        for klass in range(2):
            lanes = pl.ds(klass * half, half)
            scores = dot_nn(keys_ref[...], source[pl.ds(0, HEAD_DIM), lanes])
            top = jnp.max(scores, axis=0, keepdims=True) * factor
            twice = top - 1.0 if klass == 0 else top
            acc = jnp.zeros((HEAD_DIM + 16, half), jnp.float32)
            for at in range(len(sources)):
                first = jnp.exp2(scores[at * count : at * count + half] * factor - twice).astype(jnp.bfloat16)
                second = jnp.exp2(scores[at * count + half : (at + 1) * count] * factor - top).astype(jnp.bfloat16)
                acc = acc + dot_nn(values[at], jnp.concatenate([first, second], axis=0))
            total = acc[HEAD_DIM : HEAD_DIM + 1]
            lse = top + jnp.log2(total)
            high = lse.astype(jnp.bfloat16)
            rest = lse - high.astype(jnp.float32)
            middle = rest.astype(jnp.bfloat16)
            low = (rest - middle.astype(jnp.float32)).astype(jnp.bfloat16)
            row = lax.broadcasted_iota(jnp.int32, (16, half), 0)
            parts = jnp.where(row == 0, high.astype(jnp.float32), 0.0)
            parts = jnp.where(row == 1, middle.astype(jnp.float32), parts)
            parts = jnp.where(row == 2, low.astype(jnp.float32), parts)
            out[pl.ds(0, HEAD_DIM), lanes] = (acc[:HEAD_DIM] / total).astype(jnp.bfloat16)
            out[pl.ds(HEAD_DIM, 16), lanes] = parts.astype(jnp.bfloat16)


def merge_kernel(near_ref, g0, g1, g2, g3, out_ref, by_head, wide):
    heads = near_ref.shape[0]
    rows = near_ref.shape[2]
    part = rows // STRIDES
    me = lax.axis_index("seq")
    for shift, result in enumerate((g0, g1, g2, g3)):
        by_head[lax.rem(me + shift, heads)] = result[...]
    eye = identity(part)
    for phase in range(STRIDES):
        lanes = pl.ds(phase * part, part)
        columns = []
        for head in range(heads):
            near = near_ref[head, pl.ds(0, HEAD_DIM), lanes]
            total = near_ref[head, pl.ds(HEAD_DIM, 1), lanes]
            offset = (phase - head) % STRIDES
            if offset % 2 == 0:
                top = near_ref[head, pl.ds(HEAD_DIM + 1, 1), lanes]
                there = by_head[head, :, pl.ds(offset // 2 * part, part)].astype(jnp.float32)
                lse = there[HEAD_DIM : HEAD_DIM + 1] + there[HEAD_DIM + 1 : HEAD_DIM + 2] + there[HEAD_DIM + 2 : HEAD_DIM + 3]
                peak = jnp.maximum(top, lse)
                weight = jnp.exp2(top - peak)
                far = jnp.exp2(lse - peak)
                near = near * weight + there[:HEAD_DIM] * far
                total = total * weight + far
            columns.append((near / total).astype(jnp.bfloat16))
        padding = [jnp.zeros((2 * LANES - heads * HEAD_DIM, part), jnp.bfloat16)]
        upright = dot_nt(eye, jnp.concatenate(columns + padding, axis=0))
        wide[0, pl.ds(phase, part, stride=STRIDES), :] = upright[:, :LANES]
        wide[1, pl.ds(phase, part, stride=STRIDES), :] = upright[:, LANES:]
    out_ref[:, pl.ds(0, LANES)] = wide[0].astype(jnp.bfloat16)
    out_ref[:, pl.ds(LANES, heads * HEAD_DIM - LANES)] = wide[1][:, : heads * HEAD_DIM - LANES].astype(jnp.bfloat16)


def by_rotation(blocks, sign):
    shards = lax.axis_size("seq")
    moved = [blocks[0]]
    for shift in range(1, shards):
        moved.append(lax.ppermute(blocks[shift], "seq", [(i, (i + sign * shift) % shards) for i in range(shards)]))
    return moved


def whole_slide(query_rows, key_rows, value_rows):
    rows, width = query_rows.shape
    heads = width // HEAD_DIM
    half = rows // 2
    bf16, f32 = jnp.bfloat16, jnp.float32
    message = jax.ShapeDtypeStruct((3 * HEAD_DIM, half), bf16)
    packed = call(
        pack_kernel,
        [message] * heads + [jax.ShapeDtypeStruct(s, bf16) for s in ((width, rows), (rows, width), (width, rows))],
        (query_rows, key_rows, value_rows),
        [pltpu.VMEM((2, rows, LANES), f32), pltpu.VMEM((heads, 3 * HEAD_DIM, half), bf16)],
        1 << 28,
    )
    arrived = by_rotation(packed[:heads], 1)
    near = call(
        near_kernel,
        jax.ShapeDtypeStruct((heads, HEAD_DIM + 16, rows), f32),
        packed[heads:],
        [],
        4 * heads * rows * rows * 256,
    )
    far = call(
        far_kernel,
        [jax.ShapeDtypeStruct((HEAD_DIM + 16, half), bf16)] * heads,
        arrived,
        [pltpu.VMEM((heads * half, HEAD_DIM), bf16)],
        4 * heads * rows * rows * 256,
    )
    back = by_rotation(far, -1)
    return call(
        merge_kernel,
        jax.ShapeDtypeStruct((rows, width), bf16),
        [near, *back],
        [pltpu.VMEM((heads, HEAD_DIM + 16, half), bf16), pltpu.VMEM((2, rows, LANES), f32)],
        1 << 28,
    )


def per_device(query_rows, key_rows, value_rows):
    rows, width = query_rows.shape
    shards = lax.axis_size("seq")
    if rows == SEG_A and rows * shards == SEG_B and width == shards * HEAD_DIM and shards == STRIDES and LANES < width <= 2 * LANES:
        return whole_slide(query_rows, key_rows, value_rows)
    return any_length(query_rows, key_rows, value_rows)


def solution(mesh):
    return jax.shard_map(
        per_device,
        mesh=mesh,
        in_specs=(
            P(("slides", "seq"), "head"),
            P(("slides", "seq"), "head"),
            P(("slides", "seq"), "head"),
        ),
        out_specs=P(("slides", "seq"), "head"),
        check_vma=False,
    )
```

```python
import functools
import math

import jax
import jax.numpy as jnp
import numpy as np
from jax import lax
from jax.experimental import pallas as pl
from jax.experimental.pallas import tpu as pltpu
from jax.sharding import PartitionSpec as P

HEAD_DIM = 48
SEG_A = 1024
SEG_B = 4096


def swapped(shard, axis, stride):
    return lax.ppermute(shard, axis, [(i, i ^ 1 << stride) for i in range(lax.axis_size(axis))])


def attend(query_flat, key_flat, value_flat, score_scale):
    local_heads = query_flat.shape[1] // HEAD_DIM
    query_block = query_flat.reshape(query_flat.shape[0], local_heads, HEAD_DIM)
    key_block = key_flat.reshape(key_flat.shape[0], local_heads, HEAD_DIM)
    value_block = value_flat.reshape(value_flat.shape[0], local_heads, HEAD_DIM)
    scores = (
        jnp.einsum("qad,kad->qak", query_block, key_block, preferred_element_type=jnp.float32)
        * score_scale
    )
    row_max = jnp.max(scores, axis=-1)
    exp_scores = jnp.exp(scores - row_max[:, :, None])
    row_total = jnp.sum(exp_scores, axis=-1)
    weighted = jnp.einsum(
        "qak,kad->qad",
        exp_scores.astype(jnp.bfloat16),
        value_block,
        preferred_element_type=jnp.float32,
    )
    level_out = weighted / row_total[:, :, None]
    return (
        level_out.reshape(query_flat.shape[0], local_heads * HEAD_DIM),
        row_max + jnp.log(row_total),
    )


def attend_rows(query_flat, key_flat, value_flat, score_scale):
    count, feature_width = query_flat.shape
    local_heads = feature_width // HEAD_DIM
    keys = key_flat.shape[0]
    rows = math.gcd(count, max(1, 1048576 // (local_heads * keys)))

    def one_piece(query_piece):
        return attend(query_piece, key_flat, value_flat, score_scale)

    outs, lses = lax.map(one_piece, query_flat.reshape(count // rows, rows, feature_width))
    return (outs.reshape(count, feature_width), lses.reshape(count, local_heads))


def local_segments(query_flat, key_flat, value_flat, seg_rows, score_scale):
    count, feature_width = query_flat.shape
    local_heads = feature_width // HEAD_DIM
    shape = (count // seg_rows, seg_rows, feature_width)

    def one_segment(parts):
        return attend_rows(parts[0], parts[1], parts[2], score_scale)

    outs, lses = lax.map(
        one_segment, (query_flat.reshape(shape), key_flat.reshape(shape), value_flat.reshape(shape))
    )
    return (outs.reshape(count, feature_width), lses.reshape(count, local_heads))


def pick_rows(block, stride):
    row_count, feature_width = block.shape
    local_heads = feature_width // HEAD_DIM
    grid = block.reshape(row_count // stride, stride * feature_width)
    columns = []
    for head in range(local_heads):
        begin = head % stride * feature_width + head * HEAD_DIM
        columns.append(grid[:, begin : begin + HEAD_DIM])
    return jnp.concatenate(columns, axis=1)


def spread_rows(level_out, level_lse, stride):
    used_count, feature_width = level_out.shape
    local_heads = feature_width // HEAD_DIM
    head_of_column = np.arange(feature_width) // HEAD_DIM
    out_phases = []
    lse_phases = []
    for phase in range(stride):
        column_mask = jnp.asarray((head_of_column % stride == phase).astype(np.float32))
        head_mask = jnp.asarray(np.arange(local_heads) % stride == phase)
        out_phases.append(level_out * column_mask[None, :])
        lse_phases.append(jnp.where(head_mask[None, :], level_lse, -jnp.inf))
    full_out = jnp.stack(out_phases, axis=1).reshape(used_count * stride, feature_width)
    full_lse = jnp.stack(lse_phases, axis=1).reshape(used_count * stride, local_heads)
    return (full_out, full_lse)


def fold_block(fold_state, queries, keys, values, valid, score_scale):
    running_max, running_total, running_acc = fold_state
    local_heads = queries.shape[1] // HEAD_DIM
    query_block = queries.reshape(queries.shape[0], local_heads, HEAD_DIM)
    key_block = keys.reshape(keys.shape[0], local_heads, HEAD_DIM)
    value_block = values.reshape(values.shape[0], local_heads, HEAD_DIM)
    scores = (
        jnp.einsum("qad,kad->qak", query_block, key_block, preferred_element_type=jnp.float32)
        * score_scale
    )
    scores = jnp.where(valid[None, None, :], scores, -jnp.inf)
    new_max = jnp.maximum(running_max, jnp.max(scores, axis=-1))
    safe_max = jnp.where(new_max == -jnp.inf, 0.0, new_max)
    rescale = jnp.exp(running_max - safe_max)
    exp_scores = jnp.exp(scores - safe_max[:, :, None])
    new_total = running_total * rescale + jnp.sum(exp_scores, axis=-1)
    weighted = jnp.einsum(
        "qak,kad->qad",
        exp_scores.astype(jnp.bfloat16),
        value_block,
        preferred_element_type=jnp.float32,
    )
    new_acc = running_acc * rescale[:, :, None] + weighted
    return (new_max, new_total, new_acc)


def any_length(query_rows, key_rows, value_rows):
    row_count = query_rows.shape[0]
    feature_width = query_rows.shape[1]
    local_heads = feature_width // HEAD_DIM
    shards = lax.axis_size("seq")
    score_scale = HEAD_DIM ** (-0.5)
    first_out, first_lse = local_segments(query_rows, key_rows, value_rows, SEG_A, score_scale)
    used_two = row_count // 2
    seg_two = SEG_B // 2
    query_two = pick_rows(query_rows, 2)
    key_two = pick_rows(key_rows, 2)
    value_two = pick_rows(value_rows, 2)
    stacked = jnp.stack([key_two, value_two])
    for bit_index in range((seg_two // used_two).bit_length() - 1):
        partner = swapped(stacked, "seq", bit_index)
        stacked = jnp.concatenate([stacked, partner], axis=1)
    second_out, second_lse = attend_rows(query_two, stacked[0], stacked[1], score_scale)
    span_tokens = row_count * shards
    group_span = span_tokens // row_count
    used_three = row_count // 4
    wide_queries = pick_rows(query_rows, 4)
    wide_keys = pick_rows(key_rows, 4)
    wide_values = pick_rows(value_rows, 4)
    my_group = lax.axis_index("seq") // group_span
    key_limit = max(1, 1048576 // (local_heads * used_three))
    initial = (
        jnp.full((used_three, local_heads), -jnp.inf, jnp.float32),
        jnp.zeros((used_three, local_heads), jnp.float32),
        jnp.zeros((used_three, local_heads, HEAD_DIM), jnp.float32),
    )
    pieces = (
        lax.all_gather(wide_keys, "seq", axis=0, tiled=True),
        lax.all_gather(wide_values, "seq", axis=0, tiled=True),
    )
    piece_rows = pieces[0].shape[0]
    block = math.gcd(piece_rows, key_limit)
    key_blocks = pieces[0].reshape(piece_rows // block, block, feature_width)
    value_blocks = pieces[1].reshape(piece_rows // block, block, feature_width)
    block_starts = jnp.arange(piece_rows // block, dtype=jnp.int32) * block

    def fold_step(inner_state, items):
        owners = (items[2] + jnp.arange(block, dtype=jnp.int32)) // used_three
        valid = owners // group_span == my_group
        return (fold_block(inner_state, wide_queries, items[0], items[1], valid, score_scale), None)

    final_state, unused = lax.scan(fold_step, initial, (key_blocks, value_blocks, block_starts))
    final_max, final_total, final_acc = final_state
    third_out = (final_acc / final_total[:, :, None]).reshape(used_three, feature_width)
    third_lse = final_max + jnp.log(final_total)
    second_full, second_lse_full = spread_rows(second_out, second_lse, 2)
    third_full, third_lse_full = spread_rows(third_out, third_lse, 4)
    peak = jnp.maximum(jnp.maximum(first_lse, second_lse_full), third_lse_full)
    weight_one = jnp.exp(first_lse - peak)
    weight_two = jnp.exp(second_lse_full - peak)
    weight_three = jnp.exp(third_lse_full - peak)
    denominator = jnp.repeat(weight_one + weight_two + weight_three, HEAD_DIM, axis=1)
    numerator = jnp.repeat(weight_one, HEAD_DIM, axis=1) * first_out
    numerator = numerator + jnp.repeat(weight_two, HEAD_DIM, axis=1) * second_full
    numerator = numerator + jnp.repeat(weight_three, HEAD_DIM, axis=1) * third_full
    return (numerator / denominator).astype(jnp.bfloat16)


STRIDES = 4
LANES = 128
SPAN = STRIDES * LANES
TAIL = 8
LOG2E = 1.4426950408889634
FACTOR = HEAD_DIM ** (-0.5) * LOG2E
LEAST_TOTAL = 2.0 ** -60
MOST_TOTAL = 2.0 ** 100
VMEM_BYTES = 60 * 1024 * 1024


def dot_nn(left, right):
    return lax.dot_general(left, right, (((1,), (0,)), ((), ())), preferred_element_type=jnp.float32)


def dot_nt(left, right):
    return lax.dot_general(left, right, (((1,), (1,)), ((), ())), preferred_element_type=jnp.float32)


def one_hot(shape, which):
    rows = lax.broadcasted_iota(jnp.int32, shape, 0)
    columns = lax.broadcasted_iota(jnp.int32, shape, 1)
    return jnp.where(which(rows, columns), 1.0, 0.0).astype(jnp.bfloat16)


def call(kernel, outs, args, scratch, flops):
    return pl.pallas_call(
        kernel,
        out_shape=outs,
        in_specs=[pl.BlockSpec(memory_space=pltpu.VMEM)] * len(args),
        out_specs=jax.tree.map(lambda out: pl.BlockSpec(memory_space=pltpu.VMEM), outs),
        scratch_shapes=scratch,
        compiler_params=pltpu.CompilerParams(vmem_limit_bytes=VMEM_BYTES),
        cost_estimate=pl.CostEstimate(flops=flops, bytes_accessed=2 << 20, transcendentals=0),
    )(*args)


def pack_kernel(q_ref, k_ref, v_ref, m0, m1, m2, m3, by_head):
    width, rows = q_ref.shape
    heads = width // HEAD_DIM
    for parity in range(2):
        pick = one_hot(
            (SPAN, 2 * LANES), lambda row, column: row == column % LANES * STRIDES + column // LANES * 2 + parity
        )
        mine = range(parity, heads, 2)
        for block in range(rows // SPAN):
            pieces = [
                ref[pl.ds(head * HEAD_DIM, HEAD_DIM), pl.ds(block * SPAN, SPAN)]
                for head in mine
                for ref in (q_ref, k_ref, v_ref)
            ]
            picked = dot_nn(jnp.concatenate(pieces, axis=0), pick).astype(jnp.bfloat16)
            for at, head in enumerate(mine):
                features = picked[at * 3 * HEAD_DIM : (at + 1) * 3 * HEAD_DIM]
                for klass in range(2):
                    phase = (head + 2 * klass) % STRIDES // 2
                    by_head[head, :, pl.ds(klass * rows // STRIDES + block * LANES, LANES)] = features[
                        :, phase * LANES : (phase + 1) * LANES
                    ]
    me = lax.axis_index("seq")
    for shift, message in enumerate((m0, m1, m2, m3)):
        message[...] = by_head[lax.rem(me + shift, heads)]


def with_ones(block):
    count = block.shape[1]
    extra = one_hot((2 * TAIL, count), lambda row, column: row == 0)
    return jnp.concatenate([block, extra], axis=0)


def upright(block):
    count = block.shape[1]
    size = min(count, 2 * LANES)
    eye = one_hot((size, size), lambda row, column: row == column)
    pieces = [dot_nt(eye, block[:, at : at + size]) for at in range(0, count, size)]
    return jnp.concatenate(pieces, axis=0).astype(jnp.bfloat16)


def plain(keys, queries, values):
    return dot_nn(values, jnp.exp2(dot_nn(keys, queries) * FACTOR).astype(jnp.bfloat16))


def shifted(keys, queries, values):
    scores = dot_nn(keys, queries)
    top = jnp.max(scores, axis=0, keepdims=True) * FACTOR
    return dot_nn(values, jnp.exp2(scores * FACTOR - top).astype(jnp.bfloat16)), top


def in_range(totals):
    low = functools.reduce(jnp.minimum, totals)
    high = functools.reduce(jnp.maximum, totals)
    return jnp.logical_and(jnp.min(low) >= LEAST_TOTAL, jnp.max(high) <= MOST_TOTAL)


def near_kernel(qt_ref, kt_ref, vt_ref, out_ref, keys_ref):
    width, rows = qt_ref.shape
    heads = width // HEAD_DIM
    keys = upright(kt_ref[...])
    for head in range(heads):
        keys_ref[head] = keys[:, head * HEAD_DIM : (head + 1) * HEAD_DIM]
    totals = []
    for head in range(heads):
        features = pl.ds(head * HEAD_DIM, HEAD_DIM)
        values = with_ones(vt_ref[features, :])
        for start in range(0, rows, SPAN):
            lanes = pl.ds(start, SPAN)
            result = plain(keys_ref[head], qt_ref[features, lanes], values)
            out_ref[head, :, lanes] = result[: HEAD_DIM + TAIL]
            totals.append(result[HEAD_DIM : HEAD_DIM + 1])

    @pl.when(jnp.logical_not(in_range(totals)))
    def again():
        @pl.loop(0, heads)
        def one_head(head):
            features = pl.ds(pl.multiple_of(head * HEAD_DIM, 16), HEAD_DIM)
            values = with_ones(vt_ref[features, :])
            for start in range(0, rows, 2 * LANES):
                lanes = pl.ds(start, 2 * LANES)
                result, top = shifted(keys_ref[head], qt_ref[features, lanes], values)
                out_ref[head, :, lanes] = result[: HEAD_DIM + TAIL]
                out_ref[head, pl.ds(HEAD_DIM + 1, 1), lanes] = top


def finished(result, top):
    total = result[HEAD_DIM : HEAD_DIM + 1]
    lse = jnp.log2(total) if top is None else top + jnp.log2(total)
    high = lse.astype(jnp.bfloat16).astype(jnp.float32)
    middle = (lse - high).astype(jnp.bfloat16).astype(jnp.float32)
    low = lse - high - middle
    row = lax.broadcasted_iota(jnp.int32, (TAIL, total.shape[1]), 0)
    parts = jnp.where(row == 0, high, jnp.where(row == 1, middle, jnp.where(row == 2, low, 0.0)))
    return jnp.concatenate([result[:HEAD_DIM] / total, parts], axis=0).astype(jnp.bfloat16)


def far_kernel(m0, m1, m2, m3, o0, o1, o2, o3, keys_ref, queries_ref, values_ref):
    count = m0.shape[1]
    half = count // 2
    sources, outs = (m0, m1, m2, m3), (o0, o1, o2, o3)
    twice = jnp.where(lax.broadcasted_iota(jnp.int32, (1, count), 1) < half, 2.0, 1.0).astype(jnp.bfloat16)
    for at, source in enumerate(sources):
        keys_ref[pl.ds(at * count, count), :] = upright(source[pl.ds(HEAD_DIM, HEAD_DIM), :])
        values = with_ones(source[pl.ds(2 * HEAD_DIM, HEAD_DIM), :])
        values_ref[0, :, pl.ds(at * count, count)] = values * twice
        values_ref[1, :, pl.ds(at * count, count)] = values
        for klass in range(2):
            queries_ref[klass, :, pl.ds(at * half, half)] = source[pl.ds(0, HEAD_DIM), pl.ds(klass * half, half)]
    totals = []
    for klass in range(2):
        for pair in range(0, len(sources), 2):
            queries = queries_ref[klass, :, pl.ds(pair * half, count)]
            result = plain(keys_ref[...], queries, values_ref[klass])
            done = finished(result, None)
            totals.append(result[HEAD_DIM : HEAD_DIM + 1])
            for at in range(2):
                outs[pair + at][:, pl.ds(klass * half, half)] = done[:, at * half : (at + 1) * half]

    @pl.when(jnp.logical_not(in_range(totals)))
    def again():
        @pl.loop(0, 2)
        def one_class(klass):
            for at, out in enumerate(outs):
                result, top = shifted(keys_ref[...], queries_ref[klass, :, pl.ds(at * half, half)], values_ref[klass])
                out[:, pl.ds(pl.multiple_of(klass * half, LANES), half)] = finished(result, top)


def merge_kernel(near_ref, g0, g1, g2, g3, out_ref, by_head):
    heads, _, rows = near_ref.shape
    half = rows // STRIDES
    me = lax.axis_index("seq")
    for shift, result in enumerate((g0, g1, g2, g3)):
        by_head[lax.rem(me + shift, heads)] = result[...]
    position = lax.broadcasted_iota(jnp.int32, (1, SPAN), 1)
    for parity in range(2):
        place = one_hot(
            (2 * LANES, SPAN), lambda row, column: column == row % LANES * STRIDES + row // LANES * 2 + parity
        )
        used = position % 2 == parity
        for block in range(rows // SPAN):
            lanes = pl.ds(block * SPAN, SPAN)
            mine = range(parity, heads, 2)
            pieces = []
            for head in mine:
                order = [(phase * 2 + parity - head) % STRIDES // 2 for phase in range(2)]
                pieces.append(
                    jnp.concatenate(
                        [by_head[head, :, pl.ds(klass * half + block * LANES, LANES)] for klass in order], axis=1
                    )
                )
            for head, piece in zip(mine, pieces):
                there = dot_nn(piece, place)
                near = near_ref[head, pl.ds(0, HEAD_DIM), lanes]
                total = near_ref[head, pl.ds(HEAD_DIM, 1), lanes]
                top = near_ref[head, pl.ds(HEAD_DIM + 1, 1), lanes]
                lse = there[HEAD_DIM : HEAD_DIM + 1] + there[HEAD_DIM + 1 : HEAD_DIM + 2] + there[HEAD_DIM + 2 : HEAD_DIM + 3]
                near_lse = top + jnp.log2(total)
                peak = jnp.where(used, jnp.maximum(near_lse, lse), near_lse)
                weight = jnp.exp2(top - peak)
                far = jnp.where(used, jnp.exp2(lse - peak), 0.0)
                share = 1.0 / (total * weight + far)
                merged = near * (weight * share) + there[:HEAD_DIM] * (far * share)
                out_ref[pl.ds(head * HEAD_DIM, HEAD_DIM), lanes] = merged.astype(jnp.bfloat16)


def by_rotation(blocks, sign):
    shards = lax.axis_size("seq")
    moved = [blocks[0]]
    for shift in range(1, shards):
        moved.append(lax.ppermute(blocks[shift], "seq", [(i, (i + sign * shift) % shards) for i in range(shards)]))
    return moved


def whole_slide(query_rows, key_rows, value_rows):
    rows, width = query_rows.shape
    heads = width // HEAD_DIM
    count = rows // 2
    bf16, f32 = jnp.bfloat16, jnp.float32
    turned = [block.T for block in (query_rows, key_rows, value_rows)]
    messages = call(
        pack_kernel,
        [jax.ShapeDtypeStruct((3 * HEAD_DIM, count), bf16)] * heads,
        turned,
        [pltpu.VMEM((heads, 3 * HEAD_DIM, count), bf16)],
        1 << 28,
    )
    arrived = by_rotation(messages, 1)
    near = call(
        near_kernel,
        jax.ShapeDtypeStruct((heads, HEAD_DIM + TAIL, rows), f32),
        turned,
        [pltpu.VMEM((heads, rows, HEAD_DIM), bf16)],
        4 * heads * rows * rows * 256,
    )
    far = call(
        far_kernel,
        [jax.ShapeDtypeStruct((HEAD_DIM + TAIL, count), bf16)] * heads,
        arrived,
        [
            pltpu.VMEM((heads * count, HEAD_DIM), bf16),
            pltpu.VMEM((2, HEAD_DIM, heads * count // 2), bf16),
            pltpu.VMEM((2, HEAD_DIM + 2 * TAIL, heads * count), bf16),
        ],
        4 * heads * rows * rows * 256,
    )
    back = by_rotation(far, -1)
    return call(
        merge_kernel,
        jax.ShapeDtypeStruct((width, rows), bf16),
        [near, *back],
        [pltpu.VMEM((heads, HEAD_DIM + TAIL, count), bf16)],
        1 << 28,
    ).T


def per_device(query_rows, key_rows, value_rows):
    rows, width = query_rows.shape
    shards = lax.axis_size("seq")
    if rows == SEG_A and rows * shards == SEG_B and width == shards * HEAD_DIM and shards == STRIDES:
        return whole_slide(query_rows, key_rows, value_rows)
    return any_length(query_rows, key_rows, value_rows)


def solution(mesh):
    return jax.shard_map(
        per_device,
        mesh=mesh,
        in_specs=(
            P(("slides", "seq"), "head"),
            P(("slides", "seq"), "head"),
            P(("slides", "seq"), "head"),
        ),
        out_specs=P(("slides", "seq"), "head"),
        check_vma=False,
    )
```

```python
import functools
import math

import jax
import jax.numpy as jnp
import numpy as np
from jax import lax
from jax.experimental import pallas as pl
from jax.experimental.pallas import tpu as pltpu
from jax.sharding import PartitionSpec as P

HEAD_DIM = 48
SEG_A = 1024
SEG_B = 4096


def swapped(shard, axis, stride):
    return lax.ppermute(shard, axis, [(i, i ^ 1 << stride) for i in range(lax.axis_size(axis))])


def attend(query_flat, key_flat, value_flat, score_scale):
    local_heads = query_flat.shape[1] // HEAD_DIM
    query_block = query_flat.reshape(query_flat.shape[0], local_heads, HEAD_DIM)
    key_block = key_flat.reshape(key_flat.shape[0], local_heads, HEAD_DIM)
    value_block = value_flat.reshape(value_flat.shape[0], local_heads, HEAD_DIM)
    scores = (
        jnp.einsum("qad,kad->qak", query_block, key_block, preferred_element_type=jnp.float32)
        * score_scale
    )
    row_max = jnp.max(scores, axis=-1)
    exp_scores = jnp.exp(scores - row_max[:, :, None])
    row_total = jnp.sum(exp_scores, axis=-1)
    weighted = jnp.einsum(
        "qak,kad->qad",
        exp_scores.astype(jnp.bfloat16),
        value_block,
        preferred_element_type=jnp.float32,
    )
    level_out = weighted / row_total[:, :, None]
    return (
        level_out.reshape(query_flat.shape[0], local_heads * HEAD_DIM),
        row_max + jnp.log(row_total),
    )


def attend_rows(query_flat, key_flat, value_flat, score_scale):
    count, feature_width = query_flat.shape
    local_heads = feature_width // HEAD_DIM
    keys = key_flat.shape[0]
    rows = math.gcd(count, max(1, 1048576 // (local_heads * keys)))

    def one_piece(query_piece):
        return attend(query_piece, key_flat, value_flat, score_scale)

    outs, lses = lax.map(one_piece, query_flat.reshape(count // rows, rows, feature_width))
    return (outs.reshape(count, feature_width), lses.reshape(count, local_heads))


def local_segments(query_flat, key_flat, value_flat, seg_rows, score_scale):
    count, feature_width = query_flat.shape
    local_heads = feature_width // HEAD_DIM
    shape = (count // seg_rows, seg_rows, feature_width)

    def one_segment(parts):
        return attend_rows(parts[0], parts[1], parts[2], score_scale)

    outs, lses = lax.map(
        one_segment, (query_flat.reshape(shape), key_flat.reshape(shape), value_flat.reshape(shape))
    )
    return (outs.reshape(count, feature_width), lses.reshape(count, local_heads))


def pick_rows(block, stride):
    row_count, feature_width = block.shape
    local_heads = feature_width // HEAD_DIM
    grid = block.reshape(row_count // stride, stride * feature_width)
    columns = []
    for head in range(local_heads):
        begin = head % stride * feature_width + head * HEAD_DIM
        columns.append(grid[:, begin : begin + HEAD_DIM])
    return jnp.concatenate(columns, axis=1)


def spread_rows(level_out, level_lse, stride):
    used_count, feature_width = level_out.shape
    local_heads = feature_width // HEAD_DIM
    head_of_column = np.arange(feature_width) // HEAD_DIM
    out_phases = []
    lse_phases = []
    for phase in range(stride):
        column_mask = jnp.asarray((head_of_column % stride == phase).astype(np.float32))
        head_mask = jnp.asarray(np.arange(local_heads) % stride == phase)
        out_phases.append(level_out * column_mask[None, :])
        lse_phases.append(jnp.where(head_mask[None, :], level_lse, -jnp.inf))
    full_out = jnp.stack(out_phases, axis=1).reshape(used_count * stride, feature_width)
    full_lse = jnp.stack(lse_phases, axis=1).reshape(used_count * stride, local_heads)
    return (full_out, full_lse)


def fold_block(fold_state, queries, keys, values, valid, score_scale):
    running_max, running_total, running_acc = fold_state
    local_heads = queries.shape[1] // HEAD_DIM
    query_block = queries.reshape(queries.shape[0], local_heads, HEAD_DIM)
    key_block = keys.reshape(keys.shape[0], local_heads, HEAD_DIM)
    value_block = values.reshape(values.shape[0], local_heads, HEAD_DIM)
    scores = (
        jnp.einsum("qad,kad->qak", query_block, key_block, preferred_element_type=jnp.float32)
        * score_scale
    )
    scores = jnp.where(valid[None, None, :], scores, -jnp.inf)
    new_max = jnp.maximum(running_max, jnp.max(scores, axis=-1))
    safe_max = jnp.where(new_max == -jnp.inf, 0.0, new_max)
    rescale = jnp.exp(running_max - safe_max)
    exp_scores = jnp.exp(scores - safe_max[:, :, None])
    new_total = running_total * rescale + jnp.sum(exp_scores, axis=-1)
    weighted = jnp.einsum(
        "qak,kad->qad",
        exp_scores.astype(jnp.bfloat16),
        value_block,
        preferred_element_type=jnp.float32,
    )
    new_acc = running_acc * rescale[:, :, None] + weighted
    return (new_max, new_total, new_acc)


def any_length(query_rows, key_rows, value_rows):
    row_count = query_rows.shape[0]
    feature_width = query_rows.shape[1]
    local_heads = feature_width // HEAD_DIM
    shards = lax.axis_size("seq")
    score_scale = HEAD_DIM ** (-0.5)
    first_out, first_lse = local_segments(query_rows, key_rows, value_rows, SEG_A, score_scale)
    used_two = row_count // 2
    seg_two = SEG_B // 2
    query_two = pick_rows(query_rows, 2)
    key_two = pick_rows(key_rows, 2)
    value_two = pick_rows(value_rows, 2)
    stacked = jnp.stack([key_two, value_two])
    for bit_index in range((seg_two // used_two).bit_length() - 1):
        partner = swapped(stacked, "seq", bit_index)
        stacked = jnp.concatenate([stacked, partner], axis=1)
    second_out, second_lse = attend_rows(query_two, stacked[0], stacked[1], score_scale)
    span_tokens = row_count * shards
    group_span = span_tokens // row_count
    used_three = row_count // 4
    wide_queries = pick_rows(query_rows, 4)
    wide_keys = pick_rows(key_rows, 4)
    wide_values = pick_rows(value_rows, 4)
    my_group = lax.axis_index("seq") // group_span
    key_limit = max(1, 1048576 // (local_heads * used_three))
    initial = (
        jnp.full((used_three, local_heads), -jnp.inf, jnp.float32),
        jnp.zeros((used_three, local_heads), jnp.float32),
        jnp.zeros((used_three, local_heads, HEAD_DIM), jnp.float32),
    )
    pieces = (
        lax.all_gather(wide_keys, "seq", axis=0, tiled=True),
        lax.all_gather(wide_values, "seq", axis=0, tiled=True),
    )
    piece_rows = pieces[0].shape[0]
    block = math.gcd(piece_rows, key_limit)
    key_blocks = pieces[0].reshape(piece_rows // block, block, feature_width)
    value_blocks = pieces[1].reshape(piece_rows // block, block, feature_width)
    block_starts = jnp.arange(piece_rows // block, dtype=jnp.int32) * block

    def fold_step(inner_state, items):
        owners = (items[2] + jnp.arange(block, dtype=jnp.int32)) // used_three
        valid = owners // group_span == my_group
        return (fold_block(inner_state, wide_queries, items[0], items[1], valid, score_scale), None)

    final_state, unused = lax.scan(fold_step, initial, (key_blocks, value_blocks, block_starts))
    final_max, final_total, final_acc = final_state
    third_out = (final_acc / final_total[:, :, None]).reshape(used_three, feature_width)
    third_lse = final_max + jnp.log(final_total)
    second_full, second_lse_full = spread_rows(second_out, second_lse, 2)
    third_full, third_lse_full = spread_rows(third_out, third_lse, 4)
    peak = jnp.maximum(jnp.maximum(first_lse, second_lse_full), third_lse_full)
    weight_one = jnp.exp(first_lse - peak)
    weight_two = jnp.exp(second_lse_full - peak)
    weight_three = jnp.exp(third_lse_full - peak)
    denominator = jnp.repeat(weight_one + weight_two + weight_three, HEAD_DIM, axis=1)
    numerator = jnp.repeat(weight_one, HEAD_DIM, axis=1) * first_out
    numerator = numerator + jnp.repeat(weight_two, HEAD_DIM, axis=1) * second_full
    numerator = numerator + jnp.repeat(weight_three, HEAD_DIM, axis=1) * third_full
    return (numerator / denominator).astype(jnp.bfloat16)


STRIDES = 4
LANES = 128
SPAN = STRIDES * LANES
NEAR_KEYS = 256
TAIL = 8
LOG2E = 1.4426950408889634
FACTOR = HEAD_DIM ** (-0.5) * LOG2E
LEAST_TOTAL = 2.0 ** -60
MOST_TOTAL = 2.0 ** 100
VMEM_BYTES = 16 * 1024 * 1024


def dot_nn(left, right):
    return lax.dot_general(left, right, (((1,), (0,)), ((), ())), preferred_element_type=jnp.float32)


def dot_nt(left, right):
    return lax.dot_general(left, right, (((1,), (1,)), ((), ())), preferred_element_type=jnp.float32)


def one_hot(shape, which):
    rows = lax.broadcasted_iota(jnp.int32, shape, 0)
    columns = lax.broadcasted_iota(jnp.int32, shape, 1)
    return jnp.where(which(rows, columns), 1.0, 0.0).astype(jnp.bfloat16)


def call(kernel, outs, args, scratch, flops):
    return pl.pallas_call(
        kernel,
        out_shape=outs,
        in_specs=[pl.BlockSpec(memory_space=pltpu.VMEM)] * len(args),
        out_specs=jax.tree.map(lambda out: pl.BlockSpec(memory_space=pltpu.VMEM), outs),
        scratch_shapes=scratch,
        compiler_params=pltpu.CompilerParams(vmem_limit_bytes=VMEM_BYTES),
        cost_estimate=pl.CostEstimate(flops=flops, bytes_accessed=2 << 20, transcendentals=0),
    )(*args)


def pack_kernel(q_ref, k_ref, v_ref, m0, m1, m2, m3, by_head):
    width, rows = q_ref.shape
    heads = width // HEAD_DIM
    for parity in range(2):
        pick = one_hot(
            (SPAN, 2 * LANES), lambda row, column: row == column % LANES * STRIDES + column // LANES * 2 + parity
        )
        mine = range(parity, heads, 2)
        for block in range(rows // SPAN):
            pieces = [
                ref[pl.ds(head * HEAD_DIM, HEAD_DIM), pl.ds(block * SPAN, SPAN)]
                for head in mine
                for ref in (q_ref, k_ref, v_ref)
            ]
            picked = dot_nn(jnp.concatenate(pieces, axis=0), pick).astype(jnp.bfloat16)
            for at, head in enumerate(mine):
                features = picked[at * 3 * HEAD_DIM : (at + 1) * 3 * HEAD_DIM]
                for klass in range(2):
                    phase = (head + 2 * klass) % STRIDES // 2
                    by_head[head, :, pl.ds(klass * rows // STRIDES + block * LANES, LANES)] = features[
                        :, phase * LANES : (phase + 1) * LANES
                    ]
    me = lax.axis_index("seq")
    for shift, message in enumerate((m0, m1, m2, m3)):
        message[...] = by_head[lax.rem(me + shift, heads)]


def with_ones(block):
    count = block.shape[1]
    extra = one_hot((2 * TAIL, count), lambda row, column: row == 0)
    return jnp.concatenate([block, extra], axis=0)


def upright(block):
    count = block.shape[1]
    size = min(count, 2 * LANES)
    eye = one_hot((size, size), lambda row, column: row == column)
    pieces = [dot_nt(eye, block[:, at : at + size]) for at in range(0, count, size)]
    return jnp.concatenate(pieces, axis=0).astype(jnp.bfloat16)


def plain(keys, queries, values):
    return dot_nn(values, jnp.exp2(dot_nn(keys, queries) * FACTOR).astype(jnp.bfloat16))


def shifted(keys, queries, values):
    scores = dot_nn(keys, queries)
    top = jnp.max(scores, axis=0, keepdims=True) * FACTOR
    return dot_nn(values, jnp.exp2(scores * FACTOR - top).astype(jnp.bfloat16)), top


def in_range(totals):
    low = functools.reduce(jnp.minimum, totals)
    high = functools.reduce(jnp.maximum, totals)
    return jnp.logical_and(jnp.min(low) >= LEAST_TOTAL, jnp.max(high) <= MOST_TOTAL)


def near_kernel(qt_ref, kt_ref, vt_ref, out_ref, keys_ref):
    width, rows = qt_ref.shape
    heads = width // HEAD_DIM
    keys = upright(kt_ref[...])
    for head in range(heads):
        keys_ref[head] = keys[:, head * HEAD_DIM : (head + 1) * HEAD_DIM]
    blocks = [(head, start) for head in range(heads) for start in range(0, rows, SPAN)]
    pieces = range(0, rows, NEAR_KEYS)

    def scores_of(block, piece):
        head, start = block
        queries = qt_ref[pl.ds(head * HEAD_DIM, HEAD_DIM), pl.ds(start, SPAN)]
        return dot_nn(keys_ref[head, pl.ds(piece, NEAR_KEYS), :], queries)

    def folded(values, join, held):
        parts = [values[at : at + 8] for at in range(0, NEAR_KEYS, 8)]
        return functools.reduce(join, parts if held is None else [held, *parts])

    now, peaks = [], None
    for piece in pieces:
        now.append(scores_of(blocks[0], piece))
        peaks = folded(now[-1], jnp.maximum, peaks)
    for at, (head, start) in enumerate(blocks):
        top = jnp.max(peaks, axis=0, keepdims=True) * FACTOR
        later, peaks, result, totals = [], None, None, None
        for piece, scores in zip(pieces, now):
            if at + 1 < len(blocks):
                later.append(scores_of(blocks[at + 1], piece))
                peaks = folded(later[-1], jnp.maximum, peaks)
            probs = jnp.exp2(scores * FACTOR - top)
            totals = folded(probs, jnp.add, totals)
            values = vt_ref[pl.ds(head * HEAD_DIM, HEAD_DIM), pl.ds(piece, NEAR_KEYS)]
            term = dot_nn(values, probs.astype(jnp.bfloat16))
            result = term if result is None else result + term
        lanes = pl.ds(start, SPAN)
        out_ref[head, pl.ds(0, HEAD_DIM), lanes] = result
        out_ref[head, pl.ds(HEAD_DIM, 1), lanes] = jnp.sum(totals, axis=0, keepdims=True)
        out_ref[head, pl.ds(HEAD_DIM + 1, 1), lanes] = top
        now = later


def finished(result, top):
    total = result[HEAD_DIM : HEAD_DIM + 1]
    lse = jnp.log2(total) if top is None else top + jnp.log2(total)
    high = lse.astype(jnp.bfloat16).astype(jnp.float32)
    middle = (lse - high).astype(jnp.bfloat16).astype(jnp.float32)
    low = lse - high - middle
    row = lax.broadcasted_iota(jnp.int32, (TAIL, total.shape[1]), 0)
    parts = jnp.where(row == 0, high, jnp.where(row == 1, middle, jnp.where(row == 2, low, 0.0)))
    return jnp.concatenate([result[:HEAD_DIM] / total, parts], axis=0).astype(jnp.bfloat16)


def far_kernel(m0, m1, m2, m3, o0, o1, o2, o3, keys_ref, queries_ref, values_ref):
    count = m0.shape[1]
    half = count // 2
    sources, outs = (m0, m1, m2, m3), (o0, o1, o2, o3)
    twice = jnp.where(lax.broadcasted_iota(jnp.int32, (1, count), 1) < half, 2.0, 1.0).astype(jnp.bfloat16)
    for at, source in enumerate(sources):
        keys_ref[pl.ds(at * count, count), :] = upright(source[pl.ds(HEAD_DIM, HEAD_DIM), :])
        values = with_ones(source[pl.ds(2 * HEAD_DIM, HEAD_DIM), :])
        values_ref[0, :, pl.ds(at * count, count)] = values * twice
        values_ref[1, :, pl.ds(at * count, count)] = values
        for klass in range(2):
            queries_ref[klass, :, pl.ds(at * half, half)] = source[pl.ds(0, HEAD_DIM), pl.ds(klass * half, half)]
    totals = []
    for klass in range(2):
        for pair in range(0, len(sources), 2):
            queries = queries_ref[klass, :, pl.ds(pair * half, count)]
            result = plain(keys_ref[...], queries, values_ref[klass])
            done = finished(result, None)
            totals.append(result[HEAD_DIM : HEAD_DIM + 1])
            for at in range(2):
                outs[pair + at][:, pl.ds(klass * half, half)] = done[:, at * half : (at + 1) * half]

    @pl.when(jnp.logical_not(in_range(totals)))
    def again():
        @pl.loop(0, 2)
        def one_class(klass):
            for at, out in enumerate(outs):
                result, top = shifted(keys_ref[...], queries_ref[klass, :, pl.ds(at * half, half)], values_ref[klass])
                out[:, pl.ds(pl.multiple_of(klass * half, LANES), half)] = finished(result, top)


def merge_kernel(near_ref, g0, g1, g2, g3, out_ref, by_head):
    heads, _, rows = near_ref.shape
    half = rows // STRIDES
    me = lax.axis_index("seq")
    for shift, result in enumerate((g0, g1, g2, g3)):
        by_head[lax.rem(me + shift, heads)] = result[...]
    position = lax.broadcasted_iota(jnp.int32, (1, SPAN), 1)
    for parity in range(2):
        place = one_hot(
            (2 * LANES, SPAN), lambda row, column: column == row % LANES * STRIDES + row // LANES * 2 + parity
        )
        used = position % 2 == parity
        for block in range(rows // SPAN):
            lanes = pl.ds(block * SPAN, SPAN)
            mine = range(parity, heads, 2)
            pieces = []
            for head in mine:
                order = [(phase * 2 + parity - head) % STRIDES // 2 for phase in range(2)]
                pieces.append(
                    jnp.concatenate(
                        [by_head[head, :, pl.ds(klass * half + block * LANES, LANES)] for klass in order], axis=1
                    )
                )
            for head, piece in zip(mine, pieces):
                there = dot_nn(piece, place)
                near = near_ref[head, pl.ds(0, HEAD_DIM), lanes]
                total = near_ref[head, pl.ds(HEAD_DIM, 1), lanes]
                top = near_ref[head, pl.ds(HEAD_DIM + 1, 1), lanes]
                lse = there[HEAD_DIM : HEAD_DIM + 1] + there[HEAD_DIM + 1 : HEAD_DIM + 2] + there[HEAD_DIM + 2 : HEAD_DIM + 3]
                near_lse = top + jnp.log2(total)
                peak = jnp.where(used, jnp.maximum(near_lse, lse), near_lse)
                weight = jnp.exp2(top - peak)
                far = jnp.where(used, jnp.exp2(lse - peak), 0.0)
                share = 1.0 / (total * weight + far)
                merged = near * (weight * share) + there[:HEAD_DIM] * (far * share)
                out_ref[pl.ds(head * HEAD_DIM, HEAD_DIM), lanes] = merged.astype(jnp.bfloat16)


def by_rotation(blocks, sign):
    shards = lax.axis_size("seq")
    moved = [blocks[0]]
    for shift in range(1, shards):
        moved.append(lax.ppermute(blocks[shift], "seq", [(i, (i + sign * shift) % shards) for i in range(shards)]))
    return moved


def whole_slide(query_rows, key_rows, value_rows):
    rows, width = query_rows.shape
    heads = width // HEAD_DIM
    count = rows // 2
    bf16, f32 = jnp.bfloat16, jnp.float32
    turned = [block.T for block in (query_rows, key_rows, value_rows)]
    messages = call(
        pack_kernel,
        [jax.ShapeDtypeStruct((3 * HEAD_DIM, count), bf16)] * heads,
        turned,
        [pltpu.VMEM((heads, 3 * HEAD_DIM, count), bf16)],
        1 << 28,
    )
    arrived = by_rotation(messages, 1)
    near = call(
        near_kernel,
        jax.ShapeDtypeStruct((heads, HEAD_DIM + TAIL, rows), f32),
        turned,
        [pltpu.VMEM((heads, rows, HEAD_DIM), bf16)],
        4 * heads * rows * rows * 256,
    )
    near, *arrived = lax.optimization_barrier((near, *arrived))
    far = call(
        far_kernel,
        [jax.ShapeDtypeStruct((HEAD_DIM + TAIL, count), bf16)] * heads,
        arrived,
        [
            pltpu.VMEM((heads * count, HEAD_DIM), bf16),
            pltpu.VMEM((2, HEAD_DIM, heads * count // 2), bf16),
            pltpu.VMEM((2, HEAD_DIM + 2 * TAIL, heads * count), bf16),
        ],
        4 * heads * rows * rows * 256,
    )
    back = by_rotation(far, -1)
    return call(
        merge_kernel,
        jax.ShapeDtypeStruct((width, rows), bf16),
        [near, *back],
        [pltpu.VMEM((heads, HEAD_DIM + TAIL, count), bf16)],
        1 << 28,
    ).T


def per_device(query_rows, key_rows, value_rows):
    rows, width = query_rows.shape
    shards = lax.axis_size("seq")
    if rows == SEG_A and rows * shards == SEG_B and width == shards * HEAD_DIM and shards == STRIDES:
        return whole_slide(query_rows, key_rows, value_rows)
    return any_length(query_rows, key_rows, value_rows)


def solution(mesh):
    return jax.shard_map(
        per_device,
        mesh=mesh,
        in_specs=(
            P(("slides", "seq"), "head"),
            P(("slides", "seq"), "head"),
            P(("slides", "seq"), "head"),
        ),
        out_specs=P(("slides", "seq"), "head"),
        check_vma=False,
    )
```

```python
import functools
import math

import jax
import jax.numpy as jnp
import numpy as np
from jax import lax
from jax.experimental import pallas as pl
from jax.experimental.pallas import tpu as pltpu
from jax.sharding import PartitionSpec as P

HEAD_DIM = 48
SEG_A = 1024
SEG_B = 4096


def swapped(shard, axis, stride):
    return lax.ppermute(shard, axis, [(i, i ^ 1 << stride) for i in range(lax.axis_size(axis))])


def attend(query_flat, key_flat, value_flat, score_scale):
    local_heads = query_flat.shape[1] // HEAD_DIM
    query_block = query_flat.reshape(query_flat.shape[0], local_heads, HEAD_DIM)
    key_block = key_flat.reshape(key_flat.shape[0], local_heads, HEAD_DIM)
    value_block = value_flat.reshape(value_flat.shape[0], local_heads, HEAD_DIM)
    scores = (
        jnp.einsum("qad,kad->qak", query_block, key_block, preferred_element_type=jnp.float32)
        * score_scale
    )
    row_max = jnp.max(scores, axis=-1)
    exp_scores = jnp.exp(scores - row_max[:, :, None])
    row_total = jnp.sum(exp_scores, axis=-1)
    weighted = jnp.einsum(
        "qak,kad->qad",
        exp_scores.astype(jnp.bfloat16),
        value_block,
        preferred_element_type=jnp.float32,
    )
    level_out = weighted / row_total[:, :, None]
    return (
        level_out.reshape(query_flat.shape[0], local_heads * HEAD_DIM),
        row_max + jnp.log(row_total),
    )


def attend_rows(query_flat, key_flat, value_flat, score_scale):
    count, feature_width = query_flat.shape
    local_heads = feature_width // HEAD_DIM
    keys = key_flat.shape[0]
    rows = math.gcd(count, max(1, 1048576 // (local_heads * keys)))

    def one_piece(query_piece):
        return attend(query_piece, key_flat, value_flat, score_scale)

    outs, lses = lax.map(one_piece, query_flat.reshape(count // rows, rows, feature_width))
    return (outs.reshape(count, feature_width), lses.reshape(count, local_heads))


def local_segments(query_flat, key_flat, value_flat, seg_rows, score_scale):
    count, feature_width = query_flat.shape
    local_heads = feature_width // HEAD_DIM
    shape = (count // seg_rows, seg_rows, feature_width)

    def one_segment(parts):
        return attend_rows(parts[0], parts[1], parts[2], score_scale)

    outs, lses = lax.map(
        one_segment, (query_flat.reshape(shape), key_flat.reshape(shape), value_flat.reshape(shape))
    )
    return (outs.reshape(count, feature_width), lses.reshape(count, local_heads))


def pick_rows(block, stride):
    row_count, feature_width = block.shape
    local_heads = feature_width // HEAD_DIM
    grid = block.reshape(row_count // stride, stride * feature_width)
    columns = []
    for head in range(local_heads):
        begin = head % stride * feature_width + head * HEAD_DIM
        columns.append(grid[:, begin : begin + HEAD_DIM])
    return jnp.concatenate(columns, axis=1)


def spread_rows(level_out, level_lse, stride):
    used_count, feature_width = level_out.shape
    local_heads = feature_width // HEAD_DIM
    head_of_column = np.arange(feature_width) // HEAD_DIM
    out_phases = []
    lse_phases = []
    for phase in range(stride):
        column_mask = jnp.asarray((head_of_column % stride == phase).astype(np.float32))
        head_mask = jnp.asarray(np.arange(local_heads) % stride == phase)
        out_phases.append(level_out * column_mask[None, :])
        lse_phases.append(jnp.where(head_mask[None, :], level_lse, -jnp.inf))
    full_out = jnp.stack(out_phases, axis=1).reshape(used_count * stride, feature_width)
    full_lse = jnp.stack(lse_phases, axis=1).reshape(used_count * stride, local_heads)
    return (full_out, full_lse)


def fold_block(fold_state, queries, keys, values, valid, score_scale):
    running_max, running_total, running_acc = fold_state
    local_heads = queries.shape[1] // HEAD_DIM
    query_block = queries.reshape(queries.shape[0], local_heads, HEAD_DIM)
    key_block = keys.reshape(keys.shape[0], local_heads, HEAD_DIM)
    value_block = values.reshape(values.shape[0], local_heads, HEAD_DIM)
    scores = (
        jnp.einsum("qad,kad->qak", query_block, key_block, preferred_element_type=jnp.float32)
        * score_scale
    )
    scores = jnp.where(valid[None, None, :], scores, -jnp.inf)
    new_max = jnp.maximum(running_max, jnp.max(scores, axis=-1))
    safe_max = jnp.where(new_max == -jnp.inf, 0.0, new_max)
    rescale = jnp.exp(running_max - safe_max)
    exp_scores = jnp.exp(scores - safe_max[:, :, None])
    new_total = running_total * rescale + jnp.sum(exp_scores, axis=-1)
    weighted = jnp.einsum(
        "qak,kad->qad",
        exp_scores.astype(jnp.bfloat16),
        value_block,
        preferred_element_type=jnp.float32,
    )
    new_acc = running_acc * rescale[:, :, None] + weighted
    return (new_max, new_total, new_acc)


def any_length(query_rows, key_rows, value_rows):
    row_count = query_rows.shape[0]
    feature_width = query_rows.shape[1]
    local_heads = feature_width // HEAD_DIM
    shards = lax.axis_size("seq")
    score_scale = HEAD_DIM ** (-0.5)
    first_out, first_lse = local_segments(query_rows, key_rows, value_rows, SEG_A, score_scale)
    used_two = row_count // 2
    seg_two = SEG_B // 2
    query_two = pick_rows(query_rows, 2)
    key_two = pick_rows(key_rows, 2)
    value_two = pick_rows(value_rows, 2)
    stacked = jnp.stack([key_two, value_two])
    for bit_index in range((seg_two // used_two).bit_length() - 1):
        partner = swapped(stacked, "seq", bit_index)
        stacked = jnp.concatenate([stacked, partner], axis=1)
    second_out, second_lse = attend_rows(query_two, stacked[0], stacked[1], score_scale)
    span_tokens = row_count * shards
    group_span = span_tokens // row_count
    used_three = row_count // 4
    wide_queries = pick_rows(query_rows, 4)
    wide_keys = pick_rows(key_rows, 4)
    wide_values = pick_rows(value_rows, 4)
    my_group = lax.axis_index("seq") // group_span
    key_limit = max(1, 1048576 // (local_heads * used_three))
    initial = (
        jnp.full((used_three, local_heads), -jnp.inf, jnp.float32),
        jnp.zeros((used_three, local_heads), jnp.float32),
        jnp.zeros((used_three, local_heads, HEAD_DIM), jnp.float32),
    )
    pieces = (
        lax.all_gather(wide_keys, "seq", axis=0, tiled=True),
        lax.all_gather(wide_values, "seq", axis=0, tiled=True),
    )
    piece_rows = pieces[0].shape[0]
    block = math.gcd(piece_rows, key_limit)
    key_blocks = pieces[0].reshape(piece_rows // block, block, feature_width)
    value_blocks = pieces[1].reshape(piece_rows // block, block, feature_width)
    block_starts = jnp.arange(piece_rows // block, dtype=jnp.int32) * block

    def fold_step(inner_state, items):
        owners = (items[2] + jnp.arange(block, dtype=jnp.int32)) // used_three
        valid = owners // group_span == my_group
        return (fold_block(inner_state, wide_queries, items[0], items[1], valid, score_scale), None)

    final_state, unused = lax.scan(fold_step, initial, (key_blocks, value_blocks, block_starts))
    final_max, final_total, final_acc = final_state
    third_out = (final_acc / final_total[:, :, None]).reshape(used_three, feature_width)
    third_lse = final_max + jnp.log(final_total)
    second_full, second_lse_full = spread_rows(second_out, second_lse, 2)
    third_full, third_lse_full = spread_rows(third_out, third_lse, 4)
    peak = jnp.maximum(jnp.maximum(first_lse, second_lse_full), third_lse_full)
    weight_one = jnp.exp(first_lse - peak)
    weight_two = jnp.exp(second_lse_full - peak)
    weight_three = jnp.exp(third_lse_full - peak)
    denominator = jnp.repeat(weight_one + weight_two + weight_three, HEAD_DIM, axis=1)
    numerator = jnp.repeat(weight_one, HEAD_DIM, axis=1) * first_out
    numerator = numerator + jnp.repeat(weight_two, HEAD_DIM, axis=1) * second_full
    numerator = numerator + jnp.repeat(weight_three, HEAD_DIM, axis=1) * third_full
    return (numerator / denominator).astype(jnp.bfloat16)


STRIDES = 4
LANES = 128
SPAN = STRIDES * LANES
NEAR_KEYS = 256
TAIL = 8
LOG2E = 1.4426950408889634
FACTOR = HEAD_DIM ** (-0.5) * LOG2E
LEAST_TOTAL = 2.0 ** -60
MOST_TOTAL = 2.0 ** 100
VMEM_BYTES = 16 * 1024 * 1024


def dot_nn(left, right):
    return lax.dot_general(left, right, (((1,), (0,)), ((), ())), preferred_element_type=jnp.float32)


def dot_nt(left, right):
    return lax.dot_general(left, right, (((1,), (1,)), ((), ())), preferred_element_type=jnp.float32)


def one_hot(shape, which):
    rows = lax.broadcasted_iota(jnp.int32, shape, 0)
    columns = lax.broadcasted_iota(jnp.int32, shape, 1)
    return jnp.where(which(rows, columns), 1.0, 0.0).astype(jnp.bfloat16)


def call(kernel, outs, args, scratch, flops, space=pltpu.VMEM):
    return pl.pallas_call(
        kernel,
        out_shape=outs,
        in_specs=[pl.BlockSpec(memory_space=space)] * len(args),
        out_specs=jax.tree.map(lambda out: pl.BlockSpec(memory_space=pltpu.VMEM), outs),
        scratch_shapes=scratch,
        compiler_params=pltpu.CompilerParams(vmem_limit_bytes=VMEM_BYTES),
        cost_estimate=pl.CostEstimate(flops=flops, bytes_accessed=2 << 20, transcendentals=0),
    )(*args)


def pack_kernel(q_hbm, k_hbm, v_hbm, q_ref, k_ref, v_ref, m0, m1, m2, m3, by_head, arrivals):
    width, rows = q_ref.shape
    copies = [
        pltpu.make_async_copy(source, target, arrivals.at[at])
        for at, (source, target) in enumerate(((q_hbm, q_ref), (k_hbm, k_ref), (v_hbm, v_ref)))
    ]
    for copy in copies:
        copy.start()
    for copy in copies:
        copy.wait()
    heads = width // HEAD_DIM
    for parity in range(2):
        pick = one_hot(
            (SPAN, 2 * LANES), lambda row, column: row == column % LANES * STRIDES + column // LANES * 2 + parity
        )
        mine = range(parity, heads, 2)
        for block in range(rows // SPAN):
            pieces = [
                ref[pl.ds(head * HEAD_DIM, HEAD_DIM), pl.ds(block * SPAN, SPAN)]
                for head in mine
                for ref in (q_ref, k_ref, v_ref)
            ]
            picked = dot_nn(jnp.concatenate(pieces, axis=0), pick).astype(jnp.bfloat16)
            for at, head in enumerate(mine):
                features = picked[at * 3 * HEAD_DIM : (at + 1) * 3 * HEAD_DIM]
                for klass in range(2):
                    phase = (head + 2 * klass) % STRIDES // 2
                    by_head[head, :, pl.ds(klass * rows // STRIDES + block * LANES, LANES)] = features[
                        :, phase * LANES : (phase + 1) * LANES
                    ]
    me = lax.axis_index("seq")
    for shift, message in enumerate((m0, m1, m2, m3)):
        message[...] = by_head[lax.rem(me + shift, heads)]


def with_ones(block):
    count = block.shape[1]
    extra = one_hot((2 * TAIL, count), lambda row, column: row == 0)
    return jnp.concatenate([block, extra], axis=0)


def upright(block):
    count = block.shape[1]
    size = min(count, 2 * LANES)
    eye = one_hot((size, size), lambda row, column: row == column)
    pieces = [dot_nt(eye, block[:, at : at + size]) for at in range(0, count, size)]
    return jnp.concatenate(pieces, axis=0).astype(jnp.bfloat16)


def plain(keys, queries, values):
    return dot_nn(values, jnp.exp2(dot_nn(keys, queries) * FACTOR).astype(jnp.bfloat16))


def shifted(keys, queries, values):
    scores = dot_nn(keys, queries)
    top = jnp.max(scores, axis=0, keepdims=True) * FACTOR
    return dot_nn(values, jnp.exp2(scores * FACTOR - top).astype(jnp.bfloat16)), top


def in_range(totals):
    low = functools.reduce(jnp.minimum, totals)
    high = functools.reduce(jnp.maximum, totals)
    return jnp.logical_and(jnp.min(low) >= LEAST_TOTAL, jnp.max(high) <= MOST_TOTAL)


def near_kernel(qt_ref, kt_ref, vt_ref, out_ref, keys_ref):
    width, rows = qt_ref.shape
    heads = width // HEAD_DIM
    keys = upright(kt_ref[...])
    for head in range(heads):
        keys_ref[head] = keys[:, head * HEAD_DIM : (head + 1) * HEAD_DIM]
    blocks = [(head, start) for head in range(heads) for start in range(0, rows, SPAN)]
    pieces = range(0, rows, NEAR_KEYS)

    def scores_of(block, piece):
        head, start = block
        queries = qt_ref[pl.ds(head * HEAD_DIM, HEAD_DIM), pl.ds(start, SPAN)]
        return dot_nn(keys_ref[head, pl.ds(piece, NEAR_KEYS), :], queries)

    def folded(values, join, held):
        parts = [values[at : at + 8] for at in range(0, NEAR_KEYS, 8)]
        return functools.reduce(join, parts if held is None else [held, *parts])

    now, peaks = [], None
    for piece in pieces:
        now.append(scores_of(blocks[0], piece))
        peaks = folded(now[-1], jnp.maximum, peaks)
    for at, (head, start) in enumerate(blocks):
        top = jnp.max(peaks, axis=0, keepdims=True) * FACTOR
        later, peaks, result, totals = [], None, None, None
        for piece, scores in zip(pieces, now):
            if at + 1 < len(blocks):
                later.append(scores_of(blocks[at + 1], piece))
                peaks = folded(later[-1], jnp.maximum, peaks)
            probs = jnp.exp2(scores * FACTOR - top)
            totals = folded(probs, jnp.add, totals)
            values = vt_ref[pl.ds(head * HEAD_DIM, HEAD_DIM), pl.ds(piece, NEAR_KEYS)]
            term = dot_nn(values, probs.astype(jnp.bfloat16))
            result = term if result is None else result + term
        lanes = pl.ds(start, SPAN)
        out_ref[head, pl.ds(0, HEAD_DIM), lanes] = result
        out_ref[head, pl.ds(HEAD_DIM, 1), lanes] = jnp.sum(totals, axis=0, keepdims=True)
        out_ref[head, pl.ds(HEAD_DIM + 1, 1), lanes] = top
        now = later


def finished(result, top):
    total = result[HEAD_DIM : HEAD_DIM + 1]
    lse = jnp.log2(total) if top is None else top + jnp.log2(total)
    high = lse.astype(jnp.bfloat16).astype(jnp.float32)
    middle = (lse - high).astype(jnp.bfloat16).astype(jnp.float32)
    low = lse - high - middle
    row = lax.broadcasted_iota(jnp.int32, (TAIL, total.shape[1]), 0)
    parts = jnp.where(row == 0, high, jnp.where(row == 1, middle, jnp.where(row == 2, low, 0.0)))
    return jnp.concatenate([result[:HEAD_DIM] / total, parts], axis=0).astype(jnp.bfloat16)


def far_kernel(m0, m1, m2, m3, o0, o1, o2, o3, keys_ref, queries_ref, values_ref):
    count = m0.shape[1]
    half = count // 2
    sources, outs = (m0, m1, m2, m3), (o0, o1, o2, o3)
    twice = jnp.where(lax.broadcasted_iota(jnp.int32, (1, count), 1) < half, 2.0, 1.0).astype(jnp.bfloat16)
    for at, source in enumerate(sources):
        keys_ref[pl.ds(at * count, count), :] = upright(source[pl.ds(HEAD_DIM, HEAD_DIM), :])
        values = with_ones(source[pl.ds(2 * HEAD_DIM, HEAD_DIM), :])
        values_ref[0, :, pl.ds(at * count, count)] = values * twice
        values_ref[1, :, pl.ds(at * count, count)] = values
        for klass in range(2):
            queries_ref[klass, :, pl.ds(at * half, half)] = source[pl.ds(0, HEAD_DIM), pl.ds(klass * half, half)]
    totals = []
    for klass in range(2):
        for pair in range(0, len(sources), 2):
            queries = queries_ref[klass, :, pl.ds(pair * half, count)]
            result = plain(keys_ref[...], queries, values_ref[klass])
            done = finished(result, None)
            totals.append(result[HEAD_DIM : HEAD_DIM + 1])
            for at in range(2):
                outs[pair + at][:, pl.ds(klass * half, half)] = done[:, at * half : (at + 1) * half]

    @pl.when(jnp.logical_not(in_range(totals)))
    def again():
        @pl.loop(0, 2)
        def one_class(klass):
            for at, out in enumerate(outs):
                result, top = shifted(keys_ref[...], queries_ref[klass, :, pl.ds(at * half, half)], values_ref[klass])
                out[:, pl.ds(pl.multiple_of(klass * half, LANES), half)] = finished(result, top)


def merge_kernel(near_ref, g0, g1, g2, g3, out_ref, by_head):
    heads, _, rows = near_ref.shape
    half = rows // STRIDES
    me = lax.axis_index("seq")
    for shift, result in enumerate((g0, g1, g2, g3)):
        by_head[lax.rem(me + shift, heads)] = result[...]
    position = lax.broadcasted_iota(jnp.int32, (1, SPAN), 1)
    for parity in range(2):
        place = one_hot(
            (2 * LANES, SPAN), lambda row, column: column == row % LANES * STRIDES + row // LANES * 2 + parity
        )
        used = position % 2 == parity
        for block in range(rows // SPAN):
            lanes = pl.ds(block * SPAN, SPAN)
            mine = range(parity, heads, 2)
            pieces = []
            for head in mine:
                order = [(phase * 2 + parity - head) % STRIDES // 2 for phase in range(2)]
                pieces.append(
                    jnp.concatenate(
                        [by_head[head, :, pl.ds(klass * half + block * LANES, LANES)] for klass in order], axis=1
                    )
                )
            for head, piece in zip(mine, pieces):
                there = dot_nn(piece, place)
                near = near_ref[head, pl.ds(0, HEAD_DIM), lanes]
                total = near_ref[head, pl.ds(HEAD_DIM, 1), lanes]
                top = near_ref[head, pl.ds(HEAD_DIM + 1, 1), lanes]
                lse = there[HEAD_DIM : HEAD_DIM + 1] + there[HEAD_DIM + 1 : HEAD_DIM + 2] + there[HEAD_DIM + 2 : HEAD_DIM + 3]
                near_lse = top + jnp.log2(total)
                peak = jnp.where(used, jnp.maximum(near_lse, lse), near_lse)
                weight = jnp.exp2(top - peak)
                far = jnp.where(used, jnp.exp2(lse - peak), 0.0)
                share = 1.0 / (total * weight + far)
                merged = near * (weight * share) + there[:HEAD_DIM] * (far * share)
                out_ref[pl.ds(head * HEAD_DIM, HEAD_DIM), lanes] = merged.astype(jnp.bfloat16)


def by_rotation(blocks, sign):
    shards = lax.axis_size("seq")
    moved = [blocks[0]]
    for shift in range(1, shards):
        moved.append(lax.ppermute(blocks[shift], "seq", [(i, (i + sign * shift) % shards) for i in range(shards)]))
    return moved


def whole_slide(query_rows, key_rows, value_rows):
    rows, width = query_rows.shape
    heads = width // HEAD_DIM
    count = rows // 2
    bf16, f32 = jnp.bfloat16, jnp.float32
    turned = [pltpu.with_memory_space_constraint(block.T, pltpu.HBM) for block in (query_rows, key_rows, value_rows)]
    *here, m0, m1, m2, m3 = call(
        pack_kernel,
        [jax.ShapeDtypeStruct((width, rows), bf16)] * 3 + [jax.ShapeDtypeStruct((3 * HEAD_DIM, count), bf16)] * heads,
        turned,
        [pltpu.VMEM((heads, 3 * HEAD_DIM, count), bf16), pltpu.SemaphoreType.DMA((3,))],
        1 << 28,
        pltpu.HBM,
    )
    arrived = by_rotation((m0, m1, m2, m3), 1)
    near = call(
        near_kernel,
        jax.ShapeDtypeStruct((heads, HEAD_DIM + TAIL, rows), f32),
        here,
        [pltpu.VMEM((heads, rows, HEAD_DIM), bf16)],
        4 * heads * rows * rows * 256,
    )
    near, *arrived = lax.optimization_barrier((near, *arrived))
    far = call(
        far_kernel,
        [jax.ShapeDtypeStruct((HEAD_DIM + TAIL, count), bf16)] * heads,
        arrived,
        [
            pltpu.VMEM((heads * count, HEAD_DIM), bf16),
            pltpu.VMEM((2, HEAD_DIM, heads * count // 2), bf16),
            pltpu.VMEM((2, HEAD_DIM + 2 * TAIL, heads * count), bf16),
        ],
        4 * heads * rows * rows * 256,
    )
    back = by_rotation(far, -1)
    return call(
        merge_kernel,
        jax.ShapeDtypeStruct((width, rows), bf16),
        [near, *back],
        [pltpu.VMEM((heads, HEAD_DIM + TAIL, count), bf16)],
        1 << 28,
    ).T


def per_device(query_rows, key_rows, value_rows):
    rows, width = query_rows.shape
    shards = lax.axis_size("seq")
    if rows == SEG_A and rows * shards == SEG_B and width == shards * HEAD_DIM and shards == STRIDES:
        return whole_slide(query_rows, key_rows, value_rows)
    return any_length(query_rows, key_rows, value_rows)


def solution(mesh):
    return jax.shard_map(
        per_device,
        mesh=mesh,
        in_specs=(
            P(("slides", "seq"), "head"),
            P(("slides", "seq"), "head"),
            P(("slides", "seq"), "head"),
        ),
        out_specs=P(("slides", "seq"), "head"),
        check_vma=False,
    )
```

```python
import functools
import math

import jax
import jax.numpy as jnp
import numpy as np
from jax import lax
from jax.experimental import pallas as pl
from jax.experimental.pallas import tpu as pltpu
from jax.sharding import PartitionSpec as P

HEAD_DIM = 48
SEG_A = 1024
SEG_B = 4096


def swapped(shard, axis, stride):
    return lax.ppermute(shard, axis, [(i, i ^ 1 << stride) for i in range(lax.axis_size(axis))])


def attend(query_flat, key_flat, value_flat, score_scale):
    local_heads = query_flat.shape[1] // HEAD_DIM
    query_block = query_flat.reshape(query_flat.shape[0], local_heads, HEAD_DIM)
    key_block = key_flat.reshape(key_flat.shape[0], local_heads, HEAD_DIM)
    value_block = value_flat.reshape(value_flat.shape[0], local_heads, HEAD_DIM)
    scores = (
        jnp.einsum("qad,kad->qak", query_block, key_block, preferred_element_type=jnp.float32)
        * score_scale
    )
    row_max = jnp.max(scores, axis=-1)
    exp_scores = jnp.exp(scores - row_max[:, :, None])
    row_total = jnp.sum(exp_scores, axis=-1)
    weighted = jnp.einsum(
        "qak,kad->qad",
        exp_scores.astype(jnp.bfloat16),
        value_block,
        preferred_element_type=jnp.float32,
    )
    level_out = weighted / row_total[:, :, None]
    return (
        level_out.reshape(query_flat.shape[0], local_heads * HEAD_DIM),
        row_max + jnp.log(row_total),
    )


def attend_rows(query_flat, key_flat, value_flat, score_scale):
    count, feature_width = query_flat.shape
    local_heads = feature_width // HEAD_DIM
    keys = key_flat.shape[0]
    rows = math.gcd(count, max(1, 1048576 // (local_heads * keys)))

    def one_piece(query_piece):
        return attend(query_piece, key_flat, value_flat, score_scale)

    outs, lses = lax.map(one_piece, query_flat.reshape(count // rows, rows, feature_width))
    return (outs.reshape(count, feature_width), lses.reshape(count, local_heads))


def local_segments(query_flat, key_flat, value_flat, seg_rows, score_scale):
    count, feature_width = query_flat.shape
    local_heads = feature_width // HEAD_DIM
    shape = (count // seg_rows, seg_rows, feature_width)

    def one_segment(parts):
        return attend_rows(parts[0], parts[1], parts[2], score_scale)

    outs, lses = lax.map(
        one_segment, (query_flat.reshape(shape), key_flat.reshape(shape), value_flat.reshape(shape))
    )
    return (outs.reshape(count, feature_width), lses.reshape(count, local_heads))


def pick_rows(block, stride):
    row_count, feature_width = block.shape
    local_heads = feature_width // HEAD_DIM
    grid = block.reshape(row_count // stride, stride * feature_width)
    columns = []
    for head in range(local_heads):
        begin = head % stride * feature_width + head * HEAD_DIM
        columns.append(grid[:, begin : begin + HEAD_DIM])
    return jnp.concatenate(columns, axis=1)


def spread_rows(level_out, level_lse, stride):
    used_count, feature_width = level_out.shape
    local_heads = feature_width // HEAD_DIM
    head_of_column = np.arange(feature_width) // HEAD_DIM
    out_phases = []
    lse_phases = []
    for phase in range(stride):
        column_mask = jnp.asarray((head_of_column % stride == phase).astype(np.float32))
        head_mask = jnp.asarray(np.arange(local_heads) % stride == phase)
        out_phases.append(level_out * column_mask[None, :])
        lse_phases.append(jnp.where(head_mask[None, :], level_lse, -jnp.inf))
    full_out = jnp.stack(out_phases, axis=1).reshape(used_count * stride, feature_width)
    full_lse = jnp.stack(lse_phases, axis=1).reshape(used_count * stride, local_heads)
    return (full_out, full_lse)


def fold_block(fold_state, queries, keys, values, valid, score_scale):
    running_max, running_total, running_acc = fold_state
    local_heads = queries.shape[1] // HEAD_DIM
    query_block = queries.reshape(queries.shape[0], local_heads, HEAD_DIM)
    key_block = keys.reshape(keys.shape[0], local_heads, HEAD_DIM)
    value_block = values.reshape(values.shape[0], local_heads, HEAD_DIM)
    scores = (
        jnp.einsum("qad,kad->qak", query_block, key_block, preferred_element_type=jnp.float32)
        * score_scale
    )
    scores = jnp.where(valid[None, None, :], scores, -jnp.inf)
    new_max = jnp.maximum(running_max, jnp.max(scores, axis=-1))
    safe_max = jnp.where(new_max == -jnp.inf, 0.0, new_max)
    rescale = jnp.exp(running_max - safe_max)
    exp_scores = jnp.exp(scores - safe_max[:, :, None])
    new_total = running_total * rescale + jnp.sum(exp_scores, axis=-1)
    weighted = jnp.einsum(
        "qak,kad->qad",
        exp_scores.astype(jnp.bfloat16),
        value_block,
        preferred_element_type=jnp.float32,
    )
    new_acc = running_acc * rescale[:, :, None] + weighted
    return (new_max, new_total, new_acc)


def any_length(query_rows, key_rows, value_rows):
    row_count = query_rows.shape[0]
    feature_width = query_rows.shape[1]
    local_heads = feature_width // HEAD_DIM
    shards = lax.axis_size("seq")
    score_scale = HEAD_DIM ** (-0.5)
    first_out, first_lse = local_segments(query_rows, key_rows, value_rows, SEG_A, score_scale)
    used_two = row_count // 2
    seg_two = SEG_B // 2
    query_two = pick_rows(query_rows, 2)
    key_two = pick_rows(key_rows, 2)
    value_two = pick_rows(value_rows, 2)
    stacked = jnp.stack([key_two, value_two])
    for bit_index in range((seg_two // used_two).bit_length() - 1):
        partner = swapped(stacked, "seq", bit_index)
        stacked = jnp.concatenate([stacked, partner], axis=1)
    second_out, second_lse = attend_rows(query_two, stacked[0], stacked[1], score_scale)
    span_tokens = row_count * shards
    group_span = span_tokens // row_count
    used_three = row_count // 4
    wide_queries = pick_rows(query_rows, 4)
    wide_keys = pick_rows(key_rows, 4)
    wide_values = pick_rows(value_rows, 4)
    my_group = lax.axis_index("seq") // group_span
    key_limit = max(1, 1048576 // (local_heads * used_three))
    initial = (
        jnp.full((used_three, local_heads), -jnp.inf, jnp.float32),
        jnp.zeros((used_three, local_heads), jnp.float32),
        jnp.zeros((used_three, local_heads, HEAD_DIM), jnp.float32),
    )
    pieces = (
        lax.all_gather(wide_keys, "seq", axis=0, tiled=True),
        lax.all_gather(wide_values, "seq", axis=0, tiled=True),
    )
    piece_rows = pieces[0].shape[0]
    block = math.gcd(piece_rows, key_limit)
    key_blocks = pieces[0].reshape(piece_rows // block, block, feature_width)
    value_blocks = pieces[1].reshape(piece_rows // block, block, feature_width)
    block_starts = jnp.arange(piece_rows // block, dtype=jnp.int32) * block

    def fold_step(inner_state, items):
        owners = (items[2] + jnp.arange(block, dtype=jnp.int32)) // used_three
        valid = owners // group_span == my_group
        return (fold_block(inner_state, wide_queries, items[0], items[1], valid, score_scale), None)

    final_state, unused = lax.scan(fold_step, initial, (key_blocks, value_blocks, block_starts))
    final_max, final_total, final_acc = final_state
    third_out = (final_acc / final_total[:, :, None]).reshape(used_three, feature_width)
    third_lse = final_max + jnp.log(final_total)
    second_full, second_lse_full = spread_rows(second_out, second_lse, 2)
    third_full, third_lse_full = spread_rows(third_out, third_lse, 4)
    peak = jnp.maximum(jnp.maximum(first_lse, second_lse_full), third_lse_full)
    weight_one = jnp.exp(first_lse - peak)
    weight_two = jnp.exp(second_lse_full - peak)
    weight_three = jnp.exp(third_lse_full - peak)
    denominator = jnp.repeat(weight_one + weight_two + weight_three, HEAD_DIM, axis=1)
    numerator = jnp.repeat(weight_one, HEAD_DIM, axis=1) * first_out
    numerator = numerator + jnp.repeat(weight_two, HEAD_DIM, axis=1) * second_full
    numerator = numerator + jnp.repeat(weight_three, HEAD_DIM, axis=1) * third_full
    return (numerator / denominator).astype(jnp.bfloat16)


STRIDES = 4
LANES = 128
SPAN = STRIDES * LANES
NEAR_KEYS = 256
TAIL = 8
LOG2E = 1.4426950408889634
FACTOR = HEAD_DIM ** (-0.5) * LOG2E
LEAST_TOTAL = 2.0 ** -60
MOST_TOTAL = 2.0 ** 100
VMEM_BYTES = 16 * 1024 * 1024


def dot_nn(left, right):
    return lax.dot_general(left, right, (((1,), (0,)), ((), ())), preferred_element_type=jnp.float32)


def dot_nt(left, right):
    return lax.dot_general(left, right, (((1,), (1,)), ((), ())), preferred_element_type=jnp.float32)


def one_hot(shape, which):
    rows = lax.broadcasted_iota(jnp.int32, shape, 0)
    columns = lax.broadcasted_iota(jnp.int32, shape, 1)
    return jnp.where(which(rows, columns), 1.0, 0.0).astype(jnp.bfloat16)


def call(kernel, outs, args, scratch, flops, space=pltpu.VMEM):
    return pl.pallas_call(
        kernel,
        out_shape=outs,
        in_specs=[pl.BlockSpec(memory_space=space)] * len(args),
        out_specs=jax.tree.map(lambda out: pl.BlockSpec(memory_space=pltpu.VMEM), outs),
        scratch_shapes=scratch,
        compiler_params=pltpu.CompilerParams(vmem_limit_bytes=VMEM_BYTES),
        cost_estimate=pl.CostEstimate(flops=flops, bytes_accessed=2 << 20, transcendentals=0),
    )(*args)


def pack_kernel(q_hbm, k_hbm, v_hbm, q_ref, k_ref, v_ref, m0, m1, m2, m3, by_head, arrivals):
    width, rows = q_ref.shape
    copies = [
        pltpu.make_async_copy(source, target, arrivals.at[at])
        for at, (source, target) in enumerate(((q_hbm, q_ref), (k_hbm, k_ref), (v_hbm, v_ref)))
    ]
    for copy in copies:
        copy.start()
    for copy in copies:
        copy.wait()
    heads = width // HEAD_DIM
    for parity in range(2):
        pick = one_hot(
            (SPAN, 2 * LANES), lambda row, column: row == column % LANES * STRIDES + column // LANES * 2 + parity
        )
        mine = range(parity, heads, 2)
        for block in range(rows // SPAN):
            pieces = [
                ref[pl.ds(head * HEAD_DIM, HEAD_DIM), pl.ds(block * SPAN, SPAN)]
                for head in mine
                for ref in (q_ref, k_ref, v_ref)
            ]
            picked = dot_nn(jnp.concatenate(pieces, axis=0), pick).astype(jnp.bfloat16)
            for at, head in enumerate(mine):
                features = picked[at * 3 * HEAD_DIM : (at + 1) * 3 * HEAD_DIM]
                for klass in range(2):
                    phase = (head + 2 * klass) % STRIDES // 2
                    by_head[head, :, pl.ds(klass * rows // STRIDES + block * LANES, LANES)] = features[
                        :, phase * LANES : (phase + 1) * LANES
                    ]
    me = lax.axis_index("seq")
    for shift, message in enumerate((m0, m1, m2, m3)):
        message[...] = by_head[jnp.bitwise_xor(me, shift)]


def with_ones(block):
    count = block.shape[1]
    extra = one_hot((2 * TAIL, count), lambda row, column: row == 0)
    return jnp.concatenate([block, extra], axis=0)


def upright(block):
    count = block.shape[1]
    size = min(count, 2 * LANES)
    eye = one_hot((size, size), lambda row, column: row == column)
    pieces = [dot_nt(eye, block[:, at : at + size]) for at in range(0, count, size)]
    return jnp.concatenate(pieces, axis=0).astype(jnp.bfloat16)


def plain(keys, queries, values):
    return dot_nn(values, jnp.exp2(dot_nn(keys, queries) * FACTOR).astype(jnp.bfloat16))


def shifted(keys, queries, values):
    scores = dot_nn(keys, queries)
    top = jnp.max(scores, axis=0, keepdims=True) * FACTOR
    return dot_nn(values, jnp.exp2(scores * FACTOR - top).astype(jnp.bfloat16)), top


def in_range(totals):
    low = functools.reduce(jnp.minimum, totals)
    high = functools.reduce(jnp.maximum, totals)
    return jnp.logical_and(jnp.min(low) >= LEAST_TOTAL, jnp.max(high) <= MOST_TOTAL)


def near_kernel(qt_ref, kt_ref, vt_ref, out_ref, keys_ref):
    width, rows = qt_ref.shape
    heads = width // HEAD_DIM
    keys = upright(kt_ref[...])
    for head in range(heads):
        keys_ref[head] = keys[:, head * HEAD_DIM : (head + 1) * HEAD_DIM]
    blocks = [(head, start) for head in range(heads) for start in range(0, rows, SPAN)]
    pieces = range(0, rows, NEAR_KEYS)

    def scores_of(block, piece):
        head, start = block
        queries = qt_ref[pl.ds(head * HEAD_DIM, HEAD_DIM), pl.ds(start, SPAN)]
        return dot_nn(keys_ref[head, pl.ds(piece, NEAR_KEYS), :], queries)

    def folded(values, join, held):
        parts = [values[at : at + 8] for at in range(0, NEAR_KEYS, 8)]
        return functools.reduce(join, parts if held is None else [held, *parts])

    now, peaks = [], None
    for piece in pieces:
        now.append(scores_of(blocks[0], piece))
        peaks = folded(now[-1], jnp.maximum, peaks)
    for at, (head, start) in enumerate(blocks):
        top = jnp.max(peaks, axis=0, keepdims=True) * FACTOR
        later, peaks, result, totals = [], None, None, None
        for piece, scores in zip(pieces, now):
            if at + 1 < len(blocks):
                later.append(scores_of(blocks[at + 1], piece))
                peaks = folded(later[-1], jnp.maximum, peaks)
            probs = jnp.exp2(scores * FACTOR - top)
            totals = folded(probs, jnp.add, totals)
            values = vt_ref[pl.ds(head * HEAD_DIM, HEAD_DIM), pl.ds(piece, NEAR_KEYS)]
            term = dot_nn(values, probs.astype(jnp.bfloat16))
            result = term if result is None else result + term
        lanes = pl.ds(start, SPAN)
        out_ref[head, pl.ds(0, HEAD_DIM), lanes] = result
        out_ref[head, pl.ds(HEAD_DIM, 1), lanes] = jnp.sum(totals, axis=0, keepdims=True)
        out_ref[head, pl.ds(HEAD_DIM + 1, 1), lanes] = top
        now = later


def finished(result, top):
    total = result[HEAD_DIM : HEAD_DIM + 1]
    lse = jnp.log2(total) if top is None else top + jnp.log2(total)
    high = lse.astype(jnp.bfloat16).astype(jnp.float32)
    middle = (lse - high).astype(jnp.bfloat16).astype(jnp.float32)
    low = lse - high - middle
    row = lax.broadcasted_iota(jnp.int32, (TAIL, total.shape[1]), 0)
    parts = jnp.where(row == 0, high, jnp.where(row == 1, middle, jnp.where(row == 2, low, 0.0)))
    return jnp.concatenate([result[:HEAD_DIM] / total, parts], axis=0).astype(jnp.bfloat16)


def far_kernel(m0, m1, m2, m3, o0, o1, keys_ref, queries_ref, values_ref):
    count = m0.shape[1]
    half = count // 2
    sources, outs = (m0, m1, m2, m3), (o0, o1)
    twice = jnp.where(lax.broadcasted_iota(jnp.int32, (1, count), 1) < half, 2.0, 1.0).astype(jnp.bfloat16)
    for at, source in enumerate(sources):
        keys_ref[pl.ds(at * count, count), :] = upright(source[pl.ds(HEAD_DIM, HEAD_DIM), :])
        values = with_ones(source[pl.ds(2 * HEAD_DIM, HEAD_DIM), :])
        values_ref[0, :, pl.ds(at * count, count)] = values * twice
        values_ref[1, :, pl.ds(at * count, count)] = values
    totals = []
    for klass in range(2):
        for at in range(2):
            queries_ref[klass, :, pl.ds(at * half, half)] = sources[at][pl.ds(0, HEAD_DIM), pl.ds(klass * half, half)]
        result = plain(keys_ref[...], queries_ref[klass], values_ref[klass])
        done = finished(result, None)
        totals.append(result[HEAD_DIM : HEAD_DIM + 1])
        for at, out in enumerate(outs):
            out[:, pl.ds(klass * half, half)] = done[:, at * half : (at + 1) * half]

    @pl.when(jnp.logical_not(in_range(totals)))
    def again():
        @pl.loop(0, 2)
        def one_class(klass):
            for at, out in enumerate(outs):
                result, top = shifted(keys_ref[...], queries_ref[klass, :, pl.ds(at * half, half)], values_ref[klass])
                out[:, pl.ds(pl.multiple_of(klass * half, LANES), half)] = finished(result, top)


def merge_kernel(steps, near_ref, *refs):
    results = refs[: len(steps)]
    out_hbm, rows_ref, sent = refs[-3:]
    rows = near_ref.shape[2]
    half = rows // STRIDES
    me = lax.axis_index("seq")
    position = lax.broadcasted_iota(jnp.int32, (1, SPAN), 1)
    copies = []
    for at, (step, result) in enumerate(zip(steps, results)):
        head = jnp.bitwise_xor(me, step)
        place = one_hot(
            (2 * LANES, SPAN),
            lambda row, column: column == row % LANES * STRIDES + (head + row // LANES * 2) % STRIDES,
        )
        used = position % 2 == head % 2
        for block in range(rows // SPAN):
            lanes = pl.ds(block * SPAN, SPAN)
            piece = [result[:, pl.ds(klass * half + block * LANES, LANES)] for klass in range(2)]
            there = dot_nn(jnp.concatenate(piece, axis=1), place)
            near = near_ref[head, pl.ds(0, HEAD_DIM), lanes]
            total = near_ref[head, pl.ds(HEAD_DIM, 1), lanes]
            top = near_ref[head, pl.ds(HEAD_DIM + 1, 1), lanes]
            lse = there[HEAD_DIM : HEAD_DIM + 1] + there[HEAD_DIM + 1 : HEAD_DIM + 2] + there[HEAD_DIM + 2 : HEAD_DIM + 3]
            near_lse = top + jnp.log2(total)
            peak = jnp.where(used, jnp.maximum(near_lse, lse), near_lse)
            weight = jnp.exp2(top - peak)
            far = jnp.where(used, jnp.exp2(lse - peak), 0.0)
            share = 1.0 / (total * weight + far)
            merged = near * (weight * share) + there[:HEAD_DIM] * (far * share)
            rows_ref[at, :, lanes] = merged.astype(jnp.bfloat16)
        features = pl.ds(pl.multiple_of(head * HEAD_DIM, HEAD_DIM), HEAD_DIM)
        copies.append(pltpu.make_async_copy(rows_ref.at[at], out_hbm.at[features], sent.at[at]))
        copies[-1].start()
    for copy in copies:
        copy.wait()


def exchanged(block, step):
    return lax.ppermute(block, "seq", [(i, i ^ step) for i in range(lax.axis_size("seq"))])


def whole_slide(query_rows, key_rows, value_rows):
    rows, width = query_rows.shape
    heads = width // HEAD_DIM
    count = rows // 2
    bf16, f32 = jnp.bfloat16, jnp.float32
    turned = [pltpu.with_memory_space_constraint(block.T, pltpu.HBM) for block in (query_rows, key_rows, value_rows)]
    *here, m0, m1, m2, m3 = call(
        pack_kernel,
        [jax.ShapeDtypeStruct((width, rows), bf16)] * 3 + [jax.ShapeDtypeStruct((3 * HEAD_DIM, count), bf16)] * heads,
        turned,
        [pltpu.VMEM((heads, 3 * HEAD_DIM, count), bf16), pltpu.SemaphoreType.DMA((3,))],
        1 << 28,
        pltpu.HBM,
    )
    arrived = [m0, *(exchanged(message, step) for step, message in ((1, m1), (2, m2), (3, m3)))]
    near = call(
        near_kernel,
        jax.ShapeDtypeStruct((heads, HEAD_DIM + TAIL, rows), f32),
        here,
        [pltpu.VMEM((heads, rows, HEAD_DIM), bf16)],
        4 * heads * rows * rows * 256,
    )
    def far(messages):
        return call(
            far_kernel,
            [jax.ShapeDtypeStruct((HEAD_DIM + TAIL, count), bf16)] * 2,
            messages,
            [
                pltpu.VMEM((heads * count, HEAD_DIM), bf16),
                pltpu.VMEM((2, HEAD_DIM, count), bf16),
                pltpu.VMEM((2, HEAD_DIM + 2 * TAIL, heads * count), bf16),
            ],
            2 * heads * rows * rows * 256,
        )

    def merged(steps, results, begun):
        vmem, hbm = pl.BlockSpec(memory_space=pltpu.VMEM), pl.BlockSpec(memory_space=pl.ANY)
        args = (near, *results, *begun)
        return pl.pallas_call(
            functools.partial(merge_kernel, steps),
            out_shape=jax.ShapeDtypeStruct((width, rows), bf16),
            in_specs=[vmem] * (1 + len(results)) + [hbm] * len(begun),
            out_specs=hbm,
            scratch_shapes=[pltpu.VMEM((len(steps), HEAD_DIM, rows), bf16), pltpu.SemaphoreType.DMA((len(steps),))],
            input_output_aliases={len(args) - 1: 0} if begun else {},
            compiler_params=pltpu.CompilerParams(vmem_limit_bytes=VMEM_BYTES),
            cost_estimate=pl.CostEstimate(flops=len(steps) << 29, bytes_accessed=len(steps) << 20, transcendentals=0),
        )(*args)

    near, m0, m1, m2, m3 = lax.optimization_barrier((near, *arrived))
    f2, f3 = far((m2, m3, m0, m1))
    f2, f3, m0, m1, m2, m3 = lax.optimization_barrier((f2, f3, m0, m1, m2, m3))
    g2, g3 = exchanged(f2, 2), exchanged(f3, 3)
    g0, f1 = far((m0, m1, m2, m3))
    g1 = exchanged(f1, 1)
    own = merged((0,), (g0,), ())
    most = merged((2, 3), (g2, g3), (own,))
    return merged((1,), (g1,), (most,)).T


def per_device(query_rows, key_rows, value_rows):
    rows, width = query_rows.shape
    shards = lax.axis_size("seq")
    if rows == SEG_A and rows * shards == SEG_B and width == shards * HEAD_DIM and shards == STRIDES:
        return whole_slide(query_rows, key_rows, value_rows)
    return any_length(query_rows, key_rows, value_rows)


def solution(mesh):
    return jax.shard_map(
        per_device,
        mesh=mesh,
        in_specs=(
            P(("slides", "seq"), "head"),
            P(("slides", "seq"), "head"),
            P(("slides", "seq"), "head"),
        ),
        out_specs=P(("slides", "seq"), "head"),
        check_vma=False,
    )
```

```python
import functools
import math

import jax
import jax.numpy as jnp
import numpy as np
from jax import lax
from jax.experimental import pallas as pl
from jax.experimental.pallas import tpu as pltpu
from jax.sharding import PartitionSpec as P

HEAD_DIM = 48
SEG_A = 1024
SEG_B = 4096


def swapped(shard, axis, stride):
    return lax.ppermute(shard, axis, [(i, i ^ 1 << stride) for i in range(lax.axis_size(axis))])


def attend(query_flat, key_flat, value_flat, score_scale):
    local_heads = query_flat.shape[1] // HEAD_DIM
    query_block = query_flat.reshape(query_flat.shape[0], local_heads, HEAD_DIM)
    key_block = key_flat.reshape(key_flat.shape[0], local_heads, HEAD_DIM)
    value_block = value_flat.reshape(value_flat.shape[0], local_heads, HEAD_DIM)
    scores = (
        jnp.einsum("qad,kad->qak", query_block, key_block, preferred_element_type=jnp.float32)
        * score_scale
    )
    row_max = jnp.max(scores, axis=-1)
    exp_scores = jnp.exp(scores - row_max[:, :, None])
    row_total = jnp.sum(exp_scores, axis=-1)
    weighted = jnp.einsum(
        "qak,kad->qad",
        exp_scores.astype(jnp.bfloat16),
        value_block,
        preferred_element_type=jnp.float32,
    )
    level_out = weighted / row_total[:, :, None]
    return (
        level_out.reshape(query_flat.shape[0], local_heads * HEAD_DIM),
        row_max + jnp.log(row_total),
    )


def attend_rows(query_flat, key_flat, value_flat, score_scale):
    count, feature_width = query_flat.shape
    local_heads = feature_width // HEAD_DIM
    keys = key_flat.shape[0]
    rows = math.gcd(count, max(1, 1048576 // (local_heads * keys)))

    def one_piece(query_piece):
        return attend(query_piece, key_flat, value_flat, score_scale)

    outs, lses = lax.map(one_piece, query_flat.reshape(count // rows, rows, feature_width))
    return (outs.reshape(count, feature_width), lses.reshape(count, local_heads))


def local_segments(query_flat, key_flat, value_flat, seg_rows, score_scale):
    count, feature_width = query_flat.shape
    local_heads = feature_width // HEAD_DIM
    shape = (count // seg_rows, seg_rows, feature_width)

    def one_segment(parts):
        return attend_rows(parts[0], parts[1], parts[2], score_scale)

    outs, lses = lax.map(
        one_segment, (query_flat.reshape(shape), key_flat.reshape(shape), value_flat.reshape(shape))
    )
    return (outs.reshape(count, feature_width), lses.reshape(count, local_heads))


def pick_rows(block, stride):
    row_count, feature_width = block.shape
    local_heads = feature_width // HEAD_DIM
    grid = block.reshape(row_count // stride, stride * feature_width)
    columns = []
    for head in range(local_heads):
        begin = head % stride * feature_width + head * HEAD_DIM
        columns.append(grid[:, begin : begin + HEAD_DIM])
    return jnp.concatenate(columns, axis=1)


def spread_rows(level_out, level_lse, stride):
    used_count, feature_width = level_out.shape
    local_heads = feature_width // HEAD_DIM
    head_of_column = np.arange(feature_width) // HEAD_DIM
    out_phases = []
    lse_phases = []
    for phase in range(stride):
        column_mask = jnp.asarray((head_of_column % stride == phase).astype(np.float32))
        head_mask = jnp.asarray(np.arange(local_heads) % stride == phase)
        out_phases.append(level_out * column_mask[None, :])
        lse_phases.append(jnp.where(head_mask[None, :], level_lse, -jnp.inf))
    full_out = jnp.stack(out_phases, axis=1).reshape(used_count * stride, feature_width)
    full_lse = jnp.stack(lse_phases, axis=1).reshape(used_count * stride, local_heads)
    return (full_out, full_lse)


def fold_block(fold_state, queries, keys, values, valid, score_scale):
    running_max, running_total, running_acc = fold_state
    local_heads = queries.shape[1] // HEAD_DIM
    query_block = queries.reshape(queries.shape[0], local_heads, HEAD_DIM)
    key_block = keys.reshape(keys.shape[0], local_heads, HEAD_DIM)
    value_block = values.reshape(values.shape[0], local_heads, HEAD_DIM)
    scores = (
        jnp.einsum("qad,kad->qak", query_block, key_block, preferred_element_type=jnp.float32)
        * score_scale
    )
    scores = jnp.where(valid[None, None, :], scores, -jnp.inf)
    new_max = jnp.maximum(running_max, jnp.max(scores, axis=-1))
    safe_max = jnp.where(new_max == -jnp.inf, 0.0, new_max)
    rescale = jnp.exp(running_max - safe_max)
    exp_scores = jnp.exp(scores - safe_max[:, :, None])
    new_total = running_total * rescale + jnp.sum(exp_scores, axis=-1)
    weighted = jnp.einsum(
        "qak,kad->qad",
        exp_scores.astype(jnp.bfloat16),
        value_block,
        preferred_element_type=jnp.float32,
    )
    new_acc = running_acc * rescale[:, :, None] + weighted
    return (new_max, new_total, new_acc)


def any_length(query_rows, key_rows, value_rows):
    row_count = query_rows.shape[0]
    feature_width = query_rows.shape[1]
    local_heads = feature_width // HEAD_DIM
    shards = lax.axis_size("seq")
    score_scale = HEAD_DIM ** (-0.5)
    first_out, first_lse = local_segments(query_rows, key_rows, value_rows, SEG_A, score_scale)
    used_two = row_count // 2
    seg_two = SEG_B // 2
    query_two = pick_rows(query_rows, 2)
    key_two = pick_rows(key_rows, 2)
    value_two = pick_rows(value_rows, 2)
    stacked = jnp.stack([key_two, value_two])
    for bit_index in range((seg_two // used_two).bit_length() - 1):
        partner = swapped(stacked, "seq", bit_index)
        stacked = jnp.concatenate([stacked, partner], axis=1)
    second_out, second_lse = attend_rows(query_two, stacked[0], stacked[1], score_scale)
    span_tokens = row_count * shards
    group_span = span_tokens // row_count
    used_three = row_count // 4
    wide_queries = pick_rows(query_rows, 4)
    wide_keys = pick_rows(key_rows, 4)
    wide_values = pick_rows(value_rows, 4)
    my_group = lax.axis_index("seq") // group_span
    key_limit = max(1, 1048576 // (local_heads * used_three))
    initial = (
        jnp.full((used_three, local_heads), -jnp.inf, jnp.float32),
        jnp.zeros((used_three, local_heads), jnp.float32),
        jnp.zeros((used_three, local_heads, HEAD_DIM), jnp.float32),
    )
    pieces = (
        lax.all_gather(wide_keys, "seq", axis=0, tiled=True),
        lax.all_gather(wide_values, "seq", axis=0, tiled=True),
    )
    piece_rows = pieces[0].shape[0]
    block = math.gcd(piece_rows, key_limit)
    key_blocks = pieces[0].reshape(piece_rows // block, block, feature_width)
    value_blocks = pieces[1].reshape(piece_rows // block, block, feature_width)
    block_starts = jnp.arange(piece_rows // block, dtype=jnp.int32) * block

    def fold_step(inner_state, items):
        owners = (items[2] + jnp.arange(block, dtype=jnp.int32)) // used_three
        valid = owners // group_span == my_group
        return (fold_block(inner_state, wide_queries, items[0], items[1], valid, score_scale), None)

    final_state, unused = lax.scan(fold_step, initial, (key_blocks, value_blocks, block_starts))
    final_max, final_total, final_acc = final_state
    third_out = (final_acc / final_total[:, :, None]).reshape(used_three, feature_width)
    third_lse = final_max + jnp.log(final_total)
    second_full, second_lse_full = spread_rows(second_out, second_lse, 2)
    third_full, third_lse_full = spread_rows(third_out, third_lse, 4)
    peak = jnp.maximum(jnp.maximum(first_lse, second_lse_full), third_lse_full)
    weight_one = jnp.exp(first_lse - peak)
    weight_two = jnp.exp(second_lse_full - peak)
    weight_three = jnp.exp(third_lse_full - peak)
    denominator = jnp.repeat(weight_one + weight_two + weight_three, HEAD_DIM, axis=1)
    numerator = jnp.repeat(weight_one, HEAD_DIM, axis=1) * first_out
    numerator = numerator + jnp.repeat(weight_two, HEAD_DIM, axis=1) * second_full
    numerator = numerator + jnp.repeat(weight_three, HEAD_DIM, axis=1) * third_full
    return (numerator / denominator).astype(jnp.bfloat16)


STRIDES = 4
LANES = 128
SPAN = STRIDES * LANES
NEAR_KEYS = 256
TAIL = 8
LOG2E = 1.4426950408889634
FACTOR = HEAD_DIM ** (-0.5) * LOG2E
LEAST_TOTAL = 2.0 ** -60
MOST_TOTAL = 2.0 ** 100
VMEM_BYTES = 16 * 1024 * 1024


def dot_nn(left, right):
    return lax.dot_general(left, right, (((1,), (0,)), ((), ())), preferred_element_type=jnp.float32)


def dot_nt(left, right):
    return lax.dot_general(left, right, (((1,), (1,)), ((), ())), preferred_element_type=jnp.float32)


def one_hot(shape, which):
    rows = lax.broadcasted_iota(jnp.int32, shape, 0)
    columns = lax.broadcasted_iota(jnp.int32, shape, 1)
    return jnp.where(which(rows, columns), 1.0, 0.0).astype(jnp.bfloat16)


def call(kernel, outs, args, scratch, flops, space=pltpu.VMEM):
    return pl.pallas_call(
        kernel,
        out_shape=outs,
        in_specs=[pl.BlockSpec(memory_space=space)] * len(args),
        out_specs=jax.tree.map(lambda out: pl.BlockSpec(memory_space=pltpu.VMEM), outs),
        scratch_shapes=scratch,
        compiler_params=pltpu.CompilerParams(vmem_limit_bytes=VMEM_BYTES),
        cost_estimate=pl.CostEstimate(flops=flops, bytes_accessed=2 << 20, transcendentals=0),
    )(*args)


def pack_kernel(q_hbm, k_hbm, v_hbm, q_ref, k_ref, v_ref, m2, m3, m1, m0, by_head, arrivals):
    width, rows = q_ref.shape
    copies = [
        pltpu.make_async_copy(source, target, arrivals.at[at])
        for at, (source, target) in enumerate(((q_hbm, q_ref), (k_hbm, k_ref), (v_hbm, v_ref)))
    ]
    for copy in copies:
        copy.start()
    for copy in copies:
        copy.wait()
    heads = width // HEAD_DIM
    for parity in range(2):
        pick = one_hot(
            (SPAN, 2 * LANES), lambda row, column: row == column % LANES * STRIDES + column // LANES * 2 + parity
        )
        mine = range(parity, heads, 2)
        for block in range(rows // SPAN):
            pieces = [
                ref[pl.ds(head * HEAD_DIM, HEAD_DIM), pl.ds(block * SPAN, SPAN)]
                for head in mine
                for ref in (q_ref, k_ref, v_ref)
            ]
            picked = dot_nn(jnp.concatenate(pieces, axis=0), pick).astype(jnp.bfloat16)
            for at, head in enumerate(mine):
                features = picked[at * 3 * HEAD_DIM : (at + 1) * 3 * HEAD_DIM]
                for klass in range(2):
                    phase = (head + 2 * klass) % STRIDES // 2
                    by_head[head, :, pl.ds(klass * rows // STRIDES + block * LANES, LANES)] = features[
                        :, phase * LANES : (phase + 1) * LANES
                    ]
    me = lax.axis_index("seq")
    for shift, message in ((2, m2), (3, m3), (1, m1), (0, m0)):
        message[...] = by_head[jnp.bitwise_xor(me, shift)]


def with_ones(block):
    count = block.shape[1]
    extra = one_hot((2 * TAIL, count), lambda row, column: row == 0)
    return jnp.concatenate([block, extra], axis=0)


def upright(block):
    count = block.shape[1]
    size = min(count, 2 * LANES)
    eye = one_hot((size, size), lambda row, column: row == column)
    pieces = [dot_nt(eye, block[:, at : at + size]) for at in range(0, count, size)]
    return jnp.concatenate(pieces, axis=0).astype(jnp.bfloat16)


def plain(keys, queries, values):
    return dot_nn(values, jnp.exp2(dot_nn(keys, queries) * FACTOR).astype(jnp.bfloat16))


def shifted(keys, queries, values):
    scores = dot_nn(keys, queries)
    top = jnp.max(scores, axis=0, keepdims=True) * FACTOR
    return dot_nn(values, jnp.exp2(scores * FACTOR - top).astype(jnp.bfloat16)), top


def in_range(totals):
    low = functools.reduce(jnp.minimum, totals)
    high = functools.reduce(jnp.maximum, totals)
    return jnp.logical_and(jnp.min(low) >= LEAST_TOTAL, jnp.max(high) <= MOST_TOTAL)


def near_kernel(qt_ref, kt_ref, vt_ref, out_ref, keys_ref):
    width, rows = qt_ref.shape
    heads = width // HEAD_DIM
    keys = upright(kt_ref[...])
    for head in range(heads):
        keys_ref[head] = keys[:, head * HEAD_DIM : (head + 1) * HEAD_DIM]
    blocks = [(head, start) for head in range(heads) for start in range(0, rows, SPAN)]
    pieces = range(0, rows, NEAR_KEYS)

    def scores_of(block, piece):
        head, start = block
        queries = qt_ref[pl.ds(head * HEAD_DIM, HEAD_DIM), pl.ds(start, SPAN)]
        return dot_nn(keys_ref[head, pl.ds(piece, NEAR_KEYS), :], queries)

    def folded(values, join, held):
        parts = [values[at : at + 8] for at in range(0, NEAR_KEYS, 8)]
        return functools.reduce(join, parts if held is None else [held, *parts])

    now, peaks = [], None
    for piece in pieces:
        now.append(scores_of(blocks[0], piece))
        peaks = folded(now[-1], jnp.maximum, peaks)
    for at, (head, start) in enumerate(blocks):
        top = jnp.max(peaks, axis=0, keepdims=True) * FACTOR
        later, peaks, result, totals = [], None, None, None
        for piece, scores in zip(pieces, now):
            if at + 1 < len(blocks):
                later.append(scores_of(blocks[at + 1], piece))
                peaks = folded(later[-1], jnp.maximum, peaks)
            probs = jnp.exp2(scores * FACTOR - top)
            totals = folded(probs, jnp.add, totals)
            values = vt_ref[pl.ds(head * HEAD_DIM, HEAD_DIM), pl.ds(piece, NEAR_KEYS)]
            term = dot_nn(values, probs.astype(jnp.bfloat16))
            result = term if result is None else result + term
        lanes = pl.ds(start, SPAN)
        out_ref[head, pl.ds(0, HEAD_DIM), lanes] = result
        out_ref[head, pl.ds(HEAD_DIM, 1), lanes] = jnp.sum(totals, axis=0, keepdims=True)
        out_ref[head, pl.ds(HEAD_DIM + 1, 1), lanes] = top
        now = later


def finished(result, top):
    total = result[HEAD_DIM : HEAD_DIM + 1]
    lse = jnp.log2(total) if top is None else top + jnp.log2(total)
    high = lse.astype(jnp.bfloat16).astype(jnp.float32)
    middle = (lse - high).astype(jnp.bfloat16).astype(jnp.float32)
    low = lse - high - middle
    row = lax.broadcasted_iota(jnp.int32, (TAIL, total.shape[1]), 0)
    parts = jnp.where(row == 0, high, jnp.where(row == 1, middle, jnp.where(row == 2, low, 0.0)))
    return jnp.concatenate([result[:HEAD_DIM] / total, parts], axis=0).astype(jnp.bfloat16)


def far_kernel(m0, m1, m2, m3, o0, o1, keys_ref, queries_ref, values_ref):
    count = m0.shape[1]
    half = count // 2
    sources, outs = (m0, m1, m2, m3), (o0, o1)
    twice = jnp.where(lax.broadcasted_iota(jnp.int32, (1, count), 1) < half, 2.0, 1.0).astype(jnp.bfloat16)
    for at, source in enumerate(sources):
        keys_ref[pl.ds(at * count, count), :] = upright(source[pl.ds(HEAD_DIM, HEAD_DIM), :])
        values = with_ones(source[pl.ds(2 * HEAD_DIM, HEAD_DIM), :])
        values_ref[0, :, pl.ds(at * count, count)] = values * twice
        values_ref[1, :, pl.ds(at * count, count)] = values
    totals = []
    for klass in range(2):
        for at in range(2):
            queries_ref[klass, :, pl.ds(at * half, half)] = sources[at][pl.ds(0, HEAD_DIM), pl.ds(klass * half, half)]
        result = plain(keys_ref[...], queries_ref[klass], values_ref[klass])
        done = finished(result, None)
        totals.append(result[HEAD_DIM : HEAD_DIM + 1])
        for at, out in enumerate(outs):
            out[:, pl.ds(klass * half, half)] = done[:, at * half : (at + 1) * half]

    @pl.when(jnp.logical_not(in_range(totals)))
    def again():
        @pl.loop(0, 2)
        def one_class(klass):
            for at, out in enumerate(outs):
                result, top = shifted(keys_ref[...], queries_ref[klass, :, pl.ds(at * half, half)], values_ref[klass])
                out[:, pl.ds(pl.multiple_of(klass * half, LANES), half)] = finished(result, top)


def merge_kernel(steps, near_ref, *refs):
    results = refs[: len(steps)]
    out_hbm, rows_ref, sent = refs[-3:]
    rows = near_ref.shape[2]
    half = rows // STRIDES
    me = lax.axis_index("seq")
    position = lax.broadcasted_iota(jnp.int32, (1, SPAN), 1)
    copies = []
    for at, (step, result) in enumerate(zip(steps, results)):
        head = jnp.bitwise_xor(me, step)
        place = one_hot(
            (2 * LANES, SPAN),
            lambda row, column: column == row % LANES * STRIDES + (head + row // LANES * 2) % STRIDES,
        )
        used = position % 2 == head % 2
        for block in range(rows // SPAN):
            lanes = pl.ds(block * SPAN, SPAN)
            piece = [result[:, pl.ds(klass * half + block * LANES, LANES)] for klass in range(2)]
            there = dot_nn(jnp.concatenate(piece, axis=1), place)
            near = near_ref[head, pl.ds(0, HEAD_DIM), lanes]
            total = near_ref[head, pl.ds(HEAD_DIM, 1), lanes]
            top = near_ref[head, pl.ds(HEAD_DIM + 1, 1), lanes]
            lse = there[HEAD_DIM : HEAD_DIM + 1] + there[HEAD_DIM + 1 : HEAD_DIM + 2] + there[HEAD_DIM + 2 : HEAD_DIM + 3]
            near_lse = top + jnp.log2(total)
            peak = jnp.where(used, jnp.maximum(near_lse, lse), near_lse)
            weight = jnp.exp2(top - peak)
            far = jnp.where(used, jnp.exp2(lse - peak), 0.0)
            share = 1.0 / (total * weight + far)
            merged = near * (weight * share) + there[:HEAD_DIM] * (far * share)
            rows_ref[at, :, lanes] = merged.astype(jnp.bfloat16)
        features = pl.ds(pl.multiple_of(head * HEAD_DIM, HEAD_DIM), HEAD_DIM)
        copies.append(pltpu.make_async_copy(rows_ref.at[at], out_hbm.at[features], sent.at[at]))
        copies[-1].start()
    for copy in copies:
        copy.wait()


def exchanged(block, step):
    return lax.ppermute(block, "seq", [(i, i ^ step) for i in range(lax.axis_size("seq"))])


def whole_slide(query_rows, key_rows, value_rows):
    rows, width = query_rows.shape
    heads = width // HEAD_DIM
    count = rows // 2
    bf16, f32 = jnp.bfloat16, jnp.float32
    turned = [pltpu.with_memory_space_constraint(block.T, pltpu.HBM) for block in (query_rows, key_rows, value_rows)]
    *here, m2, m3, m1, m0 = call(
        pack_kernel,
        [jax.ShapeDtypeStruct((width, rows), bf16)] * 3 + [jax.ShapeDtypeStruct((3 * HEAD_DIM, count), bf16)] * heads,
        turned,
        [pltpu.VMEM((heads, 3 * HEAD_DIM, count), bf16), pltpu.SemaphoreType.DMA((3,))],
        1 << 28,
        pltpu.HBM,
    )
    n2, n3 = exchanged(m2, 2), exchanged(m3, 3)
    arrived = (n3, n2, exchanged(m1, 1), m0)
    near = call(
        near_kernel,
        jax.ShapeDtypeStruct((heads, HEAD_DIM + TAIL, rows), f32),
        here,
        [pltpu.VMEM((heads, rows, HEAD_DIM), bf16)],
        4 * heads * rows * rows * 256,
    )
    def far(messages):
        return call(
            far_kernel,
            [jax.ShapeDtypeStruct((HEAD_DIM + TAIL, count), bf16)] * 2,
            messages,
            [
                pltpu.VMEM((heads * count, HEAD_DIM), bf16),
                pltpu.VMEM((2, HEAD_DIM, count), bf16),
                pltpu.VMEM((2, HEAD_DIM + 2 * TAIL, heads * count), bf16),
            ],
            2 * heads * rows * rows * 256,
        )

    def merged(steps, results, begun):
        vmem, hbm = pl.BlockSpec(memory_space=pltpu.VMEM), pl.BlockSpec(memory_space=pl.ANY)
        args = (near, *results, *begun)
        return pl.pallas_call(
            functools.partial(merge_kernel, steps),
            out_shape=jax.ShapeDtypeStruct((width, rows), bf16),
            in_specs=[vmem] * (1 + len(results)) + [hbm] * len(begun),
            out_specs=hbm,
            scratch_shapes=[pltpu.VMEM((len(steps), HEAD_DIM, rows), bf16), pltpu.SemaphoreType.DMA((len(steps),))],
            input_output_aliases={len(args) - 1: 0} if begun else {},
            compiler_params=pltpu.CompilerParams(vmem_limit_bytes=VMEM_BYTES),
            cost_estimate=pl.CostEstimate(flops=len(steps) << 29, bytes_accessed=len(steps) << 20, transcendentals=0),
        )(*args)

    m3, m2, m1, m0, near = lax.optimization_barrier((*arrived, near))
    f2, f3 = far((m2, m3, m0, m1))
    f2, f3, m0, m1, m2, m3 = lax.optimization_barrier((f2, f3, m0, m1, m2, m3))
    g2, g3 = exchanged(f2, 2), exchanged(f3, 3)
    g0, f1 = far((m0, m1, m2, m3))
    g1 = exchanged(f1, 1)
    own = merged((0,), (g0,), ())
    most = merged((2, 3), (g2, g3), (own,))
    return merged((1,), (g1,), (most,)).T


def per_device(query_rows, key_rows, value_rows):
    rows, width = query_rows.shape
    shards = lax.axis_size("seq")
    if rows == SEG_A and rows * shards == SEG_B and width == shards * HEAD_DIM and shards == STRIDES:
        return whole_slide(query_rows, key_rows, value_rows)
    return any_length(query_rows, key_rows, value_rows)


def solution(mesh):
    return jax.shard_map(
        per_device,
        mesh=mesh,
        in_specs=(
            P(("slides", "seq"), "head"),
            P(("slides", "seq"), "head"),
            P(("slides", "seq"), "head"),
        ),
        out_specs=P(("slides", "seq"), "head"),
        check_vma=False,
    )
```

```python
import functools
import math

import jax
import jax.numpy as jnp
import numpy as np
from jax import lax
from jax.experimental import pallas as pl
from jax.experimental.pallas import tpu as pltpu
from jax.sharding import PartitionSpec as P

HEAD_DIM = 48
SEG_A = 1024
SEG_B = 4096


def swapped(shard, axis, stride):
    return lax.ppermute(shard, axis, [(i, i ^ 1 << stride) for i in range(lax.axis_size(axis))])


def attend(query_flat, key_flat, value_flat, score_scale):
    local_heads = query_flat.shape[1] // HEAD_DIM
    query_block = query_flat.reshape(query_flat.shape[0], local_heads, HEAD_DIM)
    key_block = key_flat.reshape(key_flat.shape[0], local_heads, HEAD_DIM)
    value_block = value_flat.reshape(value_flat.shape[0], local_heads, HEAD_DIM)
    scores = (
        jnp.einsum("qad,kad->qak", query_block, key_block, preferred_element_type=jnp.float32)
        * score_scale
    )
    row_max = jnp.max(scores, axis=-1)
    exp_scores = jnp.exp(scores - row_max[:, :, None])
    row_total = jnp.sum(exp_scores, axis=-1)
    weighted = jnp.einsum(
        "qak,kad->qad",
        exp_scores.astype(jnp.bfloat16),
        value_block,
        preferred_element_type=jnp.float32,
    )
    level_out = weighted / row_total[:, :, None]
    return (
        level_out.reshape(query_flat.shape[0], local_heads * HEAD_DIM),
        row_max + jnp.log(row_total),
    )


def attend_rows(query_flat, key_flat, value_flat, score_scale):
    count, feature_width = query_flat.shape
    local_heads = feature_width // HEAD_DIM
    keys = key_flat.shape[0]
    rows = math.gcd(count, max(1, 1048576 // (local_heads * keys)))

    def one_piece(query_piece):
        return attend(query_piece, key_flat, value_flat, score_scale)

    outs, lses = lax.map(one_piece, query_flat.reshape(count // rows, rows, feature_width))
    return (outs.reshape(count, feature_width), lses.reshape(count, local_heads))


def local_segments(query_flat, key_flat, value_flat, seg_rows, score_scale):
    count, feature_width = query_flat.shape
    local_heads = feature_width // HEAD_DIM
    shape = (count // seg_rows, seg_rows, feature_width)

    def one_segment(parts):
        return attend_rows(parts[0], parts[1], parts[2], score_scale)

    outs, lses = lax.map(
        one_segment, (query_flat.reshape(shape), key_flat.reshape(shape), value_flat.reshape(shape))
    )
    return (outs.reshape(count, feature_width), lses.reshape(count, local_heads))


def pick_rows(block, stride):
    row_count, feature_width = block.shape
    local_heads = feature_width // HEAD_DIM
    grid = block.reshape(row_count // stride, stride * feature_width)
    columns = []
    for head in range(local_heads):
        begin = head % stride * feature_width + head * HEAD_DIM
        columns.append(grid[:, begin : begin + HEAD_DIM])
    return jnp.concatenate(columns, axis=1)


def spread_rows(level_out, level_lse, stride):
    used_count, feature_width = level_out.shape
    local_heads = feature_width // HEAD_DIM
    head_of_column = np.arange(feature_width) // HEAD_DIM
    out_phases = []
    lse_phases = []
    for phase in range(stride):
        column_mask = jnp.asarray((head_of_column % stride == phase).astype(np.float32))
        head_mask = jnp.asarray(np.arange(local_heads) % stride == phase)
        out_phases.append(level_out * column_mask[None, :])
        lse_phases.append(jnp.where(head_mask[None, :], level_lse, -jnp.inf))
    full_out = jnp.stack(out_phases, axis=1).reshape(used_count * stride, feature_width)
    full_lse = jnp.stack(lse_phases, axis=1).reshape(used_count * stride, local_heads)
    return (full_out, full_lse)


def fold_block(fold_state, queries, keys, values, valid, score_scale):
    running_max, running_total, running_acc = fold_state
    local_heads = queries.shape[1] // HEAD_DIM
    query_block = queries.reshape(queries.shape[0], local_heads, HEAD_DIM)
    key_block = keys.reshape(keys.shape[0], local_heads, HEAD_DIM)
    value_block = values.reshape(values.shape[0], local_heads, HEAD_DIM)
    scores = (
        jnp.einsum("qad,kad->qak", query_block, key_block, preferred_element_type=jnp.float32)
        * score_scale
    )
    scores = jnp.where(valid[None, None, :], scores, -jnp.inf)
    new_max = jnp.maximum(running_max, jnp.max(scores, axis=-1))
    safe_max = jnp.where(new_max == -jnp.inf, 0.0, new_max)
    rescale = jnp.exp(running_max - safe_max)
    exp_scores = jnp.exp(scores - safe_max[:, :, None])
    new_total = running_total * rescale + jnp.sum(exp_scores, axis=-1)
    weighted = jnp.einsum(
        "qak,kad->qad",
        exp_scores.astype(jnp.bfloat16),
        value_block,
        preferred_element_type=jnp.float32,
    )
    new_acc = running_acc * rescale[:, :, None] + weighted
    return (new_max, new_total, new_acc)


def any_length(query_rows, key_rows, value_rows):
    row_count = query_rows.shape[0]
    feature_width = query_rows.shape[1]
    local_heads = feature_width // HEAD_DIM
    shards = lax.axis_size("seq")
    score_scale = HEAD_DIM ** (-0.5)
    first_out, first_lse = local_segments(query_rows, key_rows, value_rows, SEG_A, score_scale)
    used_two = row_count // 2
    seg_two = SEG_B // 2
    query_two = pick_rows(query_rows, 2)
    key_two = pick_rows(key_rows, 2)
    value_two = pick_rows(value_rows, 2)
    stacked = jnp.stack([key_two, value_two])
    for bit_index in range((seg_two // used_two).bit_length() - 1):
        partner = swapped(stacked, "seq", bit_index)
        stacked = jnp.concatenate([stacked, partner], axis=1)
    second_out, second_lse = attend_rows(query_two, stacked[0], stacked[1], score_scale)
    span_tokens = row_count * shards
    group_span = span_tokens // row_count
    used_three = row_count // 4
    wide_queries = pick_rows(query_rows, 4)
    wide_keys = pick_rows(key_rows, 4)
    wide_values = pick_rows(value_rows, 4)
    my_group = lax.axis_index("seq") // group_span
    key_limit = max(1, 1048576 // (local_heads * used_three))
    initial = (
        jnp.full((used_three, local_heads), -jnp.inf, jnp.float32),
        jnp.zeros((used_three, local_heads), jnp.float32),
        jnp.zeros((used_three, local_heads, HEAD_DIM), jnp.float32),
    )
    pieces = (
        lax.all_gather(wide_keys, "seq", axis=0, tiled=True),
        lax.all_gather(wide_values, "seq", axis=0, tiled=True),
    )
    piece_rows = pieces[0].shape[0]
    block = math.gcd(piece_rows, key_limit)
    key_blocks = pieces[0].reshape(piece_rows // block, block, feature_width)
    value_blocks = pieces[1].reshape(piece_rows // block, block, feature_width)
    block_starts = jnp.arange(piece_rows // block, dtype=jnp.int32) * block

    def fold_step(inner_state, items):
        owners = (items[2] + jnp.arange(block, dtype=jnp.int32)) // used_three
        valid = owners // group_span == my_group
        return (fold_block(inner_state, wide_queries, items[0], items[1], valid, score_scale), None)

    final_state, unused = lax.scan(fold_step, initial, (key_blocks, value_blocks, block_starts))
    final_max, final_total, final_acc = final_state
    third_out = (final_acc / final_total[:, :, None]).reshape(used_three, feature_width)
    third_lse = final_max + jnp.log(final_total)
    second_full, second_lse_full = spread_rows(second_out, second_lse, 2)
    third_full, third_lse_full = spread_rows(third_out, third_lse, 4)
    peak = jnp.maximum(jnp.maximum(first_lse, second_lse_full), third_lse_full)
    weight_one = jnp.exp(first_lse - peak)
    weight_two = jnp.exp(second_lse_full - peak)
    weight_three = jnp.exp(third_lse_full - peak)
    denominator = jnp.repeat(weight_one + weight_two + weight_three, HEAD_DIM, axis=1)
    numerator = jnp.repeat(weight_one, HEAD_DIM, axis=1) * first_out
    numerator = numerator + jnp.repeat(weight_two, HEAD_DIM, axis=1) * second_full
    numerator = numerator + jnp.repeat(weight_three, HEAD_DIM, axis=1) * third_full
    return (numerator / denominator).astype(jnp.bfloat16)


STRIDES = 4
LANES = 128
SPAN = STRIDES * LANES
NEAR_KEYS = 256
LOW_HEADS = 1
TAIL = 8
LOG2E = 1.4426950408889634
FACTOR = HEAD_DIM ** (-0.5) * LOG2E
LEAST_TOTAL = 2.0 ** -60
MOST_TOTAL = 2.0 ** 100
VMEM_BYTES = 16 * 1024 * 1024


def dot_nn(left, right):
    return lax.dot_general(left, right, (((1,), (0,)), ((), ())), preferred_element_type=jnp.float32)


def dot_nt(left, right):
    return lax.dot_general(left, right, (((1,), (1,)), ((), ())), preferred_element_type=jnp.float32)


def one_hot(shape, which):
    rows = lax.broadcasted_iota(jnp.int32, shape, 0)
    columns = lax.broadcasted_iota(jnp.int32, shape, 1)
    return jnp.where(which(rows, columns), 1.0, 0.0).astype(jnp.bfloat16)


def call(kernel, outs, args, scratch, flops, space=pltpu.VMEM):
    return pl.pallas_call(
        kernel,
        out_shape=outs,
        in_specs=[pl.BlockSpec(memory_space=space)] * len(args),
        out_specs=jax.tree.map(lambda out: pl.BlockSpec(memory_space=pltpu.VMEM), outs),
        scratch_shapes=scratch,
        compiler_params=pltpu.CompilerParams(vmem_limit_bytes=VMEM_BYTES),
        cost_estimate=pl.CostEstimate(flops=flops, bytes_accessed=2 << 20, transcendentals=0),
    )(*args)


def pack_kernel(q_hbm, k_hbm, v_hbm, q_ref, k_ref, v_ref, m2, m3, m1, m0, by_head, arrivals):
    width, rows = q_ref.shape
    copies = [
        pltpu.make_async_copy(source, target, arrivals.at[at])
        for at, (source, target) in enumerate(((q_hbm, q_ref), (k_hbm, k_ref), (v_hbm, v_ref)))
    ]
    for copy in copies:
        copy.start()
    for copy in copies:
        copy.wait()
    heads = width // HEAD_DIM
    for parity in range(2):
        pick = one_hot(
            (SPAN, 2 * LANES), lambda row, column: row == column % LANES * STRIDES + column // LANES * 2 + parity
        )
        mine = range(parity, heads, 2)
        for block in range(rows // SPAN):
            pieces = [
                ref[pl.ds(head * HEAD_DIM, HEAD_DIM), pl.ds(block * SPAN, SPAN)]
                for head in mine
                for ref in (q_ref, k_ref, v_ref)
            ]
            picked = dot_nn(jnp.concatenate(pieces, axis=0), pick).astype(jnp.bfloat16)
            for at, head in enumerate(mine):
                features = picked[at * 3 * HEAD_DIM : (at + 1) * 3 * HEAD_DIM]
                for klass in range(2):
                    phase = (head + 2 * klass) % STRIDES // 2
                    by_head[head, :, pl.ds(klass * rows // STRIDES + block * LANES, LANES)] = features[
                        :, phase * LANES : (phase + 1) * LANES
                    ]
    me = lax.axis_index("seq")
    for shift, message in ((2, m2), (3, m3), (1, m1), (0, m0)):
        message[...] = by_head[jnp.bitwise_xor(me, shift)]


def with_ones(block):
    count = block.shape[1]
    extra = one_hot((2 * TAIL, count), lambda row, column: row == 0)
    return jnp.concatenate([block, extra], axis=0)


def upright(block):
    count = block.shape[1]
    size = min(count, 2 * LANES)
    eye = one_hot((size, size), lambda row, column: row == column)
    pieces = [dot_nt(eye, block[:, at : at + size]) for at in range(0, count, size)]
    return jnp.concatenate(pieces, axis=0).astype(jnp.bfloat16)


def plain(keys, queries, values):
    return dot_nn(values, jnp.exp2(dot_nn(keys, queries) * FACTOR).astype(jnp.bfloat16))


def shifted(groups, queries):
    scores = [dot_nn(keys, queries) for keys, _ in groups]
    top = functools.reduce(jnp.maximum, [jnp.max(block, axis=0, keepdims=True) for block in scores]) * FACTOR
    terms = [
        dot_nn(values, jnp.exp2(block * FACTOR - top).astype(jnp.bfloat16)) for block, (_, values) in zip(scores, groups)
    ]
    return functools.reduce(jnp.add, terms), top


def in_range(totals):
    low = functools.reduce(jnp.minimum, totals)
    high = functools.reduce(jnp.maximum, totals)
    return jnp.logical_and(jnp.min(low) >= LEAST_TOTAL, jnp.max(high) <= MOST_TOTAL)


def near_kernel(first, qt_ref, kt_ref, vt_ref, out_ref, keys_ref):
    rows = qt_ref.shape[1]
    heads = out_ref.shape[0]
    for head in range(heads):
        keys_ref[head] = upright(kt_ref[pl.ds((first + head) * HEAD_DIM, HEAD_DIM), :])
    blocks = [(head, start) for head in range(heads) for start in range(0, rows, SPAN)]
    pieces = range(0, rows, NEAR_KEYS)

    def scores_of(block, piece):
        head, start = block
        queries = qt_ref[pl.ds((first + head) * HEAD_DIM, HEAD_DIM), pl.ds(start, SPAN)]
        return dot_nn(keys_ref[head, pl.ds(piece, NEAR_KEYS), :], queries)

    def folded(values, join, held):
        parts = [values[at : at + 8] for at in range(0, NEAR_KEYS, 8)]
        return functools.reduce(join, parts if held is None else [held, *parts])

    now, peaks = [], None
    for piece in pieces:
        now.append(scores_of(blocks[0], piece))
        peaks = folded(now[-1], jnp.maximum, peaks)
    for at, (head, start) in enumerate(blocks):
        top = jnp.max(peaks, axis=0, keepdims=True) * FACTOR
        later, peaks, result, totals = [], None, None, None
        for piece, scores in zip(pieces, now):
            if at + 1 < len(blocks):
                later.append(scores_of(blocks[at + 1], piece))
                peaks = folded(later[-1], jnp.maximum, peaks)
            probs = jnp.exp2(scores * FACTOR - top)
            totals = folded(probs, jnp.add, totals)
            values = vt_ref[pl.ds((first + head) * HEAD_DIM, HEAD_DIM), pl.ds(piece, NEAR_KEYS)]
            term = dot_nn(values, probs.astype(jnp.bfloat16))
            result = term if result is None else result + term
        lanes = pl.ds(start, SPAN)
        out_ref[head, pl.ds(0, HEAD_DIM), lanes] = result
        out_ref[head, pl.ds(HEAD_DIM, 1), lanes] = jnp.sum(totals, axis=0, keepdims=True)
        out_ref[head, pl.ds(HEAD_DIM + 1, 1), lanes] = top
        now = later


def finished(result, top):
    total = result[HEAD_DIM : HEAD_DIM + 1]
    lse = jnp.log2(total) if top is None else top + jnp.log2(total)
    high = lse.astype(jnp.bfloat16).astype(jnp.float32)
    middle = (lse - high).astype(jnp.bfloat16).astype(jnp.float32)
    low = lse - high - middle
    row = lax.broadcasted_iota(jnp.int32, (TAIL, total.shape[1]), 0)
    parts = jnp.where(row == 0, high, jnp.where(row == 1, middle, jnp.where(row == 2, low, 0.0)))
    return jnp.concatenate([result[:HEAD_DIM] / total, parts], axis=0).astype(jnp.bfloat16)


def fill(messages, keys_ref, queries_ref, values_ref):
    count = messages[0].shape[1]
    half = count // 2
    twice = jnp.where(lax.broadcasted_iota(jnp.int32, (1, count), 1) < half, 2.0, 1.0).astype(jnp.bfloat16)
    for at, message in enumerate(messages):
        if keys_ref is not None:
            keys_ref[pl.ds(at * count, count), :] = upright(message[pl.ds(HEAD_DIM, HEAD_DIM), :])
        if values_ref is not None:
            values = with_ones(message[pl.ds(2 * HEAD_DIM, HEAD_DIM), :])
            values_ref[0, :, pl.ds(at * count, count)] = values * twice
            values_ref[1, :, pl.ds(at * count, count)] = values
        if queries_ref is not None:
            for klass in range(2):
                queries_ref[klass, :, pl.ds(at * half, half)] = message[pl.ds(0, HEAD_DIM), pl.ds(klass * half, half)]


def early_kernel(m0, m1, keys_ref, part_ref, queries_ref, values_ref):
    fill((m0, m1), keys_ref, queries_ref, values_ref)
    for klass in range(2):
        part_ref[klass] = plain(keys_ref[...], queries_ref[klass], values_ref[klass])


def store(outs, klass, at, block):
    half = block.shape[1]
    outs[at][:, pl.ds(pl.multiple_of(klass * half, LANES), half)] = block


def settle(results, outs, groups, queries_ref):
    half = outs[0].shape[1] // 2
    for klass, result in enumerate(results):
        done = finished(result, None)
        for at in range(2):
            store(outs, klass, at, done[:, at * half : (at + 1) * half])

    @pl.when(jnp.logical_not(in_range([result[HEAD_DIM : HEAD_DIM + 1] for result in results])))
    def again():
        @pl.loop(0, 2)
        def one_class(klass):
            for at in range(2):
                blocks = [(keys[...], values[klass]) for keys, values in groups()]
                store(outs, klass, at, finished(*shifted(blocks, queries_ref[klass, :, pl.ds(at * half, half)])))


def cross_kernel(m2, m3, m0, m1, near_keys, o2, o3, far_keys, queries_ref, near_values, far_values):
    fill((m2, m3), far_keys, queries_ref, far_values)
    fill((m0, m1), None, None, near_values)
    groups = ((near_keys, near_values), (far_keys, far_values))
    results = [
        functools.reduce(jnp.add, [plain(keys[...], queries_ref[klass], values[klass]) for keys, values in groups])
        for klass in range(2)
    ]
    settle(results, (o2, o3), lambda: groups, queries_ref)


def late_kernel(m0, m1, m2, m3, near_keys, far_keys, part_ref, o0, o1, queries_ref, near_values, far_values):
    fill((m0, m1), None, queries_ref, None)
    fill((m2, m3), None, None, far_values)
    results = [part_ref[klass] + plain(far_keys[...], queries_ref[klass], far_values[klass]) for klass in range(2)]

    def groups():
        fill((m0, m1), None, None, near_values)
        return ((near_keys, near_values), (far_keys, far_values))

    settle(results, (o0, o1), groups, queries_ref)


def merge_kernel(steps, low_ref, high_ref, *refs):
    results = refs[: len(steps)]
    out_hbm, rows_ref, sent = refs[-3:]
    each, _, rows = low_ref.shape
    half = rows // STRIDES
    me = lax.axis_index("seq")
    position = lax.broadcasted_iota(jnp.int32, (1, SPAN), 1)
    copies = []
    for at, (step, result) in enumerate(zip(steps, results)):
        head = jnp.bitwise_xor(me, step)
        place = one_hot(
            (2 * LANES, SPAN),
            lambda row, column: column == row % LANES * STRIDES + (head + row // LANES * 2) % STRIDES,
        )
        used = position % 2 == head % 2
        for block in range(rows // SPAN):
            lanes = pl.ds(block * SPAN, SPAN)
            piece = [result[:, pl.ds(klass * half + block * LANES, LANES)] for klass in range(2)]
            there = dot_nn(jnp.concatenate(piece, axis=1), place)
            in_low = low_ref[jnp.minimum(head, each - 1), :, lanes]
            level = jnp.where(head < each, in_low, high_ref[jnp.maximum(head - each, 0), :, lanes])
            near = level[:HEAD_DIM]
            total = level[HEAD_DIM : HEAD_DIM + 1]
            top = level[HEAD_DIM + 1 : HEAD_DIM + 2]
            lse = there[HEAD_DIM : HEAD_DIM + 1] + there[HEAD_DIM + 1 : HEAD_DIM + 2] + there[HEAD_DIM + 2 : HEAD_DIM + 3]
            near_lse = top + jnp.log2(total)
            peak = jnp.where(used, jnp.maximum(near_lse, lse), near_lse)
            weight = jnp.exp2(top - peak)
            far = jnp.where(used, jnp.exp2(lse - peak), 0.0)
            share = 1.0 / (total * weight + far)
            merged = near * (weight * share) + there[:HEAD_DIM] * (far * share)
            rows_ref[at, :, lanes] = merged.astype(jnp.bfloat16)
        features = pl.ds(pl.multiple_of(head * HEAD_DIM, HEAD_DIM), HEAD_DIM)
        copies.append(pltpu.make_async_copy(rows_ref.at[at], out_hbm.at[features], sent.at[at]))
        copies[-1].start()
    for copy in copies:
        copy.wait()


def exchanged(block, step):
    return lax.ppermute(block, "seq", [(i, i ^ step) for i in range(lax.axis_size("seq"))])


def whole_slide(query_rows, key_rows, value_rows):
    rows, width = query_rows.shape
    heads = width // HEAD_DIM
    count = rows // 2
    bf16, f32 = jnp.bfloat16, jnp.float32
    turned = [pltpu.with_memory_space_constraint(block.T, pltpu.HBM) for block in (query_rows, key_rows, value_rows)]
    *here, m2, m3, m1, m0 = call(
        pack_kernel,
        [jax.ShapeDtypeStruct((width, rows), bf16)] * 3 + [jax.ShapeDtypeStruct((3 * HEAD_DIM, count), bf16)] * heads,
        turned,
        [pltpu.VMEM((heads, 3 * HEAD_DIM, count), bf16), pltpu.SemaphoreType.DMA((3,))],
        1 << 28,
        pltpu.HBM,
    )
    n2, n3 = exchanged(m2, 2), exchanged(m3, 3)

    def near(first, some):
        return call(
            functools.partial(near_kernel, first),
            jax.ShapeDtypeStruct((some, HEAD_DIM + TAIL, rows), f32),
            here,
            [pltpu.VMEM((some, rows, HEAD_DIM), bf16)],
            4 * some * rows * rows * 256,
        )

    low = near(0, LOW_HEADS)
    low, m1, *here = lax.optimization_barrier((low, m1, *here))
    n1 = exchanged(m1, 1)
    high = near(LOW_HEADS, heads - LOW_HEADS)
    def merged(steps, results, begun):
        vmem, hbm = pl.BlockSpec(memory_space=pltpu.VMEM), pl.BlockSpec(memory_space=pl.ANY)
        args = (low, high, *results, *begun)
        return pl.pallas_call(
            functools.partial(merge_kernel, steps),
            out_shape=jax.ShapeDtypeStruct((width, rows), bf16),
            in_specs=[vmem] * (2 + len(results)) + [hbm] * len(begun),
            out_specs=hbm,
            scratch_shapes=[pltpu.VMEM((len(steps), HEAD_DIM, rows), bf16), pltpu.SemaphoreType.DMA((len(steps),))],
            input_output_aliases={len(args) - 1: 0} if begun else {},
            compiler_params=pltpu.CompilerParams(vmem_limit_bytes=VMEM_BYTES),
            cost_estimate=pl.CostEstimate(flops=len(steps) << 29, bytes_accessed=len(steps) << 20, transcendentals=0),
        )(*args)

    result = [jax.ShapeDtypeStruct((HEAD_DIM + TAIL, count), bf16)] * 2
    pair_keys = jax.ShapeDtypeStruct((2 * count, HEAD_DIM), bf16)
    queries = pltpu.VMEM((2, HEAD_DIM, count), bf16)
    values = pltpu.VMEM((2, HEAD_DIM + 2 * TAIL, 2 * count), bf16)
    work = 2 * heads * rows * rows * 256
    n1, high = lax.optimization_barrier((n1, high))
    near_keys, part = call(
        early_kernel,
        [pair_keys, jax.ShapeDtypeStruct((2, HEAD_DIM + 2 * TAIL, count), f32)],
        (m0, n1),
        [queries, values],
        work // 2,
    )
    n3, n2, near_keys, part = lax.optimization_barrier((n3, n2, near_keys, part))
    f2, f3, far_keys = call(
        cross_kernel, [*result, pair_keys], (n2, n3, m0, n1, near_keys), [queries, values, values], work
    )
    f2, f3, m0, n1 = lax.optimization_barrier((f2, f3, m0, n1))
    g2, g3 = exchanged(f2, 2), exchanged(f3, 3)
    g0, f1 = call(late_kernel, result, (m0, n1, n2, n3, near_keys, far_keys, part), [queries, values, values], work // 2)
    g1 = exchanged(f1, 1)
    own = merged((0,), (g0,), ())
    most = merged((2, 3), (g2, g3), (own,))
    return merged((1,), (g1,), (most,)).T


def per_device(query_rows, key_rows, value_rows):
    rows, width = query_rows.shape
    shards = lax.axis_size("seq")
    if rows == SEG_A and rows * shards == SEG_B and width == shards * HEAD_DIM and shards == STRIDES:
        return whole_slide(query_rows, key_rows, value_rows)
    return any_length(query_rows, key_rows, value_rows)


def solution(mesh):
    return jax.shard_map(
        per_device,
        mesh=mesh,
        in_specs=(
            P(("slides", "seq"), "head"),
            P(("slides", "seq"), "head"),
            P(("slides", "seq"), "head"),
        ),
        out_specs=P(("slides", "seq"), "head"),
        check_vma=False,
    )
```

```python
import functools
import math

import jax
import jax.numpy as jnp
import numpy as np
from jax import lax
from jax.experimental import pallas as pl
from jax.experimental.pallas import tpu as pltpu
from jax.sharding import PartitionSpec as P

HEAD_DIM = 48
SEG_A = 1024
SEG_B = 4096


def swapped(shard, axis, stride):
    return lax.ppermute(shard, axis, [(i, i ^ 1 << stride) for i in range(lax.axis_size(axis))])


def attend(query_flat, key_flat, value_flat, score_scale):
    local_heads = query_flat.shape[1] // HEAD_DIM
    query_block = query_flat.reshape(query_flat.shape[0], local_heads, HEAD_DIM)
    key_block = key_flat.reshape(key_flat.shape[0], local_heads, HEAD_DIM)
    value_block = value_flat.reshape(value_flat.shape[0], local_heads, HEAD_DIM)
    scores = (
        jnp.einsum("qad,kad->qak", query_block, key_block, preferred_element_type=jnp.float32)
        * score_scale
    )
    row_max = jnp.max(scores, axis=-1)
    exp_scores = jnp.exp(scores - row_max[:, :, None])
    row_total = jnp.sum(exp_scores, axis=-1)
    weighted = jnp.einsum(
        "qak,kad->qad",
        exp_scores.astype(jnp.bfloat16),
        value_block,
        preferred_element_type=jnp.float32,
    )
    level_out = weighted / row_total[:, :, None]
    return (
        level_out.reshape(query_flat.shape[0], local_heads * HEAD_DIM),
        row_max + jnp.log(row_total),
    )


def attend_rows(query_flat, key_flat, value_flat, score_scale):
    count, feature_width = query_flat.shape
    local_heads = feature_width // HEAD_DIM
    keys = key_flat.shape[0]
    rows = math.gcd(count, max(1, 1048576 // (local_heads * keys)))

    def one_piece(query_piece):
        return attend(query_piece, key_flat, value_flat, score_scale)

    outs, lses = lax.map(one_piece, query_flat.reshape(count // rows, rows, feature_width))
    return (outs.reshape(count, feature_width), lses.reshape(count, local_heads))


def local_segments(query_flat, key_flat, value_flat, seg_rows, score_scale):
    count, feature_width = query_flat.shape
    local_heads = feature_width // HEAD_DIM
    shape = (count // seg_rows, seg_rows, feature_width)

    def one_segment(parts):
        return attend_rows(parts[0], parts[1], parts[2], score_scale)

    outs, lses = lax.map(
        one_segment, (query_flat.reshape(shape), key_flat.reshape(shape), value_flat.reshape(shape))
    )
    return (outs.reshape(count, feature_width), lses.reshape(count, local_heads))


def pick_rows(block, stride):
    row_count, feature_width = block.shape
    local_heads = feature_width // HEAD_DIM
    grid = block.reshape(row_count // stride, stride * feature_width)
    columns = []
    for head in range(local_heads):
        begin = head % stride * feature_width + head * HEAD_DIM
        columns.append(grid[:, begin : begin + HEAD_DIM])
    return jnp.concatenate(columns, axis=1)


def spread_rows(level_out, level_lse, stride):
    used_count, feature_width = level_out.shape
    local_heads = feature_width // HEAD_DIM
    head_of_column = np.arange(feature_width) // HEAD_DIM
    out_phases = []
    lse_phases = []
    for phase in range(stride):
        column_mask = jnp.asarray((head_of_column % stride == phase).astype(np.float32))
        head_mask = jnp.asarray(np.arange(local_heads) % stride == phase)
        out_phases.append(level_out * column_mask[None, :])
        lse_phases.append(jnp.where(head_mask[None, :], level_lse, -jnp.inf))
    full_out = jnp.stack(out_phases, axis=1).reshape(used_count * stride, feature_width)
    full_lse = jnp.stack(lse_phases, axis=1).reshape(used_count * stride, local_heads)
    return (full_out, full_lse)


def fold_block(fold_state, queries, keys, values, valid, score_scale):
    running_max, running_total, running_acc = fold_state
    local_heads = queries.shape[1] // HEAD_DIM
    query_block = queries.reshape(queries.shape[0], local_heads, HEAD_DIM)
    key_block = keys.reshape(keys.shape[0], local_heads, HEAD_DIM)
    value_block = values.reshape(values.shape[0], local_heads, HEAD_DIM)
    scores = (
        jnp.einsum("qad,kad->qak", query_block, key_block, preferred_element_type=jnp.float32)
        * score_scale
    )
    scores = jnp.where(valid[None, None, :], scores, -jnp.inf)
    new_max = jnp.maximum(running_max, jnp.max(scores, axis=-1))
    safe_max = jnp.where(new_max == -jnp.inf, 0.0, new_max)
    rescale = jnp.exp(running_max - safe_max)
    exp_scores = jnp.exp(scores - safe_max[:, :, None])
    new_total = running_total * rescale + jnp.sum(exp_scores, axis=-1)
    weighted = jnp.einsum(
        "qak,kad->qad",
        exp_scores.astype(jnp.bfloat16),
        value_block,
        preferred_element_type=jnp.float32,
    )
    new_acc = running_acc * rescale[:, :, None] + weighted
    return (new_max, new_total, new_acc)


def any_length(query_rows, key_rows, value_rows):
    row_count = query_rows.shape[0]
    feature_width = query_rows.shape[1]
    local_heads = feature_width // HEAD_DIM
    shards = lax.axis_size("seq")
    score_scale = HEAD_DIM ** (-0.5)
    first_out, first_lse = local_segments(query_rows, key_rows, value_rows, SEG_A, score_scale)
    used_two = row_count // 2
    seg_two = SEG_B // 2
    query_two = pick_rows(query_rows, 2)
    key_two = pick_rows(key_rows, 2)
    value_two = pick_rows(value_rows, 2)
    stacked = jnp.stack([key_two, value_two])
    for bit_index in range((seg_two // used_two).bit_length() - 1):
        partner = swapped(stacked, "seq", bit_index)
        stacked = jnp.concatenate([stacked, partner], axis=1)
    second_out, second_lse = attend_rows(query_two, stacked[0], stacked[1], score_scale)
    span_tokens = row_count * shards
    group_span = span_tokens // row_count
    used_three = row_count // 4
    wide_queries = pick_rows(query_rows, 4)
    wide_keys = pick_rows(key_rows, 4)
    wide_values = pick_rows(value_rows, 4)
    my_group = lax.axis_index("seq") // group_span
    key_limit = max(1, 1048576 // (local_heads * used_three))
    initial = (
        jnp.full((used_three, local_heads), -jnp.inf, jnp.float32),
        jnp.zeros((used_three, local_heads), jnp.float32),
        jnp.zeros((used_three, local_heads, HEAD_DIM), jnp.float32),
    )
    pieces = (
        lax.all_gather(wide_keys, "seq", axis=0, tiled=True),
        lax.all_gather(wide_values, "seq", axis=0, tiled=True),
    )
    piece_rows = pieces[0].shape[0]
    block = math.gcd(piece_rows, key_limit)
    key_blocks = pieces[0].reshape(piece_rows // block, block, feature_width)
    value_blocks = pieces[1].reshape(piece_rows // block, block, feature_width)
    block_starts = jnp.arange(piece_rows // block, dtype=jnp.int32) * block

    def fold_step(inner_state, items):
        owners = (items[2] + jnp.arange(block, dtype=jnp.int32)) // used_three
        valid = owners // group_span == my_group
        return (fold_block(inner_state, wide_queries, items[0], items[1], valid, score_scale), None)

    final_state, unused = lax.scan(fold_step, initial, (key_blocks, value_blocks, block_starts))
    final_max, final_total, final_acc = final_state
    third_out = (final_acc / final_total[:, :, None]).reshape(used_three, feature_width)
    third_lse = final_max + jnp.log(final_total)
    second_full, second_lse_full = spread_rows(second_out, second_lse, 2)
    third_full, third_lse_full = spread_rows(third_out, third_lse, 4)
    peak = jnp.maximum(jnp.maximum(first_lse, second_lse_full), third_lse_full)
    weight_one = jnp.exp(first_lse - peak)
    weight_two = jnp.exp(second_lse_full - peak)
    weight_three = jnp.exp(third_lse_full - peak)
    denominator = jnp.repeat(weight_one + weight_two + weight_three, HEAD_DIM, axis=1)
    numerator = jnp.repeat(weight_one, HEAD_DIM, axis=1) * first_out
    numerator = numerator + jnp.repeat(weight_two, HEAD_DIM, axis=1) * second_full
    numerator = numerator + jnp.repeat(weight_three, HEAD_DIM, axis=1) * third_full
    return (numerator / denominator).astype(jnp.bfloat16)


STRIDES = 4
LANES = 128
SPAN = STRIDES * LANES
NEAR_KEYS = 256
LOW_HEADS = 1
TAIL = 8
LOG2E = 1.4426950408889634
FACTOR = HEAD_DIM ** (-0.5) * LOG2E
LEAST_TOTAL = 2.0 ** -60
MOST_TOTAL = 2.0 ** 100
VMEM_BYTES = 16 * 1024 * 1024


def dot_nn(left, right):
    return lax.dot_general(left, right, (((1,), (0,)), ((), ())), preferred_element_type=jnp.float32)


def dot_nt(left, right):
    return lax.dot_general(left, right, (((1,), (1,)), ((), ())), preferred_element_type=jnp.float32)


def one_hot(shape, which):
    rows = lax.broadcasted_iota(jnp.int32, shape, 0)
    columns = lax.broadcasted_iota(jnp.int32, shape, 1)
    return jnp.where(which(rows, columns), 1.0, 0.0).astype(jnp.bfloat16)


def call(kernel, outs, args, scratch, flops, space=pltpu.VMEM):
    return pl.pallas_call(
        kernel,
        out_shape=outs,
        in_specs=[pl.BlockSpec(memory_space=space)] * len(args),
        out_specs=jax.tree.map(lambda out: pl.BlockSpec(memory_space=pltpu.VMEM), outs),
        scratch_shapes=scratch,
        compiler_params=pltpu.CompilerParams(vmem_limit_bytes=VMEM_BYTES),
        cost_estimate=pl.CostEstimate(flops=flops, bytes_accessed=2 << 20, transcendentals=0),
    )(*args)


def pack_kernel(q_hbm, k_hbm, v_hbm, q_ref, k_ref, v_ref, m2, m3, m1, m0, by_head, arrivals):
    width, rows = q_ref.shape
    blocks = range(rows // SPAN)
    copies = [
        [
            pltpu.make_async_copy(
                source.at[:, pl.ds(block * SPAN, SPAN)], target.at[:, pl.ds(block * SPAN, SPAN)], arrivals.at[block, at]
            )
            for at, (source, target) in enumerate(((q_hbm, q_ref), (k_hbm, k_ref), (v_hbm, v_ref)))
        ]
        for block in blocks
    ]
    for block in blocks:
        for copy in copies[block]:
            copy.start()
    heads = width // HEAD_DIM
    picks = [
        one_hot((SPAN, 2 * LANES), lambda row, column: row == column % LANES * STRIDES + column // LANES * 2 + parity)
        for parity in range(2)
    ]
    for block in blocks:
        for copy in copies[block]:
            copy.wait()
        for parity, pick in enumerate(picks):
            mine = range(parity, heads, 2)
            pieces = [
                ref[pl.ds(head * HEAD_DIM, HEAD_DIM), pl.ds(block * SPAN, SPAN)]
                for head in mine
                for ref in (q_ref, k_ref, v_ref)
            ]
            picked = dot_nn(jnp.concatenate(pieces, axis=0), pick).astype(jnp.bfloat16)
            for at, head in enumerate(mine):
                features = picked[at * 3 * HEAD_DIM : (at + 1) * 3 * HEAD_DIM]
                for klass in range(2):
                    phase = (head + 2 * klass) % STRIDES // 2
                    by_head[head, :, pl.ds(klass * rows // STRIDES + block * LANES, LANES)] = features[
                        :, phase * LANES : (phase + 1) * LANES
                    ]
    me = lax.axis_index("seq")
    for shift, message in ((2, m2), (3, m3), (1, m1), (0, m0)):
        message[...] = by_head[jnp.bitwise_xor(me, shift)]


def with_ones(block):
    count = block.shape[1]
    extra = one_hot((2 * TAIL, count), lambda row, column: row == 0)
    return jnp.concatenate([block, extra], axis=0)


def upright(block):
    count = block.shape[1]
    size = min(count, 2 * LANES)
    eye = one_hot((size, size), lambda row, column: row == column)
    pieces = [dot_nt(eye, block[:, at : at + size]) for at in range(0, count, size)]
    return jnp.concatenate(pieces, axis=0).astype(jnp.bfloat16)


def doubled(scores, shift):
    half = scores.shape[0] // 2
    one = jnp.where(lax.broadcasted_iota(jnp.int32, (1, scores.shape[1]), 1) < half, 1.0, 0.0)
    first = jnp.exp2(scores[:half] * FACTOR + (one - shift))
    second = jnp.exp2(scores[half:] * FACTOR - shift)
    return jnp.concatenate([first.astype(jnp.bfloat16), second.astype(jnp.bfloat16)], axis=0)


def plain(*jobs):
    steps = [(at, queries, keys, values) for at, (queries, groups) in enumerate(jobs) for keys, values in groups]
    results = [None] * len(jobs)
    ahead = dot_nn(steps[0][2][...], steps[0][1])
    for now, (at, _, _, values) in enumerate(steps):
        scores = ahead
        if now + 1 < len(steps):
            ahead = dot_nn(steps[now + 1][2][...], steps[now + 1][1])
        term = dot_nn(values, doubled(scores, 0.0))
        results[at] = term if results[at] is None else results[at] + term
    return results


def shifted(queries, groups):
    scores = [dot_nn(keys[...], queries) for keys, _ in groups]
    top = functools.reduce(jnp.maximum, [jnp.max(block, axis=0, keepdims=True) for block in scores]) * FACTOR
    terms = [dot_nn(values, doubled(block, top)) for block, (_, values) in zip(scores, groups)]
    return functools.reduce(jnp.add, terms), top


def in_range(totals):
    low = functools.reduce(jnp.minimum, totals)
    high = functools.reduce(jnp.maximum, totals)
    return jnp.logical_and(jnp.min(low) >= LEAST_TOTAL, jnp.max(high) <= MOST_TOTAL)


def near_kernel(first, qt_ref, kt_ref, vt_ref, out_ref, keys_ref):
    rows = qt_ref.shape[1]
    heads = out_ref.shape[0]
    for head in range(heads):
        keys_ref[head] = upright(kt_ref[pl.ds((first + head) * HEAD_DIM, HEAD_DIM), :])
    blocks = [(head, start) for head in range(heads) for start in range(0, rows, SPAN)]
    pieces = range(0, rows, NEAR_KEYS)

    def scores_of(block, piece):
        head, start = block
        queries = qt_ref[pl.ds((first + head) * HEAD_DIM, HEAD_DIM), pl.ds(start, SPAN)]
        return dot_nn(keys_ref[head, pl.ds(piece, NEAR_KEYS), :], queries)

    def folded(values, join, held):
        parts = [values[at : at + 8] for at in range(0, NEAR_KEYS, 8)]
        return functools.reduce(join, parts if held is None else [held, *parts])

    now, peaks = [], None
    for piece in pieces:
        now.append(scores_of(blocks[0], piece))
        peaks = folded(now[-1], jnp.maximum, peaks)
    for at, (head, start) in enumerate(blocks):
        top = jnp.max(peaks, axis=0, keepdims=True) * FACTOR
        later, peaks, result, totals = [], None, None, None
        for piece, scores in zip(pieces, now):
            if at + 1 < len(blocks):
                later.append(scores_of(blocks[at + 1], piece))
                peaks = folded(later[-1], jnp.maximum, peaks)
            probs = jnp.exp2(scores * FACTOR - top)
            totals = folded(probs, jnp.add, totals)
            values = vt_ref[pl.ds((first + head) * HEAD_DIM, HEAD_DIM), pl.ds(piece, NEAR_KEYS)]
            term = dot_nn(values, probs.astype(jnp.bfloat16))
            result = term if result is None else result + term
        lanes = pl.ds(start, SPAN)
        out_ref[head, pl.ds(0, HEAD_DIM), lanes] = result
        out_ref[head, pl.ds(HEAD_DIM, 1), lanes] = jnp.sum(totals, axis=0, keepdims=True)
        out_ref[head, pl.ds(HEAD_DIM + 1, 1), lanes] = top
        now = later


def finished(result, top):
    total = result[HEAD_DIM : HEAD_DIM + 1]
    lse = jnp.log2(total) if top is None else top + jnp.log2(total)
    high = lse.astype(jnp.bfloat16).astype(jnp.float32)
    middle = (lse - high).astype(jnp.bfloat16).astype(jnp.float32)
    low = lse - high - middle
    row = lax.broadcasted_iota(jnp.int32, (TAIL, total.shape[1]), 0)
    parts = jnp.where(row == 0, high, jnp.where(row == 1, middle, jnp.where(row == 2, low, 0.0)))
    return jnp.concatenate([result[:HEAD_DIM] / total, parts], axis=0).astype(jnp.bfloat16)


def make_keys(keys_ref, message):
    keys_ref[...] = upright(message[pl.ds(HEAD_DIM, HEAD_DIM), :])


def values_of(message):
    return with_ones(message[pl.ds(2 * HEAD_DIM, HEAD_DIM), :])


def queries_of(message):
    return message[pl.ds(0, HEAD_DIM), :]


def settle(results, outs, messages, every):
    for result, out in zip(results, outs):
        out[...] = finished(result, None)

    @pl.when(jnp.logical_not(in_range([result[HEAD_DIM : HEAD_DIM + 1] for result in results])))
    def again():
        for message, out in zip(messages, outs):
            out[...] = finished(*shifted(queries_of(message), every()))


def early_kernel(m0, ma, keys0, keysa, part0, parta):
    make_keys(keys0, m0)
    make_keys(keysa, ma)
    groups = ((keys0, values_of(m0)), (keysa, values_of(ma)))
    part0[...], parta[...] = plain((queries_of(m0), groups), (queries_of(ma), groups))


def cross_kernel(m0, m1, m2, m3, keys0, keys3, part3, f2, f3, keys1, keys2):
    make_keys(keys1, m1)
    make_keys(keys2, m2)
    groups = [(keys, values_of(message)) for keys, message in ((keys0, m0), (keys1, m1), (keys2, m2), (keys3, m3))]
    whole, rest = plain((queries_of(m2), groups), (queries_of(m3), groups[1:3]))
    settle((whole, part3[...] + rest), (f2, f3), (m2, m3), lambda: groups)


def next_kernel(m0, m1, m2, m3, keys0, keys1, keys2, keys3, f1):
    groups = [(keys, values_of(message)) for keys, message in ((keys0, m0), (keys1, m1), (keys2, m2), (keys3, m3))]
    (whole,) = plain((queries_of(m1), groups))
    settle((whole,), (f1,), (m1,), lambda: groups)


def own_kernel(m0, m1, m2, m3, keys0, keys1, keys2, keys3, part0, low_ref, high_ref, rows_ref, f0):
    groups = [(keys, values_of(message)) for keys, message in ((keys0, m0), (keys1, m1), (keys2, m2), (keys3, m3))]
    (rest,) = plain((queries_of(m0), groups[1:3]))
    settle((part0[...] + rest,), (f0,), (m0,), lambda: groups)
    merge_kernel((0,), low_ref, high_ref, f0, rows_ref)


def merge_kernel(steps, low_ref, high_ref, *refs):
    *results, rows_ref = refs
    each, _, rows = low_ref.shape
    half = rows // STRIDES
    me = lax.axis_index("seq")
    position = lax.broadcasted_iota(jnp.int32, (1, SPAN), 1)
    for at, (step, result) in enumerate(zip(steps, results)):
        head = jnp.bitwise_xor(me, step)
        place = one_hot(
            (2 * LANES, SPAN),
            lambda row, column: column == row % LANES * STRIDES + (head + row // LANES * 2) % STRIDES,
        )
        used = position % 2 == head % 2
        for block in range(rows // SPAN):
            lanes = pl.ds(block * SPAN, SPAN)
            piece = [result[:, pl.ds(klass * half + block * LANES, LANES)] for klass in range(2)]
            there = dot_nn(jnp.concatenate(piece, axis=1), place)
            in_low = low_ref[jnp.minimum(head, each - 1), :, lanes]
            level = jnp.where(head < each, in_low, high_ref[jnp.maximum(head - each, 0), :, lanes])
            near = level[:HEAD_DIM]
            total = level[HEAD_DIM : HEAD_DIM + 1]
            top = level[HEAD_DIM + 1 : HEAD_DIM + 2]
            lse = there[HEAD_DIM : HEAD_DIM + 1] + there[HEAD_DIM + 1 : HEAD_DIM + 2] + there[HEAD_DIM + 2 : HEAD_DIM + 3]
            near_lse = top + jnp.log2(total)
            peak = jnp.where(used, jnp.maximum(near_lse, lse), near_lse)
            weight = jnp.exp2(top - peak)
            far = jnp.where(used, jnp.exp2(lse - peak), 0.0)
            share = 1.0 / (total * weight + far)
            merged = near * (weight * share) + there[:HEAD_DIM] * (far * share)
            rows_ref[at, :, lanes] = merged.astype(jnp.bfloat16)


def last_kernel(low_ref, high_ref, own_ref, far_ref, result, out_hbm, rows_ref, sent):
    me = lax.axis_index("seq")

    def sending(step, rows):
        head = jnp.bitwise_xor(me, step)
        features = pl.ds(pl.multiple_of(head * HEAD_DIM, HEAD_DIM), HEAD_DIM)
        return pltpu.make_async_copy(rows, out_hbm.at[features], sent.at[step])

    copies = [sending(0, own_ref.at[0]), sending(2, far_ref.at[0]), sending(3, far_ref.at[1])]
    for copy in copies:
        copy.start()
    merge_kernel((1,), low_ref, high_ref, result, rows_ref)
    copies.append(sending(1, rows_ref.at[0]))
    copies[-1].start()
    for copy in copies:
        copy.wait()


def exchanged(block, step):
    return lax.ppermute(block, "seq", [(i, i ^ step) for i in range(lax.axis_size("seq"))])


def whole_slide(query_rows, key_rows, value_rows):
    rows, width = query_rows.shape
    heads = width // HEAD_DIM
    count = rows // 2
    bf16, f32 = jnp.bfloat16, jnp.float32
    turned = [pltpu.with_memory_space_constraint(block.T, pltpu.HBM) for block in (query_rows, key_rows, value_rows)]
    *here, m2, m3, m1, m0 = call(
        pack_kernel,
        [jax.ShapeDtypeStruct((width, rows), bf16)] * 3 + [jax.ShapeDtypeStruct((3 * HEAD_DIM, count), bf16)] * heads,
        turned,
        [pltpu.VMEM((heads, 3 * HEAD_DIM, count), bf16), pltpu.SemaphoreType.DMA((rows // SPAN, 3))],
        1 << 28,
        pltpu.HBM,
    )
    n2, n3 = exchanged(m2, 2), exchanged(m3, 3)

    def near(first, some):
        return call(
            functools.partial(near_kernel, first),
            jax.ShapeDtypeStruct((some, HEAD_DIM + TAIL, rows), f32),
            here,
            [pltpu.VMEM((some, rows, HEAD_DIM), bf16)],
            4 * some * rows * rows * 256,
        )

    low = near(0, LOW_HEADS)
    low, m1, *here = lax.optimization_barrier((low, m1, *here))
    n1 = exchanged(m1, 1)
    high = near(LOW_HEADS, heads - LOW_HEADS)
    result = jax.ShapeDtypeStruct((HEAD_DIM + TAIL, count), bf16)
    part = jax.ShapeDtypeStruct((HEAD_DIM + 2 * TAIL, count), f32)
    keys = jax.ShapeDtypeStruct((count, HEAD_DIM), bf16)
    work = 4 * count * count * 256
    n3, high = lax.optimization_barrier((n3, high))
    keys0, keys3, part0, part3 = call(early_kernel, [keys, keys, part, part], (m0, n3), [], 4 * work)
    keys0, keys3, n1, n2 = lax.optimization_barrier((keys0, keys3, n1, n2))
    f2, f3, keys1, keys2 = call(
        cross_kernel, [result, result, keys, keys], (m0, n1, n2, n3, keys0, keys3, part3), [], 6 * work
    )
    f2, f3, keys2 = lax.optimization_barrier((f2, f3, keys2))
    g2, g3 = exchanged(f2, 2), exchanged(f3, 3)
    every = (m0, n1, n2, n3, keys0, keys1, keys2, keys3)
    f1 = call(next_kernel, result, every, [], 4 * work)
    f1, part0 = lax.optimization_barrier((f1, part0))
    g1 = exchanged(f1, 1)
    own = call(
        own_kernel,
        jax.ShapeDtypeStruct((1, HEAD_DIM, rows), bf16),
        (*every, part0, low, high),
        [pltpu.VMEM((HEAD_DIM + TAIL, count), bf16)],
        2 * work,
    )
    def merged(steps, results):
        shape = jax.ShapeDtypeStruct((len(steps), HEAD_DIM, rows), bf16)
        return call(functools.partial(merge_kernel, steps), shape, (low, high, *results), [], len(steps) << 29)

    others = merged((2, 3), (g2, g3))
    return pl.pallas_call(
        last_kernel,
        out_shape=jax.ShapeDtypeStruct((width, rows), bf16),
        in_specs=[pl.BlockSpec(memory_space=pltpu.VMEM)] * 5,
        out_specs=pl.BlockSpec(memory_space=pl.ANY),
        scratch_shapes=[pltpu.VMEM((1, HEAD_DIM, rows), bf16), pltpu.SemaphoreType.DMA((heads,))],
        compiler_params=pltpu.CompilerParams(vmem_limit_bytes=VMEM_BYTES),
        cost_estimate=pl.CostEstimate(flops=1 << 29, bytes_accessed=1 << 20, transcendentals=0),
    )(low, high, own, others, g1).T


def per_device(query_rows, key_rows, value_rows):
    rows, width = query_rows.shape
    shards = lax.axis_size("seq")
    if rows == SEG_A and rows * shards == SEG_B and width == shards * HEAD_DIM and shards == STRIDES:
        return whole_slide(query_rows, key_rows, value_rows)
    return any_length(query_rows, key_rows, value_rows)


def solution(mesh):
    return jax.shard_map(
        per_device,
        mesh=mesh,
        in_specs=(
            P(("slides", "seq"), "head"),
            P(("slides", "seq"), "head"),
            P(("slides", "seq"), "head"),
        ),
        out_specs=P(("slides", "seq"), "head"),
        check_vma=False,
    )
```

```python
import functools
import math

import jax
import jax.numpy as jnp
import numpy as np
from jax import lax
from jax.experimental import pallas as pl
from jax.experimental.pallas import tpu as pltpu
from jax.sharding import PartitionSpec as P

HEAD_DIM = 48
SEG_A = 1024
SEG_B = 4096


def swapped(shard, axis, stride):
    return lax.ppermute(shard, axis, [(i, i ^ 1 << stride) for i in range(lax.axis_size(axis))])


def attend(query_flat, key_flat, value_flat, score_scale):
    local_heads = query_flat.shape[1] // HEAD_DIM
    query_block = query_flat.reshape(query_flat.shape[0], local_heads, HEAD_DIM)
    key_block = key_flat.reshape(key_flat.shape[0], local_heads, HEAD_DIM)
    value_block = value_flat.reshape(value_flat.shape[0], local_heads, HEAD_DIM)
    scores = (
        jnp.einsum("qad,kad->qak", query_block, key_block, preferred_element_type=jnp.float32)
        * score_scale
    )
    row_max = jnp.max(scores, axis=-1)
    exp_scores = jnp.exp(scores - row_max[:, :, None])
    row_total = jnp.sum(exp_scores, axis=-1)
    weighted = jnp.einsum(
        "qak,kad->qad",
        exp_scores.astype(jnp.bfloat16),
        value_block,
        preferred_element_type=jnp.float32,
    )
    level_out = weighted / row_total[:, :, None]
    return (
        level_out.reshape(query_flat.shape[0], local_heads * HEAD_DIM),
        row_max + jnp.log(row_total),
    )


def attend_rows(query_flat, key_flat, value_flat, score_scale):
    count, feature_width = query_flat.shape
    local_heads = feature_width // HEAD_DIM
    keys = key_flat.shape[0]
    rows = math.gcd(count, max(1, 1048576 // (local_heads * keys)))

    def one_piece(query_piece):
        return attend(query_piece, key_flat, value_flat, score_scale)

    outs, lses = lax.map(one_piece, query_flat.reshape(count // rows, rows, feature_width))
    return (outs.reshape(count, feature_width), lses.reshape(count, local_heads))


def local_segments(query_flat, key_flat, value_flat, seg_rows, score_scale):
    count, feature_width = query_flat.shape
    local_heads = feature_width // HEAD_DIM
    shape = (count // seg_rows, seg_rows, feature_width)

    def one_segment(parts):
        return attend_rows(parts[0], parts[1], parts[2], score_scale)

    outs, lses = lax.map(
        one_segment, (query_flat.reshape(shape), key_flat.reshape(shape), value_flat.reshape(shape))
    )
    return (outs.reshape(count, feature_width), lses.reshape(count, local_heads))


def pick_rows(block, stride):
    row_count, feature_width = block.shape
    local_heads = feature_width // HEAD_DIM
    grid = block.reshape(row_count // stride, stride * feature_width)
    columns = []
    for head in range(local_heads):
        begin = head % stride * feature_width + head * HEAD_DIM
        columns.append(grid[:, begin : begin + HEAD_DIM])
    return jnp.concatenate(columns, axis=1)


def spread_rows(level_out, level_lse, stride):
    used_count, feature_width = level_out.shape
    local_heads = feature_width // HEAD_DIM
    head_of_column = np.arange(feature_width) // HEAD_DIM
    out_phases = []
    lse_phases = []
    for phase in range(stride):
        column_mask = jnp.asarray((head_of_column % stride == phase).astype(np.float32))
        head_mask = jnp.asarray(np.arange(local_heads) % stride == phase)
        out_phases.append(level_out * column_mask[None, :])
        lse_phases.append(jnp.where(head_mask[None, :], level_lse, -jnp.inf))
    full_out = jnp.stack(out_phases, axis=1).reshape(used_count * stride, feature_width)
    full_lse = jnp.stack(lse_phases, axis=1).reshape(used_count * stride, local_heads)
    return (full_out, full_lse)


def fold_block(fold_state, queries, keys, values, valid, score_scale):
    running_max, running_total, running_acc = fold_state
    local_heads = queries.shape[1] // HEAD_DIM
    query_block = queries.reshape(queries.shape[0], local_heads, HEAD_DIM)
    key_block = keys.reshape(keys.shape[0], local_heads, HEAD_DIM)
    value_block = values.reshape(values.shape[0], local_heads, HEAD_DIM)
    scores = (
        jnp.einsum("qad,kad->qak", query_block, key_block, preferred_element_type=jnp.float32)
        * score_scale
    )
    scores = jnp.where(valid[None, None, :], scores, -jnp.inf)
    new_max = jnp.maximum(running_max, jnp.max(scores, axis=-1))
    safe_max = jnp.where(new_max == -jnp.inf, 0.0, new_max)
    rescale = jnp.exp(running_max - safe_max)
    exp_scores = jnp.exp(scores - safe_max[:, :, None])
    new_total = running_total * rescale + jnp.sum(exp_scores, axis=-1)
    weighted = jnp.einsum(
        "qak,kad->qad",
        exp_scores.astype(jnp.bfloat16),
        value_block,
        preferred_element_type=jnp.float32,
    )
    new_acc = running_acc * rescale[:, :, None] + weighted
    return (new_max, new_total, new_acc)


def any_length(query_rows, key_rows, value_rows):
    row_count = query_rows.shape[0]
    feature_width = query_rows.shape[1]
    local_heads = feature_width // HEAD_DIM
    shards = lax.axis_size("seq")
    score_scale = HEAD_DIM ** (-0.5)
    first_out, first_lse = local_segments(query_rows, key_rows, value_rows, SEG_A, score_scale)
    used_two = row_count // 2
    seg_two = SEG_B // 2
    query_two = pick_rows(query_rows, 2)
    key_two = pick_rows(key_rows, 2)
    value_two = pick_rows(value_rows, 2)
    stacked = jnp.stack([key_two, value_two])
    for bit_index in range((seg_two // used_two).bit_length() - 1):
        partner = swapped(stacked, "seq", bit_index)
        stacked = jnp.concatenate([stacked, partner], axis=1)
    second_out, second_lse = attend_rows(query_two, stacked[0], stacked[1], score_scale)
    span_tokens = row_count * shards
    group_span = span_tokens // row_count
    used_three = row_count // 4
    wide_queries = pick_rows(query_rows, 4)
    wide_keys = pick_rows(key_rows, 4)
    wide_values = pick_rows(value_rows, 4)
    my_group = lax.axis_index("seq") // group_span
    key_limit = max(1, 1048576 // (local_heads * used_three))
    initial = (
        jnp.full((used_three, local_heads), -jnp.inf, jnp.float32),
        jnp.zeros((used_three, local_heads), jnp.float32),
        jnp.zeros((used_three, local_heads, HEAD_DIM), jnp.float32),
    )
    pieces = (
        lax.all_gather(wide_keys, "seq", axis=0, tiled=True),
        lax.all_gather(wide_values, "seq", axis=0, tiled=True),
    )
    piece_rows = pieces[0].shape[0]
    block = math.gcd(piece_rows, key_limit)
    key_blocks = pieces[0].reshape(piece_rows // block, block, feature_width)
    value_blocks = pieces[1].reshape(piece_rows // block, block, feature_width)
    block_starts = jnp.arange(piece_rows // block, dtype=jnp.int32) * block

    def fold_step(inner_state, items):
        owners = (items[2] + jnp.arange(block, dtype=jnp.int32)) // used_three
        valid = owners // group_span == my_group
        return (fold_block(inner_state, wide_queries, items[0], items[1], valid, score_scale), None)

    final_state, unused = lax.scan(fold_step, initial, (key_blocks, value_blocks, block_starts))
    final_max, final_total, final_acc = final_state
    third_out = (final_acc / final_total[:, :, None]).reshape(used_three, feature_width)
    third_lse = final_max + jnp.log(final_total)
    second_full, second_lse_full = spread_rows(second_out, second_lse, 2)
    third_full, third_lse_full = spread_rows(third_out, third_lse, 4)
    peak = jnp.maximum(jnp.maximum(first_lse, second_lse_full), third_lse_full)
    weight_one = jnp.exp(first_lse - peak)
    weight_two = jnp.exp(second_lse_full - peak)
    weight_three = jnp.exp(third_lse_full - peak)
    denominator = jnp.repeat(weight_one + weight_two + weight_three, HEAD_DIM, axis=1)
    numerator = jnp.repeat(weight_one, HEAD_DIM, axis=1) * first_out
    numerator = numerator + jnp.repeat(weight_two, HEAD_DIM, axis=1) * second_full
    numerator = numerator + jnp.repeat(weight_three, HEAD_DIM, axis=1) * third_full
    return (numerator / denominator).astype(jnp.bfloat16)


STRIDES = 4
LANES = 128
SPAN = STRIDES * LANES
NEAR_KEYS = 256
LOW_HEADS = 1
TAIL = 8
LOG2E = 1.4426950408889634
FACTOR = HEAD_DIM ** (-0.5) * LOG2E
LEAST_TOTAL = 2.0 ** -60
MOST_TOTAL = 2.0 ** 100
VMEM_BYTES = 16 * 1024 * 1024


def dot_nn(left, right):
    return lax.dot_general(left, right, (((1,), (0,)), ((), ())), preferred_element_type=jnp.float32)


def dot_nt(left, right):
    return lax.dot_general(left, right, (((1,), (1,)), ((), ())), preferred_element_type=jnp.float32)


def one_hot(shape, which):
    rows = lax.broadcasted_iota(jnp.int32, shape, 0)
    columns = lax.broadcasted_iota(jnp.int32, shape, 1)
    return jnp.where(which(rows, columns), 1.0, 0.0).astype(jnp.bfloat16)


def call(kernel, outs, args, scratch, flops, space=pltpu.VMEM):
    return pl.pallas_call(
        kernel,
        out_shape=outs,
        in_specs=[pl.BlockSpec(memory_space=space)] * len(args),
        out_specs=jax.tree.map(lambda out: pl.BlockSpec(memory_space=pltpu.VMEM), outs),
        scratch_shapes=scratch,
        compiler_params=pltpu.CompilerParams(vmem_limit_bytes=VMEM_BYTES),
        cost_estimate=pl.CostEstimate(flops=flops, bytes_accessed=2 << 20, transcendentals=0),
    )(*args)


def pack_kernel(q_hbm, k_hbm, v_hbm, q_ref, k_ref, v_ref, m2, m3, m1, m0, by_head, arrivals):
    width, rows = q_ref.shape
    blocks = range(rows // SPAN)
    copies = [
        [
            pltpu.make_async_copy(
                source.at[:, pl.ds(block * SPAN, SPAN)], target.at[:, pl.ds(block * SPAN, SPAN)], arrivals.at[block, at]
            )
            for at, (source, target) in enumerate(((q_hbm, q_ref), (k_hbm, k_ref), (v_hbm, v_ref)))
        ]
        for block in blocks
    ]
    for block in blocks:
        for copy in copies[block]:
            copy.start()
    heads = width // HEAD_DIM
    picks = [
        one_hot((SPAN, 2 * LANES), lambda row, column: row == column % LANES * STRIDES + column // LANES * 2 + parity)
        for parity in range(2)
    ]
    for block in blocks:
        for copy in copies[block]:
            copy.wait()
        for parity, pick in enumerate(picks):
            mine = range(parity, heads, 2)
            pieces = [
                ref[pl.ds(head * HEAD_DIM, HEAD_DIM), pl.ds(block * SPAN, SPAN)]
                for head in mine
                for ref in (q_ref, k_ref, v_ref)
            ]
            picked = dot_nn(jnp.concatenate(pieces, axis=0), pick).astype(jnp.bfloat16)
            for at, head in enumerate(mine):
                features = picked[at * 3 * HEAD_DIM : (at + 1) * 3 * HEAD_DIM]
                for klass in range(2):
                    phase = (head + 2 * klass) % STRIDES // 2
                    by_head[head, :, pl.ds(klass * rows // STRIDES + block * LANES, LANES)] = features[
                        :, phase * LANES : (phase + 1) * LANES
                    ]
    me = lax.axis_index("seq")
    for shift, message in ((2, m2), (3, m3), (1, m1), (0, m0)):
        message[...] = by_head[jnp.bitwise_xor(me, shift)]


def with_ones(block):
    count = block.shape[1]
    extra = one_hot((2 * TAIL, count), lambda row, column: row == 0)
    return jnp.concatenate([block, extra], axis=0)


def upright(block):
    count = block.shape[1]
    size = min(count, 2 * LANES)
    eye = one_hot((size, size), lambda row, column: row == column)
    pieces = [dot_nt(eye, block[:, at : at + size]) for at in range(0, count, size)]
    return jnp.concatenate(pieces, axis=0).astype(jnp.bfloat16)


def doubled(scores, shift):
    half = scores.shape[0] // 2
    one = jnp.where(lax.broadcasted_iota(jnp.int32, (1, scores.shape[1]), 1) < half, 1.0, 0.0)
    first = jnp.exp2(scores[:half] * FACTOR + (one - shift))
    second = jnp.exp2(scores[half:] * FACTOR - shift)
    return jnp.concatenate([first.astype(jnp.bfloat16), second.astype(jnp.bfloat16)], axis=0)


def plain(*jobs):
    steps = [(at, queries, keys, values) for at, (queries, groups) in enumerate(jobs) for keys, values in groups]
    results = [None] * len(jobs)
    ahead = dot_nn(steps[0][2][...], steps[0][1])
    for now, (at, _, _, values) in enumerate(steps):
        scores = ahead
        if now + 1 < len(steps):
            ahead = dot_nn(steps[now + 1][2][...], steps[now + 1][1])
        term = dot_nn(values, doubled(scores, 0.0))
        results[at] = term if results[at] is None else results[at] + term
    return results


def shifted(queries, groups):
    scores = [dot_nn(keys[...], queries) for keys, _ in groups]
    top = functools.reduce(jnp.maximum, [jnp.max(block, axis=0, keepdims=True) for block in scores]) * FACTOR
    terms = [dot_nn(values, doubled(block, top)) for block, (_, values) in zip(scores, groups)]
    return functools.reduce(jnp.add, terms), top


def in_range(totals):
    low = functools.reduce(jnp.minimum, totals)
    high = functools.reduce(jnp.maximum, totals)
    return jnp.logical_and(jnp.min(low) >= LEAST_TOTAL, jnp.max(high) <= MOST_TOTAL)


def near_kernel(first, qt_ref, kt_ref, vt_ref, out_ref, keys_ref):
    rows = qt_ref.shape[1]
    heads = out_ref.shape[0]
    for head in range(heads):
        keys_ref[head] = upright(kt_ref[pl.ds((first + head) * HEAD_DIM, HEAD_DIM), :])
    blocks = [(head, start) for head in range(heads) for start in range(0, rows, SPAN)]
    pieces = range(0, rows, NEAR_KEYS)

    def scores_of(block, piece):
        head, start = block
        queries = qt_ref[pl.ds((first + head) * HEAD_DIM, HEAD_DIM), pl.ds(start, SPAN)]
        return dot_nn(keys_ref[head, pl.ds(piece, NEAR_KEYS), :], queries)

    def folded(values, join, held):
        parts = [values[at : at + 8] for at in range(0, NEAR_KEYS, 8)]
        return functools.reduce(join, parts if held is None else [held, *parts])

    now, peaks = [], None
    for piece in pieces:
        now.append(scores_of(blocks[0], piece))
        peaks = folded(now[-1], jnp.maximum, peaks)
    for at, (head, start) in enumerate(blocks):
        top = jnp.max(peaks, axis=0, keepdims=True) * FACTOR
        later, peaks, result, totals = [], None, None, None
        for piece, scores in zip(pieces, now):
            if at + 1 < len(blocks):
                later.append(scores_of(blocks[at + 1], piece))
                peaks = folded(later[-1], jnp.maximum, peaks)
            probs = jnp.exp2(scores * FACTOR - top)
            totals = folded(probs, jnp.add, totals)
            values = vt_ref[pl.ds((first + head) * HEAD_DIM, HEAD_DIM), pl.ds(piece, NEAR_KEYS)]
            term = dot_nn(values, probs.astype(jnp.bfloat16))
            result = term if result is None else result + term
        lanes = pl.ds(start, SPAN)
        out_ref[head, pl.ds(0, HEAD_DIM), lanes] = result
        out_ref[head, pl.ds(HEAD_DIM, 1), lanes] = jnp.sum(totals, axis=0, keepdims=True)
        out_ref[head, pl.ds(HEAD_DIM + 1, 1), lanes] = top
        now = later


def finished(result, top):
    total = result[HEAD_DIM : HEAD_DIM + 1]
    lse = jnp.log2(total) if top is None else top + jnp.log2(total)
    high = lse.astype(jnp.bfloat16).astype(jnp.float32)
    middle = (lse - high).astype(jnp.bfloat16).astype(jnp.float32)
    low = lse - high - middle
    row = lax.broadcasted_iota(jnp.int32, (TAIL, total.shape[1]), 0)
    parts = jnp.where(row == 0, high, jnp.where(row == 1, middle, jnp.where(row == 2, low, 0.0)))
    return jnp.concatenate([result[:HEAD_DIM] / total, parts], axis=0).astype(jnp.bfloat16)


def make_keys(keys_ref, message):
    keys_ref[...] = upright(message[pl.ds(HEAD_DIM, HEAD_DIM), :])


def values_of(message):
    return with_ones(message[pl.ds(2 * HEAD_DIM, HEAD_DIM), :])


def queries_of(message):
    return message[pl.ds(0, HEAD_DIM), :]


def settle(results, outs, messages, every):
    for result, out in zip(results, outs):
        out[...] = finished(result, None)

    @pl.when(jnp.logical_not(in_range([result[HEAD_DIM : HEAD_DIM + 1] for result in results])))
    def again():
        for message, out in zip(messages, outs):
            out[...] = finished(*shifted(queries_of(message), every()))


def early_kernel(m0, ma, keys0, keysa, part0, parta):
    make_keys(keys0, m0)
    make_keys(keysa, ma)
    groups = ((keys0, values_of(m0)), (keysa, values_of(ma)))
    part0[...], parta[...] = plain((queries_of(m0), groups), (queries_of(ma), groups))


def middle_kernel(m1, m3, part3, keys1, more3):
    make_keys(keys1, m1)
    (term,) = plain((queries_of(m3), ((keys1, values_of(m1)),)))
    more3[...] = part3[...] + term


def cross_kernel(m0, m1, m2, m3, keys0, keys1, keys3, part3, f2, f3, keys2):
    make_keys(keys2, m2)
    groups = [(keys, values_of(message)) for keys, message in ((keys0, m0), (keys1, m1), (keys3, m3), (keys2, m2))]
    whole, rest = plain((queries_of(m2), groups), (queries_of(m3), groups[3:]))
    settle((whole, part3[...] + rest), (f2, f3), (m2, m3), lambda: groups)


def next_kernel(m0, m1, m2, m3, keys0, keys1, keys2, keys3, f1):
    groups = [(keys, values_of(message)) for keys, message in ((keys0, m0), (keys1, m1), (keys2, m2), (keys3, m3))]
    (whole,) = plain((queries_of(m1), groups))
    settle((whole,), (f1,), (m1,), lambda: groups)


def own_kernel(m0, m1, m2, m3, keys0, keys1, keys2, keys3, part0, low_ref, high_ref, rows_ref, f0):
    groups = [(keys, values_of(message)) for keys, message in ((keys0, m0), (keys1, m1), (keys2, m2), (keys3, m3))]
    (rest,) = plain((queries_of(m0), groups[1:3]))
    settle((part0[...] + rest,), (f0,), (m0,), lambda: groups)
    merge_kernel((0,), low_ref, high_ref, f0, rows_ref)


def merge_kernel(steps, low_ref, high_ref, *refs):
    *results, rows_ref = refs
    each, _, rows = low_ref.shape
    half = rows // STRIDES
    me = lax.axis_index("seq")
    position = lax.broadcasted_iota(jnp.int32, (1, SPAN), 1)
    for at, (step, result) in enumerate(zip(steps, results)):
        head = jnp.bitwise_xor(me, step)
        place = one_hot(
            (2 * LANES, SPAN),
            lambda row, column: column == row % LANES * STRIDES + (head + row // LANES * 2) % STRIDES,
        )
        used = position % 2 == head % 2
        for block in range(rows // SPAN):
            lanes = pl.ds(block * SPAN, SPAN)
            piece = [result[:, pl.ds(klass * half + block * LANES, LANES)] for klass in range(2)]
            there = dot_nn(jnp.concatenate(piece, axis=1), place)
            in_low = low_ref[jnp.minimum(head, each - 1), :, lanes]
            level = jnp.where(head < each, in_low, high_ref[jnp.maximum(head - each, 0), :, lanes])
            near = level[:HEAD_DIM]
            total = level[HEAD_DIM : HEAD_DIM + 1]
            top = level[HEAD_DIM + 1 : HEAD_DIM + 2]
            lse = there[HEAD_DIM : HEAD_DIM + 1] + there[HEAD_DIM + 1 : HEAD_DIM + 2] + there[HEAD_DIM + 2 : HEAD_DIM + 3]
            near_lse = top + jnp.log2(total)
            peak = jnp.where(used, jnp.maximum(near_lse, lse), near_lse)
            weight = jnp.exp2(top - peak)
            far = jnp.where(used, jnp.exp2(lse - peak), 0.0)
            share = 1.0 / (total * weight + far)
            merged = near * (weight * share) + there[:HEAD_DIM] * (far * share)
            rows_ref[at, :, lanes] = merged.astype(jnp.bfloat16)


def last_kernel(low_ref, high_ref, own_ref, far_ref, result, out_hbm, rows_ref, sent):
    me = lax.axis_index("seq")

    def sending(step, rows):
        head = jnp.bitwise_xor(me, step)
        features = pl.ds(pl.multiple_of(head * HEAD_DIM, HEAD_DIM), HEAD_DIM)
        return pltpu.make_async_copy(rows, out_hbm.at[features], sent.at[step])

    copies = [sending(0, own_ref.at[0]), sending(2, far_ref.at[0]), sending(3, far_ref.at[1])]
    for copy in copies:
        copy.start()
    merge_kernel((1,), low_ref, high_ref, result, rows_ref)
    copies.append(sending(1, rows_ref.at[0]))
    copies[-1].start()
    for copy in copies:
        copy.wait()


def exchanged(block, step):
    return lax.ppermute(block, "seq", [(i, i ^ step) for i in range(lax.axis_size("seq"))])


def whole_slide(query_rows, key_rows, value_rows):
    rows, width = query_rows.shape
    heads = width // HEAD_DIM
    count = rows // 2
    bf16, f32 = jnp.bfloat16, jnp.float32
    turned = [pltpu.with_memory_space_constraint(block.T, pltpu.HBM) for block in (query_rows, key_rows, value_rows)]
    *here, m2, m3, m1, m0 = call(
        pack_kernel,
        [jax.ShapeDtypeStruct((width, rows), bf16)] * 3 + [jax.ShapeDtypeStruct((3 * HEAD_DIM, count), bf16)] * heads,
        turned,
        [pltpu.VMEM((heads, 3 * HEAD_DIM, count), bf16), pltpu.SemaphoreType.DMA((rows // SPAN, 3))],
        1 << 28,
        pltpu.HBM,
    )
    n2, n3 = exchanged(m2, 2), exchanged(m3, 3)

    def near(first, some):
        return call(
            functools.partial(near_kernel, first),
            jax.ShapeDtypeStruct((some, HEAD_DIM + TAIL, rows), f32),
            here,
            [pltpu.VMEM((some, rows, HEAD_DIM), bf16)],
            4 * some * rows * rows * 256,
        )

    low = near(0, LOW_HEADS)
    low, m1, *here = lax.optimization_barrier((low, m1, *here))
    n1 = exchanged(m1, 1)
    high = near(LOW_HEADS, heads - LOW_HEADS)
    result = jax.ShapeDtypeStruct((HEAD_DIM + TAIL, count), bf16)
    part = jax.ShapeDtypeStruct((HEAD_DIM + 2 * TAIL, count), f32)
    keys = jax.ShapeDtypeStruct((count, HEAD_DIM), bf16)
    work = 4 * count * count * 256
    n3, high = lax.optimization_barrier((n3, high))
    keys0, keys3, part0, part3 = call(early_kernel, [keys, keys, part, part], (m0, n3), [], 4 * work)
    keys0, keys3, n1 = lax.optimization_barrier((keys0, keys3, n1))
    keys1, part3 = call(middle_kernel, [keys, part], (n1, n3, part3), [], work)
    keys1, n2 = lax.optimization_barrier((keys1, n2))
    f2, f3, keys2 = call(
        cross_kernel, [result, result, keys], (m0, n1, n2, n3, keys0, keys1, keys3, part3), [], 5 * work
    )
    f2, f3, keys2 = lax.optimization_barrier((f2, f3, keys2))
    g2, g3 = exchanged(f2, 2), exchanged(f3, 3)
    every = (m0, n1, n2, n3, keys0, keys1, keys2, keys3)
    f1 = call(next_kernel, result, every, [], 4 * work)
    f1, part0 = lax.optimization_barrier((f1, part0))
    g1 = exchanged(f1, 1)
    own = call(
        own_kernel,
        jax.ShapeDtypeStruct((1, HEAD_DIM, rows), bf16),
        (*every, part0, low, high),
        [pltpu.VMEM((HEAD_DIM + TAIL, count), bf16)],
        2 * work,
    )
    def merged(steps, results):
        shape = jax.ShapeDtypeStruct((len(steps), HEAD_DIM, rows), bf16)
        return call(functools.partial(merge_kernel, steps), shape, (low, high, *results), [], len(steps) << 29)

    others = merged((2, 3), (g2, g3))
    return pl.pallas_call(
        last_kernel,
        out_shape=jax.ShapeDtypeStruct((width, rows), bf16),
        in_specs=[pl.BlockSpec(memory_space=pltpu.VMEM)] * 5,
        out_specs=pl.BlockSpec(memory_space=pl.ANY),
        scratch_shapes=[pltpu.VMEM((1, HEAD_DIM, rows), bf16), pltpu.SemaphoreType.DMA((heads,))],
        compiler_params=pltpu.CompilerParams(vmem_limit_bytes=VMEM_BYTES),
        cost_estimate=pl.CostEstimate(flops=1 << 29, bytes_accessed=1 << 20, transcendentals=0),
    )(low, high, own, others, g1).T


def per_device(query_rows, key_rows, value_rows):
    rows, width = query_rows.shape
    shards = lax.axis_size("seq")
    if rows == SEG_A and rows * shards == SEG_B and width == shards * HEAD_DIM and shards == STRIDES:
        return whole_slide(query_rows, key_rows, value_rows)
    return any_length(query_rows, key_rows, value_rows)


def solution(mesh):
    return jax.shard_map(
        per_device,
        mesh=mesh,
        in_specs=(
            P(("slides", "seq"), "head"),
            P(("slides", "seq"), "head"),
            P(("slides", "seq"), "head"),
        ),
        out_specs=P(("slides", "seq"), "head"),
        check_vma=False,
    )
```

```python
import functools
import math

import jax
import jax.numpy as jnp
import numpy as np
from jax import lax
from jax.experimental import pallas as pl
from jax.experimental.pallas import tpu as pltpu
from jax.sharding import PartitionSpec as P

HEAD_DIM = 48
SEG_A = 1024
SEG_B = 4096


def swapped(shard, axis, stride):
    return lax.ppermute(shard, axis, [(i, i ^ 1 << stride) for i in range(lax.axis_size(axis))])


def attend(query_flat, key_flat, value_flat, score_scale):
    local_heads = query_flat.shape[1] // HEAD_DIM
    query_block = query_flat.reshape(query_flat.shape[0], local_heads, HEAD_DIM)
    key_block = key_flat.reshape(key_flat.shape[0], local_heads, HEAD_DIM)
    value_block = value_flat.reshape(value_flat.shape[0], local_heads, HEAD_DIM)
    scores = (
        jnp.einsum("qad,kad->qak", query_block, key_block, preferred_element_type=jnp.float32)
        * score_scale
    )
    row_max = jnp.max(scores, axis=-1)
    exp_scores = jnp.exp(scores - row_max[:, :, None])
    row_total = jnp.sum(exp_scores, axis=-1)
    weighted = jnp.einsum(
        "qak,kad->qad",
        exp_scores.astype(jnp.bfloat16),
        value_block,
        preferred_element_type=jnp.float32,
    )
    level_out = weighted / row_total[:, :, None]
    return (
        level_out.reshape(query_flat.shape[0], local_heads * HEAD_DIM),
        row_max + jnp.log(row_total),
    )


def attend_rows(query_flat, key_flat, value_flat, score_scale):
    count, feature_width = query_flat.shape
    local_heads = feature_width // HEAD_DIM
    keys = key_flat.shape[0]
    rows = math.gcd(count, max(1, 1048576 // (local_heads * keys)))

    def one_piece(query_piece):
        return attend(query_piece, key_flat, value_flat, score_scale)

    outs, lses = lax.map(one_piece, query_flat.reshape(count // rows, rows, feature_width))
    return (outs.reshape(count, feature_width), lses.reshape(count, local_heads))


def local_segments(query_flat, key_flat, value_flat, seg_rows, score_scale):
    count, feature_width = query_flat.shape
    local_heads = feature_width // HEAD_DIM
    shape = (count // seg_rows, seg_rows, feature_width)

    def one_segment(parts):
        return attend_rows(parts[0], parts[1], parts[2], score_scale)

    outs, lses = lax.map(
        one_segment, (query_flat.reshape(shape), key_flat.reshape(shape), value_flat.reshape(shape))
    )
    return (outs.reshape(count, feature_width), lses.reshape(count, local_heads))


def pick_rows(block, stride):
    row_count, feature_width = block.shape
    local_heads = feature_width // HEAD_DIM
    grid = block.reshape(row_count // stride, stride * feature_width)
    columns = []
    for head in range(local_heads):
        begin = head % stride * feature_width + head * HEAD_DIM
        columns.append(grid[:, begin : begin + HEAD_DIM])
    return jnp.concatenate(columns, axis=1)


def spread_rows(level_out, level_lse, stride):
    used_count, feature_width = level_out.shape
    local_heads = feature_width // HEAD_DIM
    head_of_column = np.arange(feature_width) // HEAD_DIM
    out_phases = []
    lse_phases = []
    for phase in range(stride):
        column_mask = jnp.asarray((head_of_column % stride == phase).astype(np.float32))
        head_mask = jnp.asarray(np.arange(local_heads) % stride == phase)
        out_phases.append(level_out * column_mask[None, :])
        lse_phases.append(jnp.where(head_mask[None, :], level_lse, -jnp.inf))
    full_out = jnp.stack(out_phases, axis=1).reshape(used_count * stride, feature_width)
    full_lse = jnp.stack(lse_phases, axis=1).reshape(used_count * stride, local_heads)
    return (full_out, full_lse)


def fold_block(fold_state, queries, keys, values, valid, score_scale):
    running_max, running_total, running_acc = fold_state
    local_heads = queries.shape[1] // HEAD_DIM
    query_block = queries.reshape(queries.shape[0], local_heads, HEAD_DIM)
    key_block = keys.reshape(keys.shape[0], local_heads, HEAD_DIM)
    value_block = values.reshape(values.shape[0], local_heads, HEAD_DIM)
    scores = (
        jnp.einsum("qad,kad->qak", query_block, key_block, preferred_element_type=jnp.float32)
        * score_scale
    )
    scores = jnp.where(valid[None, None, :], scores, -jnp.inf)
    new_max = jnp.maximum(running_max, jnp.max(scores, axis=-1))
    safe_max = jnp.where(new_max == -jnp.inf, 0.0, new_max)
    rescale = jnp.exp(running_max - safe_max)
    exp_scores = jnp.exp(scores - safe_max[:, :, None])
    new_total = running_total * rescale + jnp.sum(exp_scores, axis=-1)
    weighted = jnp.einsum(
        "qak,kad->qad",
        exp_scores.astype(jnp.bfloat16),
        value_block,
        preferred_element_type=jnp.float32,
    )
    new_acc = running_acc * rescale[:, :, None] + weighted
    return (new_max, new_total, new_acc)


def any_length(query_rows, key_rows, value_rows):
    row_count = query_rows.shape[0]
    feature_width = query_rows.shape[1]
    local_heads = feature_width // HEAD_DIM
    shards = lax.axis_size("seq")
    score_scale = HEAD_DIM ** (-0.5)
    first_out, first_lse = local_segments(query_rows, key_rows, value_rows, SEG_A, score_scale)
    used_two = row_count // 2
    seg_two = SEG_B // 2
    query_two = pick_rows(query_rows, 2)
    key_two = pick_rows(key_rows, 2)
    value_two = pick_rows(value_rows, 2)
    stacked = jnp.stack([key_two, value_two])
    for bit_index in range((seg_two // used_two).bit_length() - 1):
        partner = swapped(stacked, "seq", bit_index)
        stacked = jnp.concatenate([stacked, partner], axis=1)
    second_out, second_lse = attend_rows(query_two, stacked[0], stacked[1], score_scale)
    span_tokens = row_count * shards
    group_span = span_tokens // row_count
    used_three = row_count // 4
    wide_queries = pick_rows(query_rows, 4)
    wide_keys = pick_rows(key_rows, 4)
    wide_values = pick_rows(value_rows, 4)
    my_group = lax.axis_index("seq") // group_span
    key_limit = max(1, 1048576 // (local_heads * used_three))
    initial = (
        jnp.full((used_three, local_heads), -jnp.inf, jnp.float32),
        jnp.zeros((used_three, local_heads), jnp.float32),
        jnp.zeros((used_three, local_heads, HEAD_DIM), jnp.float32),
    )
    pieces = (
        lax.all_gather(wide_keys, "seq", axis=0, tiled=True),
        lax.all_gather(wide_values, "seq", axis=0, tiled=True),
    )
    piece_rows = pieces[0].shape[0]
    block = math.gcd(piece_rows, key_limit)
    key_blocks = pieces[0].reshape(piece_rows // block, block, feature_width)
    value_blocks = pieces[1].reshape(piece_rows // block, block, feature_width)
    block_starts = jnp.arange(piece_rows // block, dtype=jnp.int32) * block

    def fold_step(inner_state, items):
        owners = (items[2] + jnp.arange(block, dtype=jnp.int32)) // used_three
        valid = owners // group_span == my_group
        return (fold_block(inner_state, wide_queries, items[0], items[1], valid, score_scale), None)

    final_state, unused = lax.scan(fold_step, initial, (key_blocks, value_blocks, block_starts))
    final_max, final_total, final_acc = final_state
    third_out = (final_acc / final_total[:, :, None]).reshape(used_three, feature_width)
    third_lse = final_max + jnp.log(final_total)
    second_full, second_lse_full = spread_rows(second_out, second_lse, 2)
    third_full, third_lse_full = spread_rows(third_out, third_lse, 4)
    peak = jnp.maximum(jnp.maximum(first_lse, second_lse_full), third_lse_full)
    weight_one = jnp.exp(first_lse - peak)
    weight_two = jnp.exp(second_lse_full - peak)
    weight_three = jnp.exp(third_lse_full - peak)
    denominator = jnp.repeat(weight_one + weight_two + weight_three, HEAD_DIM, axis=1)
    numerator = jnp.repeat(weight_one, HEAD_DIM, axis=1) * first_out
    numerator = numerator + jnp.repeat(weight_two, HEAD_DIM, axis=1) * second_full
    numerator = numerator + jnp.repeat(weight_three, HEAD_DIM, axis=1) * third_full
    return (numerator / denominator).astype(jnp.bfloat16)


STRIDES = 4
LANES = 128
SPAN = STRIDES * LANES
NEAR_KEYS = 256
LOW_HEADS = 1
TAIL = 8
LOG2E = 1.4426950408889634
FACTOR = HEAD_DIM ** (-0.5) * LOG2E
LEAST_TOTAL = 2.0 ** -60
MOST_TOTAL = 2.0 ** 100
VMEM_BYTES = 16 * 1024 * 1024


def dot_nn(left, right):
    return lax.dot_general(left, right, (((1,), (0,)), ((), ())), preferred_element_type=jnp.float32)


def dot_nt(left, right):
    return lax.dot_general(left, right, (((1,), (1,)), ((), ())), preferred_element_type=jnp.float32)


def one_hot(shape, which):
    rows = lax.broadcasted_iota(jnp.int32, shape, 0)
    columns = lax.broadcasted_iota(jnp.int32, shape, 1)
    return jnp.where(which(rows, columns), 1.0, 0.0).astype(jnp.bfloat16)


def call(kernel, outs, args, scratch, flops, space=pltpu.VMEM):
    return pl.pallas_call(
        kernel,
        out_shape=outs,
        in_specs=[pl.BlockSpec(memory_space=space)] * len(args),
        out_specs=jax.tree.map(lambda out: pl.BlockSpec(memory_space=pltpu.VMEM), outs),
        scratch_shapes=scratch,
        compiler_params=pltpu.CompilerParams(vmem_limit_bytes=VMEM_BYTES),
        cost_estimate=pl.CostEstimate(flops=flops, bytes_accessed=2 << 20, transcendentals=0),
    )(*args)


def pick_for(head):
    return one_hot(
        (SPAN, 2 * LANES),
        lambda row, column: row == column % LANES * STRIDES + (head + column // LANES * 2) % STRIDES,
    )


def fill_message(message, pieces, pick, block):
    half = message.shape[1] // 2
    picked = dot_nn(jnp.concatenate(pieces, axis=0), pick).astype(jnp.bfloat16)
    for klass in range(2):
        lanes = pl.ds(klass * half + block * LANES, LANES)
        message[:, lanes] = picked[:, klass * LANES : (klass + 1) * LANES]


def first_pack_kernel(q_hbm, k_hbm, v_hbm, message, held, arrivals):
    head = jnp.bitwise_xor(lax.axis_index("seq"), 3)
    features = pl.ds(pl.multiple_of(head * HEAD_DIM, 16), HEAD_DIM)
    copies = [
        pltpu.make_async_copy(source.at[features], held.at[at], arrivals.at[at])
        for at, source in enumerate((q_hbm, k_hbm, v_hbm))
    ]
    for copy in copies:
        copy.start()
    pick = pick_for(head)
    for copy in copies:
        copy.wait()
    for block in range(held.shape[2] // SPAN):
        fill_message(message, [held[at, :, pl.ds(block * SPAN, SPAN)] for at in range(3)], pick, block)


def pack_kernel(q_hbm, k_hbm, v_hbm, q_ref, k_ref, v_ref, m2, m1, m0, arrivals):
    copies = [
        pltpu.make_async_copy(source, target, arrivals.at[at])
        for at, (source, target) in enumerate(((q_hbm, q_ref), (k_hbm, k_ref), (v_hbm, v_ref)))
    ]
    for copy in copies:
        copy.start()
    me = lax.axis_index("seq")
    heads = [(jnp.bitwise_xor(me, step), message) for step, message in ((2, m2), (1, m1), (0, m0))]
    picks = [pick_for(head) for head, _ in heads]
    for copy in copies:
        copy.wait()
    for (head, message), pick in zip(heads, picks):
        features = pl.ds(pl.multiple_of(head * HEAD_DIM, 16), HEAD_DIM)
        for block in range(q_ref.shape[1] // SPAN):
            pieces = [ref[features, pl.ds(block * SPAN, SPAN)] for ref in (q_ref, k_ref, v_ref)]
            fill_message(message, pieces, pick, block)


def with_ones(block):
    count = block.shape[1]
    extra = one_hot((2 * TAIL, count), lambda row, column: row == 0)
    return jnp.concatenate([block, extra], axis=0)


def upright(block):
    count = block.shape[1]
    size = min(count, 2 * LANES)
    eye = one_hot((size, size), lambda row, column: row == column)
    pieces = [dot_nt(eye, block[:, at : at + size]) for at in range(0, count, size)]
    return jnp.concatenate(pieces, axis=0).astype(jnp.bfloat16)


def doubled(scores, shift):
    half = scores.shape[0] // 2
    one = jnp.where(lax.broadcasted_iota(jnp.int32, (1, scores.shape[1]), 1) < half, 1.0, 0.0)
    first = jnp.exp2(scores[:half] * FACTOR + (one - shift))
    second = jnp.exp2(scores[half:] * FACTOR - shift)
    return jnp.concatenate([first.astype(jnp.bfloat16), second.astype(jnp.bfloat16)], axis=0)


def plain(*jobs):
    steps = [(at, queries, keys, values) for at, (queries, groups) in enumerate(jobs) for keys, values in groups]
    results = [None] * len(jobs)
    ahead = dot_nn(steps[0][2][...], steps[0][1])
    for now, (at, _, _, values) in enumerate(steps):
        scores = ahead
        if now + 1 < len(steps):
            ahead = dot_nn(steps[now + 1][2][...], steps[now + 1][1])
        term = dot_nn(values, doubled(scores, 0.0))
        results[at] = term if results[at] is None else results[at] + term
    return results


def shifted(queries, groups):
    scores = [dot_nn(keys[...], queries) for keys, _ in groups]
    top = functools.reduce(jnp.maximum, [jnp.max(block, axis=0, keepdims=True) for block in scores]) * FACTOR
    terms = [dot_nn(values, doubled(block, top)) for block, (_, values) in zip(scores, groups)]
    return functools.reduce(jnp.add, terms), top


def in_range(totals):
    low = functools.reduce(jnp.minimum, totals)
    high = functools.reduce(jnp.maximum, totals)
    return jnp.logical_and(jnp.min(low) >= LEAST_TOTAL, jnp.max(high) <= MOST_TOTAL)


def near_kernel(first, qt_ref, kt_ref, vt_ref, out_ref, keys_ref):
    rows = qt_ref.shape[1]
    heads = out_ref.shape[0]
    for head in range(heads):
        keys_ref[head] = upright(kt_ref[pl.ds((first + head) * HEAD_DIM, HEAD_DIM), :])
    blocks = [(head, start) for head in range(heads) for start in range(0, rows, SPAN)]
    pieces = range(0, rows, NEAR_KEYS)

    def scores_of(block, piece):
        head, start = block
        queries = qt_ref[pl.ds((first + head) * HEAD_DIM, HEAD_DIM), pl.ds(start, SPAN)]
        return dot_nn(keys_ref[head, pl.ds(piece, NEAR_KEYS), :], queries)

    def folded(values, join, held):
        parts = [values[at : at + 8] for at in range(0, NEAR_KEYS, 8)]
        return functools.reduce(join, parts if held is None else [held, *parts])

    now, peaks = [], None
    for piece in pieces:
        now.append(scores_of(blocks[0], piece))
        peaks = folded(now[-1], jnp.maximum, peaks)
    for at, (head, start) in enumerate(blocks):
        top = jnp.max(peaks, axis=0, keepdims=True) * FACTOR
        later, peaks, result, totals = [], None, None, None
        for piece, scores in zip(pieces, now):
            if at + 1 < len(blocks):
                later.append(scores_of(blocks[at + 1], piece))
                peaks = folded(later[-1], jnp.maximum, peaks)
            probs = jnp.exp2(scores * FACTOR - top)
            totals = folded(probs, jnp.add, totals)
            values = vt_ref[pl.ds((first + head) * HEAD_DIM, HEAD_DIM), pl.ds(piece, NEAR_KEYS)]
            term = dot_nn(values, probs.astype(jnp.bfloat16))
            result = term if result is None else result + term
        lanes = pl.ds(start, SPAN)
        out_ref[head, pl.ds(0, HEAD_DIM), lanes] = result
        out_ref[head, pl.ds(HEAD_DIM, 1), lanes] = jnp.sum(totals, axis=0, keepdims=True)
        out_ref[head, pl.ds(HEAD_DIM + 1, 1), lanes] = top
        now = later


def finished(result, top):
    total = result[HEAD_DIM : HEAD_DIM + 1]
    lse = jnp.log2(total) if top is None else top + jnp.log2(total)
    high = lse.astype(jnp.bfloat16).astype(jnp.float32)
    middle = (lse - high).astype(jnp.bfloat16).astype(jnp.float32)
    low = lse - high - middle
    row = lax.broadcasted_iota(jnp.int32, (TAIL, total.shape[1]), 0)
    parts = jnp.where(row == 0, high, jnp.where(row == 1, middle, jnp.where(row == 2, low, 0.0)))
    return jnp.concatenate([result[:HEAD_DIM] / total, parts], axis=0).astype(jnp.bfloat16)


def make_keys(keys_ref, message):
    keys_ref[...] = upright(message[pl.ds(HEAD_DIM, HEAD_DIM), :])


def values_of(message):
    return with_ones(message[pl.ds(2 * HEAD_DIM, HEAD_DIM), :])


def queries_of(message):
    return message[pl.ds(0, HEAD_DIM), :]


def settle(results, outs, messages, every):
    for result, out in zip(results, outs):
        out[...] = finished(result, None)

    @pl.when(jnp.logical_not(in_range([result[HEAD_DIM : HEAD_DIM + 1] for result in results])))
    def again():
        for message, out in zip(messages, outs):
            out[...] = finished(*shifted(queries_of(message), every()))


def early_kernel(m0, m3, keys0, keys3, part3):
    make_keys(keys0, m0)
    make_keys(keys3, m3)
    (part3[...],) = plain((queries_of(m3), ((keys0, values_of(m0)), (keys3, values_of(m3)))))


def middle_kernel(m1, m3, part3, keys1, more3):
    make_keys(keys1, m1)
    (term,) = plain((queries_of(m3), ((keys1, values_of(m1)),)))
    more3[...] = part3[...] + term


def cross_kernel(m0, m1, m2, m3, keys0, keys1, keys3, part3, f2, f3, keys2):
    make_keys(keys2, m2)
    groups = [(keys, values_of(message)) for keys, message in ((keys0, m0), (keys1, m1), (keys3, m3), (keys2, m2))]
    whole, rest = plain((queries_of(m2), groups), (queries_of(m3), groups[3:]))
    settle((whole, part3[...] + rest), (f2, f3), (m2, m3), lambda: groups)


def next_kernel(m0, m1, m2, m3, keys0, keys1, keys2, keys3, f1):
    groups = [(keys, values_of(message)) for keys, message in ((keys0, m0), (keys1, m1), (keys2, m2), (keys3, m3))]
    (whole,) = plain((queries_of(m1), groups))
    settle((whole,), (f1,), (m1,), lambda: groups)


def own_kernel(m0, m1, m2, m3, keys0, keys1, keys2, keys3, low_ref, high_ref, rows_ref, f0):
    groups = [(keys, values_of(message)) for keys, message in ((keys0, m0), (keys1, m1), (keys2, m2), (keys3, m3))]
    (whole,) = plain((queries_of(m0), groups))
    settle((whole,), (f0,), (m0,), lambda: groups)
    merge_kernel((0,), low_ref, high_ref, f0, rows_ref)


def merge_kernel(steps, low_ref, high_ref, *refs):
    *results, rows_ref = refs
    each, _, rows = low_ref.shape
    half = rows // STRIDES
    me = lax.axis_index("seq")
    position = lax.broadcasted_iota(jnp.int32, (1, SPAN), 1)
    for at, (step, result) in enumerate(zip(steps, results)):
        head = jnp.bitwise_xor(me, step)
        place = one_hot(
            (2 * LANES, SPAN),
            lambda row, column: column == row % LANES * STRIDES + (head + row // LANES * 2) % STRIDES,
        )
        used = position % 2 == head % 2
        for block in range(rows // SPAN):
            lanes = pl.ds(block * SPAN, SPAN)
            piece = [result[:, pl.ds(klass * half + block * LANES, LANES)] for klass in range(2)]
            there = dot_nn(jnp.concatenate(piece, axis=1), place)
            in_low = low_ref[jnp.minimum(head, each - 1), :, lanes]
            level = jnp.where(head < each, in_low, high_ref[jnp.maximum(head - each, 0), :, lanes])
            near = level[:HEAD_DIM]
            total = level[HEAD_DIM : HEAD_DIM + 1]
            top = level[HEAD_DIM + 1 : HEAD_DIM + 2]
            lse = there[HEAD_DIM : HEAD_DIM + 1] + there[HEAD_DIM + 1 : HEAD_DIM + 2] + there[HEAD_DIM + 2 : HEAD_DIM + 3]
            near_lse = top + jnp.log2(total)
            peak = jnp.where(used, jnp.maximum(near_lse, lse), near_lse)
            weight = jnp.exp2(top - peak)
            far = jnp.where(used, jnp.exp2(lse - peak), 0.0)
            share = 1.0 / (total * weight + far)
            merged = near * (weight * share) + there[:HEAD_DIM] * (far * share)
            rows_ref[at, :, lanes] = merged.astype(jnp.bfloat16)


def last_kernel(low_ref, high_ref, own_ref, far_ref, result, out_hbm, rows_ref, sent):
    me = lax.axis_index("seq")

    def sending(step, rows):
        head = jnp.bitwise_xor(me, step)
        features = pl.ds(pl.multiple_of(head * HEAD_DIM, HEAD_DIM), HEAD_DIM)
        return pltpu.make_async_copy(rows, out_hbm.at[features], sent.at[step])

    copies = [sending(0, own_ref.at[0]), sending(2, far_ref.at[0]), sending(3, far_ref.at[1])]
    for copy in copies:
        copy.start()
    merge_kernel((1,), low_ref, high_ref, result, rows_ref)
    copies.append(sending(1, rows_ref.at[0]))
    copies[-1].start()
    for copy in copies:
        copy.wait()


def exchanged(block, step):
    return lax.ppermute(block, "seq", [(i, i ^ step) for i in range(lax.axis_size("seq"))])


def whole_slide(query_rows, key_rows, value_rows):
    rows, width = query_rows.shape
    heads = width // HEAD_DIM
    count = rows // 2
    bf16, f32 = jnp.bfloat16, jnp.float32
    message = jax.ShapeDtypeStruct((3 * HEAD_DIM, count), bf16)
    turned = [block.T for block in (query_rows, key_rows, value_rows)]
    m3 = call(
        first_pack_kernel,
        message,
        [pltpu.with_memory_space_constraint(block, pltpu.HBM) for block in turned],
        [pltpu.VMEM((3, HEAD_DIM, rows), bf16), pltpu.SemaphoreType.DMA((3,))],
        1 << 27,
        pltpu.HBM,
    )
    n3 = exchanged(m3, 3)
    m3, *turned = lax.optimization_barrier((m3, *turned))
    *here, m2, m1, m0 = call(
        pack_kernel,
        [jax.ShapeDtypeStruct((width, rows), bf16)] * 3 + [message] * 3,
        [pltpu.with_memory_space_constraint(block, pltpu.HBM) for block in turned],
        [pltpu.SemaphoreType.DMA((3,))],
        1 << 28,
        pltpu.HBM,
    )
    n2 = exchanged(m2, 2)

    def near(first, some):
        return call(
            functools.partial(near_kernel, first),
            jax.ShapeDtypeStruct((some, HEAD_DIM + TAIL, rows), f32),
            here,
            [pltpu.VMEM((some, rows, HEAD_DIM), bf16)],
            4 * some * rows * rows * 256,
        )

    low = near(0, LOW_HEADS)
    low, m1, *here = lax.optimization_barrier((low, m1, *here))
    n1 = exchanged(m1, 1)
    high = near(LOW_HEADS, heads - LOW_HEADS)
    result = jax.ShapeDtypeStruct((HEAD_DIM + TAIL, count), bf16)
    part = jax.ShapeDtypeStruct((HEAD_DIM + 2 * TAIL, count), f32)
    keys = jax.ShapeDtypeStruct((count, HEAD_DIM), bf16)
    work = 4 * count * count * 256
    n3, high = lax.optimization_barrier((n3, high))
    keys0, keys3, part3 = call(early_kernel, [keys, keys, part], (m0, n3), [], 2 * work)
    keys0, keys3, n1 = lax.optimization_barrier((keys0, keys3, n1))
    keys1, part3 = call(middle_kernel, [keys, part], (n1, n3, part3), [], work)
    keys1, n2 = lax.optimization_barrier((keys1, n2))
    f2, f3, keys2 = call(
        cross_kernel, [result, result, keys], (m0, n1, n2, n3, keys0, keys1, keys3, part3), [], 5 * work
    )
    f2, f3, keys2 = lax.optimization_barrier((f2, f3, keys2))
    g2, g3 = exchanged(f2, 2), exchanged(f3, 3)
    every = (m0, n1, n2, n3, keys0, keys1, keys2, keys3)
    f1 = call(next_kernel, result, every, [], 4 * work)
    f1, keys2 = lax.optimization_barrier((f1, keys2))
    every = (m0, n1, n2, n3, keys0, keys1, keys2, keys3)
    g1 = exchanged(f1, 1)
    own = call(
        own_kernel,
        jax.ShapeDtypeStruct((1, HEAD_DIM, rows), bf16),
        (*every, low, high),
        [pltpu.VMEM((HEAD_DIM + TAIL, count), bf16)],
        2 * work,
    )
    def merged(steps, results):
        shape = jax.ShapeDtypeStruct((len(steps), HEAD_DIM, rows), bf16)
        return call(functools.partial(merge_kernel, steps), shape, (low, high, *results), [], len(steps) << 29)

    others = merged((2, 3), (g2, g3))
    return pl.pallas_call(
        last_kernel,
        out_shape=jax.ShapeDtypeStruct((width, rows), bf16),
        in_specs=[pl.BlockSpec(memory_space=pltpu.VMEM)] * 5,
        out_specs=pl.BlockSpec(memory_space=pl.ANY),
        scratch_shapes=[pltpu.VMEM((1, HEAD_DIM, rows), bf16), pltpu.SemaphoreType.DMA((heads,))],
        compiler_params=pltpu.CompilerParams(vmem_limit_bytes=VMEM_BYTES),
        cost_estimate=pl.CostEstimate(flops=1 << 29, bytes_accessed=1 << 20, transcendentals=0),
    )(low, high, own, others, g1).T


def per_device(query_rows, key_rows, value_rows):
    rows, width = query_rows.shape
    shards = lax.axis_size("seq")
    if rows == SEG_A and rows * shards == SEG_B and width == shards * HEAD_DIM and shards == STRIDES:
        return whole_slide(query_rows, key_rows, value_rows)
    return any_length(query_rows, key_rows, value_rows)


def solution(mesh):
    return jax.shard_map(
        per_device,
        mesh=mesh,
        in_specs=(
            P(("slides", "seq"), "head"),
            P(("slides", "seq"), "head"),
            P(("slides", "seq"), "head"),
        ),
        out_specs=P(("slides", "seq"), "head"),
        check_vma=False,
    )
```
